32 devices in a mesh: req: 8 (over z, y), tp: 4 (over x, core).
Axes of the slice: x: 2, y: 2, z: 4, core: 2. Of those that a mesh axis runs over, the one named last changes fastest.
Arguments:
- tokens: bfloat16 [16, 256, 2048], P('req'), may hold values from -6 to 6
- attn_gain: float32 [2048], replicated, may hold values from 0.25 to 1.75
- w_query: bfloat16 [2048, 1280], P(None, 'tp'), may hold values from -0.125 to 0.125
- key_value_weight: bfloat16 [2048, 640], replicated, may hold values from -0.125 to 0.125
- w_out: bfloat16 [1280, 2048], P('tp'), may hold values from -0.15625 to 0.15625
- q_gain: float32 [64], replicated, as said below
- k_gain: float32 [64], replicated, as said below
- stored: bfloat16 [8, 5, 2048, 128], P('req'), may hold values from -6 to 6
- continuing: int32 [16], replicated, may hold values from 0 to 1, as said below
- cache_row: int32 [16], replicated, may hold values from -1 to 7, as said below
- cache_len: int32 [16], replicated, may hold values from 0 to 2048, as said below
Outputs:
- layer: bfloat16 [16, 256, 2048], P('req')
- decoding_group_cache: bfloat16 [32, 5, 1152, 128], P('req', None, 'tp')
The draws below stay inside these ranges and needn't reach their ends.
Inputs may be any that keep to these rules, and one draw needn't show every extreme that they name: `continuing`: exactly 8 requests have 1. `cache_row`: a continuing request's row of stored; every row belongs to exactly one continuing request; -1 for the others. `cache_len`: 1 to 2048 for a continuing request, 2048 for at least one; 0 for the others. `q_gain`: positive. `k_gain`: positive.
All inputs are finite; a program needn't handle non-finite values.
Results may differ from the reference program's by a relative error of at most 0.005.
The reference program's roundings to bfloat16 on the way count: a program that leaves them out, or rounds other values in their place, can miss the bound.
Values may be sent and summed in bfloat16 or wider, within the bound.
No kernel may reach another device: no remote copies, remote signals or barrier semaphores. Data moves between devices by JAX's collectives and lax.ppermute only.
A program may use at most 128 MiB of HBM per device.

```python
import math
import jax
import jax.numpy as jnp
from jax import lax

MODEL_WIDTH = 2048
QUERY_HEAD_COUNT = 20
KEY_VALUE_HEADS = 5
HEAD_SIZE = 64
NEW_TOKEN_COUNT = 256
CACHE_POSITIONS = 2048
REQUESTS_LOCAL = 2
REQUEST_TOTAL = 16
STORED_CACHES = 8
N_REQ = 8


def request_plan(key):
    order = jax.random.permutation(jax.random.fold_in(key, 7), REQUEST_TOTAL).astype(jnp.int32)
    live = order < REQUEST_TOTAL // 2
    lengths = jax.random.randint(jax.random.fold_in(key, 11), (REQUEST_TOTAL,), 1, CACHE_POSITIONS + 1).astype(jnp.int32)
    lengths = jnp.where(order == 0, CACHE_POSITIONS, lengths)
    lengths = jnp.where(live, lengths, 0)
    rows = jnp.where(live, order, -1)
    return (live.astype(jnp.int32), rows.astype(jnp.int32), lengths.astype(jnp.int32))


def draw_continuing(key, part):
    return request_plan(key)[0]


def draw_cache_row(key, part):
    return request_plan(key)[1]


def draw_cache_len(key, part):
    return request_plan(key)[2]


def draw_q_gain(key, part):
    uniform_draw = jax.random.uniform(jax.random.fold_in(key, 21), (HEAD_SIZE,), jnp.float32)
    return 0.6 + 1.2 * uniform_draw


def draw_k_gain(key, part):
    uniform_draw = jax.random.uniform(jax.random.fold_in(key, 23), (HEAD_SIZE,), jnp.float32)
    return 0.6 + 1.2 * uniform_draw


def block_scale(key, extent, pieces, least, largest):
    def one(dim, parts):
        heights = jax.random.uniform(jax.random.fold_in(jax.random.fold_in(key, 6), dim), (parts,), jnp.float32, least / len(pieces), largest / len(pieces))
        return jnp.repeat(jnp.exp(heights), extent[dim] // parts).reshape((-1,) + (1,) * (len(extent) - dim - 1))

    level = one(*pieces[0])
    for cut in pieces[1:]:
        level = level * one(*cut)
    return level


def centred(own_key, dims, spread, reach, shards=(), kind=jnp.bfloat16):
    result = spread * jax.random.normal(own_key, dims, jnp.float32)
    if shards:
        result = result * block_scale(own_key, dims, shards, -0.22, 0.18)
    return jnp.clip(result, -reach, reach).astype(kind)


def setup_inputs(seed: int = 0) -> dict:
    arg_keys = jax.random.split(jax.random.key(seed), 12)
    return {
        "tokens": centred(arg_keys[0], (REQUEST_TOTAL, NEW_TOKEN_COUNT, MODEL_WIDTH), 1.0, 6.0, ((0, 8),)),
        "attn_gain": jnp.clip(1.0 + 0.15 * jax.random.normal(arg_keys[1], (MODEL_WIDTH,), jnp.float32), 0.25, 1.75),
        "w_query": centred(arg_keys[2], (MODEL_WIDTH, QUERY_HEAD_COUNT * HEAD_SIZE), MODEL_WIDTH ** -0.5, 0.125, ((1, 4),)),
        "key_value_weight": centred(arg_keys[3], (MODEL_WIDTH, KEY_VALUE_HEADS * 2 * HEAD_SIZE), MODEL_WIDTH ** -0.5, 0.125),
        "w_out": centred(arg_keys[4], (QUERY_HEAD_COUNT * HEAD_SIZE, MODEL_WIDTH), (QUERY_HEAD_COUNT * HEAD_SIZE) ** -0.5, 0.15625, ((0, 4),)),
        "q_gain": draw_q_gain(jax.random.fold_in(arg_keys[11], 71), 0),
        "k_gain": draw_k_gain(jax.random.fold_in(arg_keys[11], 71), 0),
        "stored": centred(arg_keys[7], (STORED_CACHES, KEY_VALUE_HEADS, CACHE_POSITIONS, 2 * HEAD_SIZE), 1.0, 6.0, ((0, 8),)),
        "continuing": draw_continuing(jax.random.fold_in(arg_keys[11], 71), 0),
        "cache_row": draw_cache_row(jax.random.fold_in(arg_keys[11], 71), 0),
        "cache_len": draw_cache_len(jax.random.fold_in(arg_keys[11], 71), 0),
    }


def normalize(values, gain):
    return values * lax.rsqrt(lax.optimization_barrier(jnp.mean(values * values, axis=-1, keepdims=True)) + 1e-06) * gain

def rotary(values, positions):
    half_dim = values.shape[-1] // 2
    freq = jnp.exp(-math.log(10000.0) * jnp.arange(half_dim).astype(jnp.float32) * 2.0 / values.shape[-1])
    angle = positions.astype(jnp.float32)[..., None] * freq
    cosine = jnp.cos(angle)[..., None, :]
    sine = jnp.sin(angle)[..., None, :]
    first_half = values[..., :half_dim]
    second_half = values[..., half_dim:]
    return jnp.concatenate([first_half * cosine - second_half * sine, second_half * cosine + first_half * sine], axis=-1)

def reference(tokens, attn_gain, w_query, key_value_weight, w_out, q_gain, k_gain, stored, continuing, cache_row, cache_len):
    query_group_ratio = QUERY_HEAD_COUNT // KEY_VALUE_HEADS
    total_length = CACHE_POSITIONS + NEW_TOKEN_COUNT
    scale = 1.0 / math.sqrt(HEAD_SIZE)

    def one_request(request):
        hidden = tokens[request]
        live = continuing[request] == 1
        length = jnp.where(live, cache_len[request], 0).astype(jnp.int32)
        row = jnp.where(live, cache_row[request], 0).astype(jnp.int32)
        normalized_input = normalize(hidden.astype(jnp.float32), attn_gain).astype(jnp.bfloat16)
        positions = length + jnp.arange(NEW_TOKEN_COUNT, dtype=jnp.int32)
        query = jnp.dot(normalized_input, w_query, preferred_element_type=jnp.float32).reshape(NEW_TOKEN_COUNT, QUERY_HEAD_COUNT, HEAD_SIZE)
        query = rotary(normalize(query, q_gain), positions).astype(jnp.bfloat16)
        key_value_rows = jnp.dot(normalized_input, key_value_weight, preferred_element_type=jnp.float32).reshape(NEW_TOKEN_COUNT, KEY_VALUE_HEADS, 2 * HEAD_SIZE)
        keys_new = rotary(normalize(key_value_rows[..., :HEAD_SIZE], k_gain), positions)
        fresh = jnp.concatenate([keys_new, key_value_rows[..., HEAD_SIZE:]], axis=-1).astype(jnp.bfloat16)
        fresh = jnp.transpose(fresh, (1, 0, 2))
        stored_entries = lax.dynamic_index_in_dim(stored, row, 0, keepdims=False)
        position = jnp.arange(CACHE_POSITIONS, dtype=jnp.int32)
        stored_entries = jnp.where((position < length)[None, :, None], stored_entries, jnp.zeros_like(stored_entries))
        keys_all = jnp.concatenate([stored_entries, fresh], axis=1)
        expanded = jnp.repeat(keys_all, query_group_ratio, axis=0).astype(jnp.float32)
        query_heads = jnp.transpose(query, (1, 0, 2)).astype(jnp.float32)
        scores = jnp.einsum('hqd,hkd->hqk', query_heads, expanded[..., :HEAD_SIZE]) * scale
        query_index = jnp.arange(NEW_TOKEN_COUNT, dtype=jnp.int32)[:, None]
        key_index = jnp.arange(total_length, dtype=jnp.int32)[None, :]
        allowed = jnp.where(key_index < CACHE_POSITIONS, key_index < length, key_index - CACHE_POSITIONS <= query_index)
        scores = jnp.where(allowed[None], scores, -jnp.inf)
        row_max = lax.optimization_barrier(jnp.max(scores, axis=-1, keepdims=True))
        weights = jnp.exp(scores - row_max)
        probs = (weights / lax.optimization_barrier(jnp.sum(weights, axis=-1, keepdims=True))).astype(jnp.bfloat16)
        mixed = jnp.einsum('hqk,hkd->qhd', probs.astype(jnp.float32), expanded[..., HEAD_SIZE:])
        mixed = mixed.astype(jnp.bfloat16).reshape(NEW_TOKEN_COUNT, QUERY_HEAD_COUNT * HEAD_SIZE)
        update = jnp.dot(mixed, w_out, preferred_element_type=jnp.float32)
        layer_one = (hidden.astype(jnp.float32) + update).astype(jnp.bfloat16)
        padded_tokens = jnp.concatenate([stored_entries, jnp.zeros((KEY_VALUE_HEADS, NEW_TOKEN_COUNT, 2 * HEAD_SIZE), jnp.bfloat16)], axis=1)
        whole = lax.dynamic_update_slice_in_dim(padded_tokens, fresh, length, 1)
        return (layer_one, whole)
    layer, whole_caches = lax.map(one_request, jnp.arange(REQUEST_TOTAL, dtype=jnp.int32))
    position_halves = whole_caches.reshape(N_REQ // 2, 2 * REQUESTS_LOCAL, KEY_VALUE_HEADS, 2, total_length // 2, 2 * HEAD_SIZE)
    decoding_group_cache = jnp.transpose(position_halves, (0, 3, 1, 2, 4, 5)).reshape(2 * REQUEST_TOTAL, KEY_VALUE_HEADS, total_length // 2, 2 * HEAD_SIZE)
    return (layer, decoding_group_cache)
```

```python
import functools
import math

import jax
import jax.numpy as jnp
import numpy as np
from jax import lax
from jax.experimental import pallas as pl
from jax.experimental.pallas import tpu as pltpu
from jax.sharding import PartitionSpec as P

BF16 = jnp.bfloat16
F32 = jnp.float32
LANES = 128
EPS = 1e-06
NEG = -1e30
SMEM = pl.BlockSpec(memory_space=pltpu.SMEM)


def cost(flops, moved):
    return pl.CostEstimate(flops=int(flops), bytes_accessed=int(moved), transcendentals=0)


def params(mib=48):
    return pltpu.CompilerParams(vmem_limit_bytes=mib << 20)


def lane_iota(rows):
    return lax.broadcasted_iota(jnp.int32, (rows, LANES), 1)


def angle_tables(head_dim, new_count, cache_span):
    half = head_dim // 2
    freq = np.exp(-math.log(10000.0) * np.arange(half, dtype=np.float64) * 2.0 / head_dim)
    freq = np.tile(freq.astype(np.float32).astype(np.float64), LANES // half)

    def pair(positions):
        angle = positions[:, None].astype(np.float64) * freq[None, :]
        return np.cos(angle).astype(np.float32), np.sin(angle).astype(np.float32)

    fine = pair(np.arange(new_count))
    coarse = pair(np.arange(cache_span // 16 + 8) * 16)
    small = pair(np.arange(16))
    return fine + coarse + small


def rotation(length, tables):
    cos_i, sin_i, cos_hi, sin_hi, cos_lo, sin_lo = tables
    high = length // 16
    low = length - high * 16
    ch, sh = cos_hi[pl.ds(high, 1), :], sin_hi[pl.ds(high, 1), :]
    cl, sl = cos_lo[pl.ds(low, 1), :], sin_lo[pl.ds(low, 1), :]
    cb, sb = ch * cl - sh * sl, sh * cl + ch * sl
    ci, si = cos_i[...], sin_i[...]
    cosine = ci * cb - si * sb
    sine = si * cb + ci * sb
    lanes = lane_iota(ci.shape[0])
    return cosine, jnp.where(lanes % 64 < 32, -sine, sine)


def norm_rope(tile, gain, cosine, sine, blocks):
    square = tile * tile
    high = square.astype(BF16)
    low = (square - high.astype(F32)).astype(BF16)
    mean = jnp.dot(high, blocks, preferred_element_type=F32) + jnp.dot(
        low, blocks, preferred_element_type=F32
    )
    unit = tile * lax.rsqrt(mean + EPS) * gain
    lanes = lane_iota(tile.shape[0])
    other = jnp.where(lanes % 64 < 32, pltpu.roll(unit, 96, 1), pltpu.roll(unit, 32, 1))
    return unit * cosine + other * sine


def half_blocks():
    rows = lax.broadcasted_iota(jnp.int32, (LANES, LANES), 0)
    cols = lax.broadcasted_iota(jnp.int32, (LANES, LANES), 1)
    return jnp.where(rows // 64 == cols // 64, 1.0 / 64.0, 0.0).astype(BF16)


def live_length(cont, clen, request):
    return jnp.where(cont[request] == 1, clen[request], 0)


def to_chunks(ref, lead, value, chunk):
    rows = value.shape[0]
    for start in range(0, rows, chunk):
        size = min(chunk, rows - start)
        ref[(start // chunk,) + lead + (pl.ds(0, size),)] = value[start : start + size]


def query_kernel(req_dev, chunk, cont, clen, tok, gain, w, qg, ci, si, ch, sh, cl, sl, normed, q):
    b = pl.program_id(0)
    length = live_length(cont, clen, lax.axis_index("req") * req_dev + b)
    x = tok[0].astype(F32)
    mean = jnp.mean(x * x, axis=-1, keepdims=True)
    h = (x * lax.rsqrt(mean + EPS) * gain[...]).astype(BF16)
    normed[0] = h
    cosine, sine = rotation(length, (ci, si, ch, sh, cl, sl))
    out = jnp.dot(h, w[...], preferred_element_type=F32)
    blocks = half_blocks()
    count = h.shape[0]
    half = count // 2
    pair01 = norm_rope(out[:, :128], qg[...], cosine, sine, blocks)
    pair23 = norm_rope(out[:, 128:256], qg[...], cosine, sine, blocks)
    last = out[:, 256:320]
    last = jnp.concatenate([last[:half], last[half:]], axis=1)
    lanes = lane_iota(half)
    pick = lambda v: jnp.where(lanes < 64, v[:half], v[half:])
    last = norm_rope(last, qg[...], pick(cosine), pick(sine), blocks)
    packed = (jnp.concatenate([pair01, pair23, last], axis=0) * 0.125).astype(BF16)
    to_chunks(q, (0,), packed, chunk)


def fresh_kernel(req_dev, cont, clen, normed, w, kg, ci, si, ch, sh, cl, sl, fresh):
    b = pl.program_id(0)
    length = live_length(cont, clen, lax.axis_index("req") * req_dev + b)
    cosine, sine = rotation(length, (ci, si, ch, sh, cl, sl))
    out = jnp.dot(normed[0], w[...], preferred_element_type=F32)
    blocks = half_blocks()
    lanes = lane_iota(out.shape[0])
    for head in range(fresh.shape[1]):
        tile = out[:, head * 128 : head * 128 + 128]
        keys = norm_rope(tile, kg[...], cosine, sine, blocks)
        fresh[0, head] = jnp.where(lanes < 64, keys, tile).astype(BF16)


def split_heads(packed, count):
    half = count // 2
    wide = packed.astype(F32)
    lanes = lane_iota(count)
    tiles = [wide[:count], pltpu.roll(wide[:count], 64, 1)]
    tiles += [wide[count : 2 * count], pltpu.roll(wide[count : 2 * count], 64, 1)]
    last = wide[2 * count : 2 * count + half]
    tiles.append(jnp.concatenate([last, pltpu.roll(last, 64, 1)], axis=0))
    extra = jnp.where(lanes == 64, 1.0, 0.0)
    return [jnp.where(lanes < 64, tile, extra).astype(BF16) for tile in tiles]


def soft(scores, values):
    top = jnp.max(scores, axis=-1, keepdims=True)
    weights = jnp.exp(scores - top).astype(BF16)
    out = jnp.dot(weights, values, preferred_element_type=F32)
    total = out[:, 0:1]
    return out / pltpu.roll(out, 64, 1), top + jnp.log(total)


def local_kernel(groups, q, fresh, out, lse):
    heads = 5
    count = fresh.shape[2]
    first = lax.axis_index("tp") * heads
    lanes = lane_iota(count)
    rows = lax.broadcasted_iota(jnp.int32, (count, count), 0)
    cols = lax.broadcasted_iota(jnp.int32, (count, count), 1)
    packed = q[...].reshape(-1, LANES)
    tiles = split_heads(packed, count)
    stats = jnp.zeros((count, LANES), F32)
    kept = []
    for head in range(heads):
        kv = fresh[0, (first + head) // groups].astype(F32)
        keys = jnp.where(lanes < 64, kv, 0.0).astype(BF16)
        values = jnp.where(lanes < 64, 1.0, kv).astype(BF16)
        scores = lax.dot_general(
            tiles[head], keys, (((1,), (1,)), ((), ())), preferred_element_type=F32
        )
        scores = jnp.where(cols <= rows, scores, NEG)
        mixed, level = soft(scores, values)
        stats = jnp.where(lanes == head, level, stats)
        kept.append(mixed)
    roll = lambda v: pltpu.roll(v, 64, 1)
    out[0, 0] = jnp.where(lanes < 64, roll(kept[0]), kept[1])
    out[0, 1] = jnp.where(lanes < 64, roll(kept[2]), kept[3])
    out[0, 2] = jnp.where(lanes < 64, roll(kept[4]), 0.0)
    lse[0] = stats


def route_kernel(by_row, requests, cont, crow, src, dst):
    def step(r, carry):
        if by_row:

            @pl.when(cont[r] == 1)
            def _():
                dst[crow[r]] = src[r]

        else:
            dst[r] = src[jnp.where(cont[r] == 1, crow[r], 0)]
        return carry

    lax.fori_loop(0, requests, step, 0)


def row_kernel(requests, chunk, cont, crow, clen, q, kv_ref, out, q_sc, o_sc, s_sc):
    head = pl.program_id(0)
    count = q_sc.shape[1]
    heads = q_sc.shape[0]
    row = lax.axis_index("req")

    def find(r, length):
        mine = jnp.logical_and(cont[r] == 1, crow[r] == row)
        return jnp.where(mine, clen[r], length)

    length = lax.fori_loop(0, requests, find, 0)

    @pl.when(head == 0)
    def _():
        packed = q[...].reshape(-1, LANES)
        for number, tile in enumerate(split_heads(packed, count)):
            q_sc[number] = tile
        s_sc[...] = jnp.zeros_like(s_sc)

    span = kv_ref.shape[2]
    kv = kv_ref[0, 0].astype(F32)
    lanes = lane_iota(span)
    position = lax.broadcasted_iota(jnp.int32, (span, LANES), 0)
    bias = jnp.where(jnp.logical_and(lanes == 64, position >= length), NEG, 0.0)
    keys = jnp.where(lanes < 64, kv, bias).astype(BF16)
    values = jnp.where(lanes < 64, 1.0, kv).astype(BF16)
    scores = lax.dot_general(
        q_sc[head], keys, (((1,), (1,)), ((), ())), preferred_element_type=F32
    )
    mixed, level = soft(scores, values)
    o_sc[head] = mixed
    s_sc[...] = jnp.where(lane_iota(count) == head, level, s_sc[...])

    @pl.when(head == heads - 1)
    def _():
        lanes = lane_iota(count)
        roll = lambda v, n: pltpu.roll(v, n, 1)
        level = s_sc[...]
        high = level.astype(BF16).astype(F32)
        mid = (level - high).astype(BF16).astype(F32)
        low = (level - high - mid).astype(BF16).astype(F32)
        stats = roll(high, 64) + roll(mid, 64 + heads) + roll(low, 64 + 2 * heads)
        tiles = [
            jnp.where(lanes < 64, roll(o_sc[0], 64), o_sc[1]),
            jnp.where(lanes < 64, roll(o_sc[2], 64), o_sc[3]),
            jnp.where(lanes < 64, roll(o_sc[4], 64), stats),
        ]
        to_chunks(out, (), jnp.concatenate(tiles, axis=0).astype(BF16), chunk)


def merge_kernel(req_dev, cont, far, near, lse, mixed):
    heads = 5
    count = near.shape[2]
    b = pl.program_id(0)
    request = lax.axis_index("req") * req_dev + b
    live = cont[request] == 1
    lanes = lane_iota(count)
    roll = lambda v, n: pltpu.roll(v, n, 1)
    packed = far[...].reshape(-1, LANES)
    tiles = [packed[p * count : (p + 1) * count].astype(F32) for p in range(3)]
    stats = roll(tiles[2], 64) + roll(tiles[2], 64 - heads) + roll(tiles[2], 64 - 2 * heads)
    far_level = jnp.where(jnp.logical_and(live, lanes < heads), stats, NEG)
    near_level = lse[0]
    top = jnp.maximum(far_level, near_level)
    far_part = jnp.exp(far_level - top)
    near_part = jnp.exp(near_level - top)
    share = far_part / (far_part + near_part)
    done = []
    for p in range(3):
        left = share[:, 2 * p : 2 * p + 1]
        right = share[:, 2 * p + 1 : 2 * p + 2] if 2 * p + 1 < heads else left
        weight = jnp.where(lanes < 64, left, right)
        done.append(weight * tiles[p] + (1.0 - weight) * near[0, p])
    half = count // 2
    last = jnp.where(lane_iota(half) < 64, done[2][:half], roll(done[2][half:], 64))
    mixed[0] = jnp.concatenate([done[0], done[1], last], axis=0).astype(BF16)


def project_kernel(m0, m1, m2, m3, w0, w1, w2, w3, tok, out, lhs):
    req_dev, count, block = out.shape
    half = count // 2

    @pl.when(pl.program_id(0) == 0)
    def _():
        lanes = lane_iota(half)
        sources = (m0, m1, m2, m3)
        for b in range(req_dev):
            base = b * count
            for number, m in enumerate(sources):
                for p in range(2):
                    col = number * 256 + p * 128
                    lhs[base : base + count, col : col + 128] = m[b, p * count : (p + 1) * count]
            for pair in range(2):
                left = sources[2 * pair][b, 2 * count :].astype(F32)
                right = sources[2 * pair + 1][b, 2 * count :].astype(F32)
                above = jnp.where(lanes < 64, left, pltpu.roll(right, 64, 1))
                below = jnp.where(lanes < 64, pltpu.roll(left, 64, 1), right)
                col = 1024 + pair * 128
                lhs[base : base + half, col : col + 128] = above.astype(BF16)
                lhs[base + half : base + count, col : col + 128] = below.astype(BF16)

    total = tok[...].reshape(req_dev * count, block).astype(F32)
    ws = (w0, w1, w2, w3)
    for number, w in enumerate(ws):
        total += jnp.dot(
            lhs[:, number * 256 : number * 256 + 256], w[:256], preferred_element_type=F32
        )
    rest = jnp.concatenate([w[256:] for w in ws], axis=0)
    total += jnp.dot(lhs[:, 1024:], rest, preferred_element_type=F32)
    out[...] = total.astype(BF16).reshape(req_dev, count, block)


def segment_kernel(segments, stored, own, other, sem):
    place, tp_place = lax.axis_index("req"), lax.axis_index("tp")
    per_side = segments // 2
    mine = (place % 2) * per_side + tp_place
    theirs = (1 - place % 2) * per_side + tp_place
    segment = own.shape[1]
    span = stored.shape[2]
    for which, dst in ((mine, own), (theirs, other)):
        for number in range(segments):
            size = min(segment, span - number * segment)
            if size <= 0:
                continue

            @pl.when(which == number)
            def _():
                copy = pltpu.make_async_copy(
                    stored.at[0, :, pl.ds(number * segment, size), :],
                    dst.at[:, pl.ds(0, size), :],
                    sem,
                )
                copy.start()
                copy.wait()


def cache_kernel(req_dev, cont, crow, clen, rows, mine, theirs, out, wide, cached, sem):
    l = pl.program_id(0)
    place, tp_place = lax.axis_index("req"), lax.axis_index("tp")
    side = place % 2
    kv_heads, segment = out.shape[1], out.shape[2]
    count = mine.shape[2]
    tp_count = lax.axis_size("tp")
    request = (place // 2) * 2 * req_dev + l
    length = live_length(cont, clen, request)
    row = jnp.where(cont[request] == 1, crow[request], 0)
    copy = pltpu.make_async_copy(rows.at[row // 2, (row % 2) ^ side], cached, sem)
    copy.start()
    start = (side * tp_count + tp_place) * segment
    shift = jnp.clip(start - length, -segment, count) + segment
    position = start + lax.broadcasted_iota(jnp.int32, (segment, LANES), 0)
    old = position < length
    new = jnp.logical_and(position >= length, position < length + count)
    local = l // req_dev == side
    copy.wait()
    for head in range(kv_heads):

        @pl.when(local)
        def _():
            wide[segment : segment + count] = mine[0, head].astype(F32)

        @pl.when(jnp.logical_not(local))
        def _():
            wide[segment : segment + count] = theirs[0, head].astype(F32)

        moved = wide[pl.ds(shift, segment), :]
        kept = cached[head].astype(F32)
        out[0, head] = jnp.where(old, kept, jnp.where(new, moved, 0.0)).astype(BF16)


def permuted(value, axis, mask):
    pairs = [(source, source ^ mask) for source in range(lax.axis_size(axis))]
    return lax.ppermute(value, axis, pairs)


def exchanged(value):
    return lax.all_to_all(value, "req", split_axis=0, concat_axis=0, tiled=True)


def full(shape):
    return pl.BlockSpec(shape, lambda *_: (0,) * len(shape))


def on_device(
    tokens,
    attn_gain,
    w_query,
    key_value_weight,
    w_out,
    q_gain,
    k_gain,
    stored,
    continuing,
    cache_row,
    cache_len,
):
    n_req = lax.axis_size("req")
    tp_count = lax.axis_size("tp")
    req_dev, count, width = tokens.shape
    head_dim = q_gain.shape[0]
    kv_heads = key_value_weight.shape[1] // (2 * head_dim)
    heads = w_query.shape[1] // head_dim
    groups = heads * tp_count // kv_heads
    span = stored.shape[2]
    requests = continuing.shape[0]
    segments = 2 * tp_count
    segment = (span + count) // segments
    q_rows = heads * head_dim * count // LANES
    o_rows = -(-heads * head_dim // LANES) * count
    q_chunk = -(-q_rows // (16 * n_req)) * 16
    o_chunk = -(-o_rows // (16 * n_req)) * 16

    tables = tuple(jnp.asarray(t) for t in angle_tables(head_dim, count, span))
    table_specs = [full(t.shape) for t in tables]
    gain_row = attn_gain.reshape(1, width)
    q_gain_row = jnp.tile(q_gain.reshape(1, head_dim), (1, LANES // head_dim))
    k_gain_row = jnp.tile(k_gain.reshape(1, head_dim), (1, LANES // head_dim))
    any_spec = pl.BlockSpec(memory_space=pl.ANY)

    own_part, other_part = pl.pallas_call(
        functools.partial(segment_kernel, segments),
        out_shape=(jax.ShapeDtypeStruct((kv_heads, segment, LANES), BF16),) * 2,
        in_specs=[any_spec],
        out_specs=(any_spec, any_spec),
        scratch_shapes=[pltpu.SemaphoreType.DMA],
        compiler_params=params(),
        cost_estimate=cost(0, 4 * kv_heads * segment * LANES * 2),
        name="segments",
    )(stored)
    partner_part = permuted(other_part, "req", 1)
    both = jnp.stack([own_part, partner_part])
    column = [list(range(side, n_req, 2)) for side in range(2)]
    rows = lax.all_gather(both, "req", axis_index_groups=column)

    w_x = permuted(w_out, "tp", tp_count // 2)
    w_c = permuted(w_out, "tp", 1)
    w_xc = permuted(w_x, "tp", 1)

    normed, q = pl.pallas_call(
        functools.partial(query_kernel, req_dev, q_chunk),
        grid=(req_dev,),
        out_shape=(
            jax.ShapeDtypeStruct(tokens.shape, BF16),
            jax.ShapeDtypeStruct((n_req, req_dev, q_chunk, LANES), BF16),
        ),
        in_specs=[
            SMEM,
            SMEM,
            pl.BlockSpec((1, count, width), lambda b: (b, 0, 0)),
            full((1, width)),
            full(w_query.shape),
            full((1, LANES)),
        ]
        + table_specs,
        out_specs=(
            pl.BlockSpec((1, count, width), lambda b: (b, 0, 0)),
            pl.BlockSpec((n_req, 1, q_chunk, LANES), lambda b: (0, b, 0, 0)),
        ),
        compiler_params=params(),
        cost_estimate=cost(2 * req_dev * count * width * 384, 6 << 20),
        name="query",
    )(continuing, cache_len, tokens, gain_row, w_query, q_gain_row, *tables)

    q_mid = exchanged(q).reshape(requests, q_chunk, LANES)

    fresh = pl.pallas_call(
        functools.partial(fresh_kernel, req_dev),
        grid=(req_dev,),
        out_shape=jax.ShapeDtypeStruct((req_dev, kv_heads, count, LANES), BF16),
        in_specs=[
            SMEM,
            SMEM,
            pl.BlockSpec((1, count, width), lambda b: (b, 0, 0)),
            full(key_value_weight.shape),
            full((1, LANES)),
        ]
        + table_specs,
        out_specs=pl.BlockSpec((1, kv_heads, count, LANES), lambda b: (b, 0, 0, 0)),
        compiler_params=params(),
        cost_estimate=cost(2 * req_dev * count * width * 640, 6 << 20),
        name="fresh",
    )(continuing, cache_len, normed, key_value_weight, k_gain_row, *tables)
    fresh_partner = permuted(fresh, "req", 1)

    near, near_lse = pl.pallas_call(
        functools.partial(local_kernel, groups),
        grid=(req_dev,),
        out_shape=(
            jax.ShapeDtypeStruct((req_dev, 3, count, LANES), F32),
            jax.ShapeDtypeStruct((req_dev, count, LANES), F32),
        ),
        in_specs=[
            pl.BlockSpec((n_req, 1, q_chunk, LANES), lambda b: (0, b, 0, 0)),
            pl.BlockSpec((1, kv_heads, count, LANES), lambda b: (b, 0, 0, 0)),
        ],
        out_specs=(
            pl.BlockSpec((1, 3, count, LANES), lambda b: (b, 0, 0, 0)),
            pl.BlockSpec((1, count, LANES), lambda b: (b, 0, 0)),
        ),
        compiler_params=params(),
        cost_estimate=cost(4 * req_dev * heads * count * count * 256, 4 << 20),
        name="attend_new",
    )(q, fresh)

    q_out = pl.pallas_call(
        functools.partial(route_kernel, True, requests),
        out_shape=jax.ShapeDtypeStruct((n_req, q_chunk, LANES), BF16),
        in_specs=[SMEM, SMEM, pl.BlockSpec(memory_space=pltpu.VMEM)],
        out_specs=pl.BlockSpec(memory_space=pltpu.VMEM),
        compiler_params=params(),
        cost_estimate=cost(0, 1 << 20),
        name="route_query",
    )(continuing, cache_row, q_mid)
    q_row = exchanged(q_out)

    def kv_index(h):
        return (0, (lax.axis_index("tp") * heads + h) // groups, 0, 0)

    far = pl.pallas_call(
        functools.partial(row_kernel, requests, o_chunk),
        grid=(heads,),
        out_shape=jax.ShapeDtypeStruct((n_req, o_chunk, LANES), BF16),
        in_specs=[
            SMEM,
            SMEM,
            SMEM,
            full((n_req, q_chunk, LANES)),
            pl.BlockSpec((1, 1, span, LANES), kv_index),
        ],
        out_specs=full((n_req, o_chunk, LANES)),
        scratch_shapes=[
            pltpu.VMEM((heads, count, LANES), BF16),
            pltpu.VMEM((heads, count, LANES), F32),
            pltpu.VMEM((count, LANES), F32),
        ],
        compiler_params=params(),
        cost_estimate=cost(4 * heads * count * span * 256, 2 << 20),
        name="attend_row",
    )(continuing, cache_row, cache_len, q_row, stored)

    far_mid = exchanged(far)
    far_out = pl.pallas_call(
        functools.partial(route_kernel, False, requests),
        out_shape=jax.ShapeDtypeStruct((requests, o_chunk, LANES), BF16),
        in_specs=[SMEM, SMEM, pl.BlockSpec(memory_space=pltpu.VMEM)],
        out_specs=pl.BlockSpec(memory_space=pltpu.VMEM),
        compiler_params=params(),
        cost_estimate=cost(0, 1 << 20),
        name="route_result",
    )(continuing, cache_row, far_mid)
    far_home = exchanged(far_out.reshape(n_req, req_dev, o_chunk, LANES))

    mixed = pl.pallas_call(
        functools.partial(merge_kernel, req_dev),
        grid=(req_dev,),
        out_shape=jax.ShapeDtypeStruct((req_dev, q_rows, LANES), BF16),
        in_specs=[
            SMEM,
            pl.BlockSpec((n_req, 1, o_chunk, LANES), lambda b: (0, b, 0, 0)),
            pl.BlockSpec((1, 3, count, LANES), lambda b: (b, 0, 0, 0)),
            pl.BlockSpec((1, count, LANES), lambda b: (b, 0, 0)),
        ],
        out_specs=pl.BlockSpec((1, q_rows, LANES), lambda b: (b, 0, 0)),
        compiler_params=params(),
        cost_estimate=cost(0, 3 << 20),
        name="merge",
    )(continuing, far_home, near, near_lse)

    m_x = permuted(mixed, "tp", tp_count // 2)
    m_c = permuted(mixed, "tp", 1)
    m_xc = permuted(m_x, "tp", 1)

    block = 512
    m_spec = full((req_dev, q_rows, LANES))
    w_spec = pl.BlockSpec((heads * head_dim, block), lambda n: (0, n))
    t_spec = pl.BlockSpec((req_dev, count, block), lambda n: (0, 0, n))
    layer = pl.pallas_call(
        project_kernel,
        grid=(width // block,),
        out_shape=jax.ShapeDtypeStruct(tokens.shape, BF16),
        in_specs=[m_spec] * 4 + [w_spec] * 4 + [t_spec],
        out_specs=t_spec,
        scratch_shapes=[pltpu.VMEM((req_dev * count, 1280), BF16)],
        compiler_params=params(),
        cost_estimate=cost(2 * req_dev * count * width * 1280, 10 << 20),
        name="project",
    )(mixed, m_x, m_c, m_xc, w_out, w_x, w_c, w_xc, tokens)

    new_spec = pl.BlockSpec((1, kv_heads, count, LANES), lambda l: (l % req_dev, 0, 0, 0))
    cache = pl.pallas_call(
        functools.partial(cache_kernel, req_dev),
        grid=(2 * req_dev,),
        out_shape=jax.ShapeDtypeStruct((2 * req_dev, kv_heads, segment, LANES), BF16),
        in_specs=[SMEM, SMEM, SMEM, any_spec, new_spec, new_spec],
        out_specs=pl.BlockSpec((1, kv_heads, segment, LANES), lambda l: (l, 0, 0, 0)),
        scratch_shapes=[
            pltpu.VMEM((2 * segment + count, LANES), F32),
            pltpu.VMEM((kv_heads, segment, LANES), BF16),
            pltpu.SemaphoreType.DMA,
        ],
        compiler_params=params(),
        cost_estimate=cost(0, 5 << 20),
        name="cache",
    )(continuing, cache_row, cache_len, rows, fresh, fresh_partner)
    return (layer, cache)


def solution(mesh):
    return jax.shard_map(
        on_device,
        mesh=mesh,
        in_specs=(
            P("req", None, None),
            P(),
            P(None, "tp"),
            P(),
            P("tp", None),
            P(),
            P(),
            P("req", None, None, None),
            P(),
            P(),
            P(),
        ),
        out_specs=(P("req", None, None), P("req", None, "tp", None)),
        check_vma=False,
    )
```

```python
import functools
import math

import jax
import jax.numpy as jnp
import numpy as np
from jax import lax
from jax.experimental import pallas as pl
from jax.experimental.pallas import tpu as pltpu
from jax.sharding import PartitionSpec as P

BF16 = jnp.bfloat16
F32 = jnp.float32
LANES = 128
EPS = 1e-06
NEG = -1e30
SMEM = pl.BlockSpec(memory_space=pltpu.SMEM)


HINT = pl.CostEstimate(flops=0, bytes_accessed=1024, transcendentals=0)


def cost(flops, moved):
    return pl.CostEstimate(flops=int(flops), bytes_accessed=int(moved), transcendentals=0)


def params(mib=20):
    return pltpu.CompilerParams(vmem_limit_bytes=mib << 20)


def lane_iota(rows):
    return lax.broadcasted_iota(jnp.int32, (rows, LANES), 1)


def angle_tables(head_dim, new_count, cache_span):
    half = head_dim // 2
    freq = np.exp(-math.log(10000.0) * np.arange(half, dtype=np.float64) * 2.0 / head_dim)
    freq = np.tile(freq.astype(np.float32).astype(np.float64), LANES // half)

    def pair(positions):
        angle = positions[:, None].astype(np.float64) * freq[None, :]
        return np.cos(angle).astype(np.float32), np.sin(angle).astype(np.float32)

    fine = pair(np.arange(new_count))
    coarse = pair(np.arange(cache_span // 16 + 8) * 16)
    small = pair(np.arange(16))
    return np.stack([np.concatenate(part) for part in zip(fine, small, coarse)])


def rotation(length, count, table):
    high = length // 16
    low = length - high * 16
    row = lambda which, place: table[which, pl.ds(place, 1), :]
    ch, sh = row(0, count + 16 + high), row(1, count + 16 + high)
    cl, sl = row(0, count + low), row(1, count + low)
    cb, sb = ch * cl - sh * sl, sh * cl + ch * sl
    ci, si = table[0, :count], table[1, :count]
    cosine = ci * cb - si * sb
    sine = si * cb + ci * sb
    lanes = lane_iota(ci.shape[0])
    return cosine, jnp.where(lanes % 64 < 32, -sine, sine)


def norm_rope(tile, gain, cosine, sine, blocks):
    square = tile * tile
    high = square.astype(BF16)
    low = (square - high.astype(F32)).astype(BF16)
    mean = jnp.dot(high, blocks, preferred_element_type=F32) + jnp.dot(
        low, blocks, preferred_element_type=F32
    )
    unit = tile * lax.rsqrt(mean + EPS) * gain
    lanes = lane_iota(tile.shape[0])
    other = jnp.where(lanes % 64 < 32, pltpu.roll(unit, 96, 1), pltpu.roll(unit, 32, 1))
    return unit * cosine + other * sine


def half_blocks():
    rows = lax.broadcasted_iota(jnp.int32, (LANES, LANES), 0)
    cols = lax.broadcasted_iota(jnp.int32, (LANES, LANES), 1)
    return jnp.where(rows // 64 == cols // 64, 1.0 / 64.0, 0.0).astype(BF16)


def live(meta, request):
    return meta[0, request] == 1


def live_length(meta, request):
    return jnp.where(live(meta, request), meta[2, request], 0)


def to_chunks(ref, lead, value, chunk):
    rows = value.shape[0]
    for start in range(0, rows, chunk):
        size = min(chunk, rows - start)
        ref[(start // chunk,) + lead + (pl.ds(0, size),)] = value[start : start + size]


def normalized(tok, gain):
    x = tok[0].astype(F32)
    mean = jnp.mean(x * x, axis=-1, keepdims=True)
    return (x * lax.rsqrt(mean + EPS) * gain[...]).astype(BF16)


def query_kernel(req_dev, chunk, cont, clen, tok, gain, w, qg, table, q):
    b = pl.program_id(0)
    count = tok.shape[1]
    half = count // 2
    request = lax.axis_index("req") * req_dev + b
    length = jnp.where(cont[request] == 1, clen[request], 0)
    out = lax.dot_general(
        normalized(tok, gain), w[...], (((1,), (1,)), ((), ())), preferred_element_type=F32
    )
    cosine, sine = rotation(length, count, table)
    blocks = half_blocks()
    gains = jnp.concatenate([qg[...]] * 2, axis=1)
    pair01 = norm_rope(out[:, :128], gains, cosine, sine, blocks)
    pair23 = norm_rope(out[:, 128:256], gains, cosine, sine, blocks)
    last = out[:, 256:320]
    last = jnp.concatenate([last[:half], last[half:]], axis=1)
    lanes = lane_iota(half)
    pick = lambda v: jnp.where(lanes < 64, v[:half], v[half:])
    last = norm_rope(last, gains, pick(cosine), pick(sine), blocks)
    packed = (jnp.concatenate([pair01, pair23, last], axis=0) * 0.125).astype(BF16)
    to_chunks(q, (0,), packed, chunk)


def fresh_kernel(req_dev, meta, tok, gain, w, kg, table, after, fresh):
    del after
    b = pl.program_id(0)
    count = tok.shape[1]
    length = live_length(meta, lax.axis_index("req") * req_dev + b)
    out = jnp.dot(normalized(tok, gain), w[...], preferred_element_type=F32)
    cosine, sine = rotation(length, count, table)
    blocks = half_blocks()
    lanes = lane_iota(count)
    gains = jnp.concatenate([kg[...]] * 2, axis=1)
    for head in range(fresh.shape[1]):
        tile = out[:, head * 128 : head * 128 + 128]
        keys = norm_rope(tile, gains, cosine, sine, blocks)
        fresh[0, head] = jnp.where(lanes < 64, keys, tile).astype(BF16)


def split_heads(packed, count):
    half = count // 2
    wide = packed.astype(F32)
    lanes = lane_iota(count)
    tiles = [wide[:count], pltpu.roll(wide[:count], 64, 1)]
    tiles += [wide[count : 2 * count], pltpu.roll(wide[count : 2 * count], 64, 1)]
    last = wide[2 * count : 2 * count + half]
    tiles.append(jnp.concatenate([last, pltpu.roll(last, 64, 1)], axis=0))
    return [jnp.where(lanes < 64, tile, 0.0).astype(BF16) for tile in tiles]


def soft(scores, values):
    top = jnp.max(scores, axis=-1, keepdims=True)
    weights = jnp.exp(scores - top)
    total = jnp.sum(weights, axis=-1, keepdims=True)
    out = jnp.dot(weights.astype(BF16), values, preferred_element_type=F32)
    return out / total, top + jnp.log(total)


def local_kernel(groups, q, fresh, out):
    heads = 5
    count = fresh.shape[2]
    first = lax.axis_index("tp") * heads
    lanes = lane_iota(count)
    rows = lax.broadcasted_iota(jnp.int32, (count, count), 0)
    cols = lax.broadcasted_iota(jnp.int32, (count, count), 1)
    packed = q[...].reshape(-1, LANES)
    tiles = split_heads(packed, count)
    stats = jnp.zeros((count, LANES), F32)
    kept = []
    for head in range(heads):
        kv = fresh[0, (first + head) // groups]
        scores = lax.dot_general(
            tiles[head], kv, (((1,), (1,)), ((), ())), preferred_element_type=F32
        )
        scores = jnp.where(cols <= rows, scores, NEG)
        mixed, level = soft(scores, kv)
        stats = jnp.where(lanes == head, level, stats)
        kept.append(mixed)
    roll = lambda v: pltpu.roll(v, 64, 1)
    out[0, 0] = jnp.where(lanes < 64, roll(kept[0]), kept[1])
    out[0, 1] = jnp.where(lanes < 64, roll(kept[2]), kept[3])
    out[0, 2] = jnp.where(lanes < 64, roll(kept[4]), roll(stats))


def each(requests, step):
    if requests <= 32:
        for r in range(requests):
            step(r)
    else:
        pl.loop(0, requests)(step)


def route_query_kernel(requests, meta, src, dst):
    def step(r):
        @pl.when(live(meta, r))
        def _():
            dst[meta[1, r]] = src[r]

    each(requests, step)


def route_result_kernel(requests, meta, src, dst):
    def step(r):
        dst[r] = src[jnp.where(live(meta, r), meta[1, r], 0)]

    each(requests, step)


def row_kernel(requests, groups, chunk, meta, q, stored, out, q_sc, o_sc, s_sc, kv_sc, b_sc, sem):
    head = pl.program_id(0)
    heads, count = q_sc.shape[:2]
    span, kv_heads = kv_sc.shape[1], stored.shape[1]
    first = lax.axis_index("tp") * heads // groups
    which = (lax.axis_index("tp") * heads + head) // groups - first

    def fetch(number):
        source = stored.at[0, jnp.minimum(first + number, kv_heads - 1)]
        return pltpu.make_async_copy(source, kv_sc.at[number], sem.at[number])

    @pl.when(head == 0)
    def _():
        fetch(0).start()
        fetch(1).start()
        row = lax.axis_index("req")

        def find(r, length):
            mine = jnp.logical_and(live(meta, r), meta[1, r] == row)
            return jnp.where(mine, meta[2, r], length)

        length = lax.fori_loop(0, requests, find, 0)
        position = lax.broadcasted_iota(jnp.int32, (8, span), 1)
        b_sc[...] = jnp.where(position < length, 0.0, NEG)
        packed = q[...].reshape(-1, LANES)
        for number, tile in enumerate(split_heads(packed, count)):
            q_sc[number] = tile
        s_sc[...] = jnp.zeros_like(s_sc)
        fetch(0).wait()
        fetch(1).wait()

    kv = kv_sc[which]
    scores = lax.dot_general(
        q_sc[head], kv, (((1,), (1,)), ((), ())), preferred_element_type=F32
    )
    mixed, level = soft(scores + b_sc[0:1, :], kv)
    o_sc[head] = mixed
    s_sc[...] = jnp.where(lane_iota(count) == head, level, s_sc[...])

    @pl.when(head == heads - 1)
    def _():
        lanes = lane_iota(count)
        roll = lambda v, n: pltpu.roll(v, n, 1)
        level = s_sc[...]
        high = level.astype(BF16).astype(F32)
        mid = (level - high).astype(BF16).astype(F32)
        low = (level - high - mid).astype(BF16).astype(F32)
        stats = roll(high, 64) + roll(mid, 64 + heads) + roll(low, 64 + 2 * heads)
        tiles = [
            jnp.where(lanes < 64, roll(o_sc[0], 64), o_sc[1]),
            jnp.where(lanes < 64, roll(o_sc[2], 64), o_sc[3]),
            jnp.where(lanes < 64, roll(o_sc[4], 64), stats),
        ]
        to_chunks(out, (), jnp.concatenate(tiles, axis=0).astype(BF16), chunk)


def merge_kernel(req_dev, meta, far, near, mixed):
    heads = 5
    count = near.shape[2]
    b = pl.program_id(0)
    request = lax.axis_index("req") * req_dev + b
    lanes = lane_iota(count)
    roll = lambda v, n: pltpu.roll(v, n, 1)
    packed = far[...].reshape(-1, LANES)
    tiles = [packed[p * count : (p + 1) * count].astype(F32) for p in range(3)]
    stats = roll(tiles[2], 64) + roll(tiles[2], 64 - heads) + roll(tiles[2], 64 - 2 * heads)
    far_level = jnp.where(jnp.logical_and(live(meta, request), lanes < heads), stats, NEG)
    near_level = jnp.where(lanes < heads, roll(near[0, 2], 64), 0.0)
    top = jnp.maximum(far_level, near_level)
    far_part = jnp.exp(far_level - top)
    near_part = jnp.exp(near_level - top)
    share = far_part / (far_part + near_part)
    done = []
    for p in range(3):
        left = share[:, 2 * p : 2 * p + 1]
        right = share[:, 2 * p + 1 : 2 * p + 2] if 2 * p + 1 < heads else left
        weight = jnp.where(lanes < 64, left, right)
        done.append(weight * tiles[p] + (1.0 - weight) * near[0, p])
    half = count // 2
    last = jnp.where(lane_iota(half) < 64, done[2][:half], roll(done[2][half:], 64))
    mixed[0] = jnp.concatenate([done[0], done[1], last], axis=0).astype(BF16)


def project_kernel(m_a, m_b, w_a, w_b, base, out, lhs):
    req_dev, count, block = out.shape
    half = count // 2
    sources = (m_a, m_b)

    @pl.when(pl.program_id(0) == 0)
    def _():
        lanes = lane_iota(half)
        for b in range(req_dev):
            start = b * count
            for number, m in enumerate(sources):
                for p in range(2):
                    col = number * 256 + p * 128
                    lhs[start : start + count, col : col + 128] = m[b, p * count : (p + 1) * count]
            left = m_a[b, 2 * count :].astype(F32)
            right = m_b[b, 2 * count :].astype(F32)
            above = jnp.where(lanes < 64, left, pltpu.roll(right, 64, 1))
            below = jnp.where(lanes < 64, pltpu.roll(left, 64, 1), right)
            lhs[start : start + half, 512:640] = above.astype(BF16)
            lhs[start + half : start + count, 512:640] = below.astype(BF16)

    total = base[...].reshape(req_dev * count, block).astype(F32)
    weights = jnp.concatenate([w_a[:256], w_b[:256], w_a[256:], w_b[256:]], axis=0)
    total += jnp.dot(lhs[...], weights, preferred_element_type=F32)
    out[...] = total.astype(out.dtype).reshape(req_dev, count, block)


def held(plane, here):
    apart = plane ^ here
    mid = jnp.logical_or(here == 1, here == 2)
    return jnp.where(apart < 2, apart, jnp.where(mid, 5 - apart, 2 + apart))


def cache_kernel(req_dev, span, meta, *refs):
    blocks, (mine, theirs, _, out, wide, kept_sc, sem) = refs[:-7], refs[-7:]
    l = pl.program_id(0)
    place, tp_place = lax.axis_index("req"), lax.axis_index("tp")
    side = place % 2
    kv_heads, segment = out.shape[1], out.shape[2]
    count = mine.shape[2]

    def fetch(number, action):
        request = (place // 2) * 2 * req_dev + number
        row = jnp.where(live(meta, request), meta[1, request], 0)
        plane, which = row // 2, (row % 2) ^ side
        dst = kept_sc.at[number, :, pl.ds(0, segment), :]
        if len(blocks) == 1:
            action(pltpu.make_async_copy(blocks[0].at[plane, which], dst, sem.at[number]))
            return
        for step, block in enumerate(blocks):

            @pl.when(held(plane, place // 2) == step)
            def _():
                action(pltpu.make_async_copy(block.at[which], dst, sem.at[number]))

    @pl.when(l == 0)
    def _():
        for number in range(2 * req_dev):
            fetch(number, lambda copy: copy.start())

    length = live_length(meta, (place // 2) * 2 * req_dev + l)
    start = (side * lax.axis_size("tp") + tp_place) * segment
    skip = pl.multiple_of(start - jnp.minimum(start, span - segment), 16)
    shift = jnp.clip(start - length, -segment, count) + segment
    position = start + lax.broadcasted_iota(jnp.int32, (segment, LANES), 0)
    old = position < length
    new = jnp.logical_and(position >= length, position < length + count)
    local = l // req_dev == side
    for head in range(kv_heads):

        @pl.when(local)
        def _():
            wide[head, segment : segment + count] = mine[0, head].astype(F32)

        @pl.when(jnp.logical_not(local))
        def _():
            wide[head, segment : segment + count] = theirs[0, head].astype(F32)

    fetch(l, lambda copy: copy.wait())
    for head in range(kv_heads):
        moved = wide[head, pl.ds(shift, segment), :]
        kept = kept_sc[l, head, pl.ds(skip, segment), :].astype(F32)
        out[0, head] = jnp.where(old, kept, jnp.where(new, moved, 0.0)).astype(BF16)


def permuted(value, axis, mask):
    pairs = [(source, source ^ mask) for source in range(lax.axis_size(axis))]
    return lax.ppermute(value, axis, pairs)


def exchanged(value):
    return lax.all_to_all(value, "req", split_axis=0, concat_axis=0, tiled=True)


def full(shape):
    return pl.BlockSpec(shape, lambda *_: (0,) * len(shape))


def on_device(
    tokens,
    attn_gain,
    w_query,
    key_value_weight,
    w_out,
    q_gain,
    k_gain,
    stored,
    continuing,
    cache_row,
    cache_len,
):
    n_req = lax.axis_size("req")
    tp_count = lax.axis_size("tp")
    req_dev, count, width = tokens.shape
    head_dim = q_gain.shape[0]
    kv_heads = key_value_weight.shape[1] // (2 * head_dim)
    heads = w_query.shape[1] // head_dim
    groups = heads * tp_count // kv_heads
    span = stored.shape[2]
    requests = continuing.shape[0]
    segments = 2 * tp_count
    segment = (span + count) // segments
    q_rows = heads * head_dim * count // LANES
    o_rows = -(-heads * head_dim // LANES) * count
    q_chunk = -(-q_rows // (16 * n_req)) * 16
    o_chunk = -(-o_rows // (16 * n_req)) * 16

    table = jnp.asarray(angle_tables(head_dim, count, span))
    table_spec = full(table.shape)
    meta = jnp.stack([continuing, cache_row, cache_len])
    gain_row = attn_gain.reshape(1, width)
    q_gain_row = q_gain.reshape(1, head_dim)
    k_gain_row = k_gain.reshape(1, head_dim)
    w_query_rows = w_query.T
    any_spec = pl.BlockSpec(memory_space=pl.ANY)
    hbm_spec = pl.BlockSpec(memory_space=pltpu.HBM)
    vmem_spec = pl.BlockSpec(memory_space=pltpu.VMEM)
    token_spec = pl.BlockSpec((1, count, width), lambda b: (b, 0, 0))

    side = lax.axis_index("req") % 2
    tp_place = lax.axis_index("tp")

    def part(which):
        start = (which * tp_count + tp_place) * segment
        return lax.dynamic_slice_in_dim(stored[0], start, segment, 1)

    own_part, other_part = part(side), part(1 - side)
    partner_part = permuted(other_part, "req", 1)
    q = pl.pallas_call(
        functools.partial(query_kernel, req_dev, q_chunk),
        grid=(req_dev,),
        out_shape=jax.ShapeDtypeStruct((n_req, req_dev, q_chunk, LANES), BF16),
        in_specs=[
            SMEM,
            SMEM,
            token_spec,
            full((1, width)),
            full(w_query_rows.shape),
            full((1, head_dim)),
            table_spec,
        ],
        out_specs=pl.BlockSpec((n_req, 1, q_chunk, LANES), lambda b: (0, b, 0, 0)),
        compiler_params=params(60),
        cost_estimate=cost(2 * req_dev * count * width * 384, 6 << 20),
        name="query",
    )(continuing, cache_len, tokens, gain_row, w_query_rows, q_gain_row, table)
    q_mid = exchanged(q).reshape(requests, q_chunk, LANES)

    partner_part = lax.optimization_barrier((partner_part, q))[0]
    both = jnp.stack([own_part, partner_part])
    planes = n_req // 2
    hops = planes == 4

    def crossed(value, pairs):
        pairs = [(2 * a + parity, 2 * b + parity) for a, b in pairs for parity in range(2)]
        return lax.ppermute(value, "req", pairs)

    if hops:
        outer = [(z, z ^ 1) for z in range(planes)]
        beside = crossed(both, outer)
        middle = crossed(both, [(1, 2), (2, 1)])
        far_middle = crossed(beside, [(1, 2), (2, 1)])
        outward = crossed(middle, [(1, 0), (2, 3)])
        far_outward = crossed(far_middle, [(1, 0), (2, 3)])
        blocks = [both, beside, middle, far_middle, outward, far_outward]
    else:
        column = [list(range(parity, n_req, 2)) for parity in range(2)]
        blocks = [lax.all_gather(both, "req", axis_index_groups=column)]
        beside = middle = far_middle = outward = both

    w_x = permuted(w_out, "tp", tp_count // 2)
    w_c = permuted(w_out, "tp", 1)
    w_xc = permuted(w_x, "tp", 1)

    fresh = pl.pallas_call(
        functools.partial(fresh_kernel, req_dev),
        grid=(req_dev,),
        out_shape=jax.ShapeDtypeStruct((req_dev, kv_heads, count, LANES), BF16),
        in_specs=[
            SMEM,
            token_spec,
            full((1, width)),
            full(key_value_weight.shape),
            full((1, head_dim)),
            table_spec,
            any_spec,
        ],
        out_specs=pl.BlockSpec((1, kv_heads, count, LANES), lambda b: (b, 0, 0, 0)),
        compiler_params=params(),
        cost_estimate=HINT,
        name="fresh",
    )(meta, tokens, gain_row, key_value_weight, k_gain_row, table, q)

    q_out = pl.pallas_call(
        functools.partial(route_query_kernel, requests),
        out_shape=jax.ShapeDtypeStruct((n_req, q_chunk, LANES), BF16),
        in_specs=[SMEM, vmem_spec],
        out_specs=vmem_spec,
        compiler_params=params(),
        cost_estimate=cost(0, 1 << 20),
        name="route_query",
    )(meta, q_mid)
    q_row = lax.optimization_barrier((exchanged(q_out), beside, middle, fresh))[0]
    fresh_partner = permuted(fresh, "req", 1)

    near = pl.pallas_call(
        functools.partial(local_kernel, groups),
        grid=(req_dev,),
        out_shape=jax.ShapeDtypeStruct((req_dev, 3, count, LANES), F32),
        in_specs=[
            pl.BlockSpec((n_req, 1, q_chunk, LANES), lambda b: (0, b, 0, 0)),
            pl.BlockSpec((1, kv_heads, count, LANES), lambda b: (b, 0, 0, 0)),
        ],
        out_specs=pl.BlockSpec((1, 3, count, LANES), lambda b: (b, 0, 0, 0)),
        compiler_params=params(),
        cost_estimate=HINT,
        name="attend_new",
    )(q, fresh)

    far = pl.pallas_call(
        functools.partial(row_kernel, requests, groups, o_chunk),
        grid=(heads,),
        out_shape=jax.ShapeDtypeStruct((n_req, o_chunk, LANES), BF16),
        in_specs=[SMEM, full((n_req, q_chunk, LANES)), any_spec],
        out_specs=full((n_req, o_chunk, LANES)),
        scratch_shapes=[
            pltpu.VMEM((heads, count, LANES), BF16),
            pltpu.VMEM((heads, count, LANES), F32),
            pltpu.VMEM((count, LANES), F32),
            pltpu.VMEM((2, span, LANES), BF16),
            pltpu.VMEM((8, span), F32),
            pltpu.SemaphoreType.DMA((2,)),
        ],
        compiler_params=params(60),
        cost_estimate=cost(4 * heads * count * span * 256, 32 << 20),
        name="attend_row",
    )(meta, q_row, stored)

    far_mid = exchanged(far)
    far_out = pl.pallas_call(
        functools.partial(route_result_kernel, requests),
        out_shape=jax.ShapeDtypeStruct((requests, o_chunk, LANES), BF16),
        in_specs=[SMEM, vmem_spec],
        out_specs=vmem_spec,
        compiler_params=params(),
        cost_estimate=cost(0, 1 << 20),
        name="route_result",
    )(meta, far_mid)
    far_home = exchanged(far_out.reshape(n_req, req_dev, o_chunk, LANES))
    far_home = lax.optimization_barrier((far_home, far_middle, outward))[0]

    mixed = pl.pallas_call(
        functools.partial(merge_kernel, req_dev),
        grid=(req_dev,),
        out_shape=jax.ShapeDtypeStruct((req_dev, q_rows, LANES), BF16),
        in_specs=[
            SMEM,
            pl.BlockSpec((n_req, 1, o_chunk, LANES), lambda b: (0, b, 0, 0)),
            pl.BlockSpec((1, 3, count, LANES), lambda b: (b, 0, 0, 0)),
        ],
        out_specs=pl.BlockSpec((1, q_rows, LANES), lambda b: (b, 0, 0)),
        compiler_params=params(),
        cost_estimate=HINT,
        name="merge",
    )(meta, far_home, near)

    m_x = permuted(mixed, "tp", tp_count // 2)
    m_c = permuted(mixed, "tp", 1)

    block = 512
    t_spec = pl.BlockSpec((req_dev, count, block), lambda n: (0, 0, n))

    def project(m_a, m_b, w_a, w_b, base, dtype, name):
        m_spec = full((req_dev, q_rows, LANES))
        w_spec = pl.BlockSpec((heads * head_dim, block), lambda n: (0, n))
        return pl.pallas_call(
            project_kernel,
            grid=(width // block,),
            out_shape=jax.ShapeDtypeStruct(tokens.shape, dtype),
            in_specs=[m_spec] * 2 + [w_spec] * 2 + [t_spec],
            out_specs=t_spec,
            scratch_shapes=[pltpu.VMEM((req_dev * count, 640), BF16)],
            compiler_params=params(),
            cost_estimate=cost(2 * req_dev * count * width * 640, 6 << 20),
            name=name,
        )(m_a, m_b, w_a, w_b, base)

    partial = project(mixed, m_c, w_out, w_c, tokens, F32, "project_chip")
    new_spec = pl.BlockSpec((1, kv_heads, count, LANES), lambda l: (l % req_dev, 0, 0, 0))
    cache = pl.pallas_call(
        functools.partial(cache_kernel, req_dev, span),
        grid=(2 * req_dev,),
        in_specs=[SMEM] + [any_spec] * len(blocks) + [new_spec, new_spec, any_spec],
        out_specs=pl.BlockSpec((1, kv_heads, segment, LANES), lambda l: (l, 0, 0, 0)),
        scratch_shapes=[
            pltpu.VMEM((kv_heads, 2 * segment + count, LANES), F32),
            pltpu.VMEM((2 * req_dev, kv_heads, 2 * segment, LANES), BF16),
            pltpu.SemaphoreType.DMA((2 * req_dev,)),
        ],
        out_shape=jax.ShapeDtypeStruct((2 * req_dev, kv_heads, segment, LANES), BF16),
        compiler_params=params(),
        cost_estimate=HINT,
        name="cache",
    )(meta, *blocks, fresh, fresh_partner, partial)
    m_x = lax.optimization_barrier((m_x, partial, cache))[0]
    m_xc = permuted(m_x, "tp", 1)
    layer = project(m_x, m_xc, w_x, w_xc, partial, BF16, "project_rest")

    return (layer, cache)


def solution(mesh):
    return jax.shard_map(
        on_device,
        mesh=mesh,
        in_specs=(
            P("req", None, None),
            P(),
            P(None, "tp"),
            P(),
            P("tp", None),
            P(),
            P(),
            P("req", None, None, None),
            P(),
            P(),
            P(),
        ),
        out_specs=(P("req", None, None), P("req", None, "tp", None)),
        check_vma=False,
    )
```

```python
import functools
import math

import jax
import jax.numpy as jnp
import numpy as np
from jax import lax
from jax.experimental import pallas as pl
from jax.experimental.pallas import tpu as pltpu
from jax.sharding import PartitionSpec as P

BF16 = jnp.bfloat16
F32 = jnp.float32
LANES = 128
EPS = 1e-06
NEG = -1e30
SMEM = pl.BlockSpec(memory_space=pltpu.SMEM)


HINT = pl.CostEstimate(flops=0, bytes_accessed=1024, transcendentals=0)


def cost(flops, moved):
    return pl.CostEstimate(flops=int(flops), bytes_accessed=int(moved), transcendentals=0)


def params(mib=20):
    return pltpu.CompilerParams(vmem_limit_bytes=mib << 20)


def lane_iota(rows):
    return lax.broadcasted_iota(jnp.int32, (rows, LANES), 1)


def angle_tables(head_dim, new_count, cache_span):
    half = head_dim // 2
    freq = np.exp(-math.log(10000.0) * np.arange(half, dtype=np.float64) * 2.0 / head_dim)
    freq = np.tile(freq.astype(np.float32).astype(np.float64), LANES // half)

    def pair(positions):
        angle = positions[:, None].astype(np.float64) * freq[None, :]
        return np.cos(angle).astype(np.float32), np.sin(angle).astype(np.float32)

    fine = pair(np.arange(new_count))
    coarse = pair(np.arange(cache_span // 16 + 8) * 16)
    small = pair(np.arange(16))
    return np.stack([np.concatenate(part) for part in zip(fine, small, coarse)])


def rotation(length, count, table):
    high = length // 16
    low = length - high * 16
    row = lambda which, place: table[which, pl.ds(place, 1), :]
    ch, sh = row(0, count + 16 + high), row(1, count + 16 + high)
    cl, sl = row(0, count + low), row(1, count + low)
    cb, sb = ch * cl - sh * sl, sh * cl + ch * sl
    ci, si = table[0, :count], table[1, :count]
    cosine = ci * cb - si * sb
    sine = si * cb + ci * sb
    lanes = lane_iota(ci.shape[0])
    return cosine, jnp.where(lanes % 64 < 32, -sine, sine)


def norm_rope(tile, gain, cosine, sine, blocks):
    square = tile * tile
    high = square.astype(BF16)
    low = (square - high.astype(F32)).astype(BF16)
    mean = jnp.dot(high, blocks, preferred_element_type=F32) + jnp.dot(
        low, blocks, preferred_element_type=F32
    )
    unit = tile * lax.rsqrt(mean + EPS) * gain
    lanes = lane_iota(tile.shape[0])
    other = jnp.where(lanes % 64 < 32, pltpu.roll(unit, 96, 1), pltpu.roll(unit, 32, 1))
    return unit * cosine + other * sine


def half_blocks():
    rows = lax.broadcasted_iota(jnp.int32, (LANES, LANES), 0)
    cols = lax.broadcasted_iota(jnp.int32, (LANES, LANES), 1)
    return jnp.where(rows // 64 == cols // 64, 1.0 / 64.0, 0.0).astype(BF16)


def live(meta, request):
    return meta[0, request] == 1


def live_length(meta, request):
    return jnp.where(live(meta, request), meta[2, request], 0)


def to_chunks(ref, lead, value, chunk):
    rows = value.shape[0]
    for start in range(0, rows, chunk):
        size = min(chunk, rows - start)
        ref[(start // chunk,) + lead + (pl.ds(0, size),)] = value[start : start + size]


def normalized(tok, gain):
    x = tok[0].astype(F32)
    mean = jnp.mean(x * x, axis=-1, keepdims=True)
    return (x * lax.rsqrt(mean + EPS) * gain[...]).astype(BF16)


def query_kernel(req_dev, chunk, cont, clen, tok, gain, w, qg, table, q):
    b = pl.program_id(0)
    count = tok.shape[1]
    half = count // 2
    request = lax.axis_index("req") * req_dev + b
    length = jnp.where(cont[request] == 1, clen[request], 0)
    out = lax.dot_general(
        normalized(tok, gain), w[...], (((1,), (1,)), ((), ())), preferred_element_type=F32
    )
    cosine, sine = rotation(length, count, table)
    blocks = half_blocks()
    gains = jnp.concatenate([qg[...]] * 2, axis=1)
    pair01 = norm_rope(out[:, :128], gains, cosine, sine, blocks)
    pair23 = norm_rope(out[:, 128:256], gains, cosine, sine, blocks)
    last = out[:, 256:320]
    last = jnp.concatenate([last[:half], last[half:]], axis=1)
    lanes = lane_iota(half)
    pick = lambda v: jnp.where(lanes < 64, v[:half], v[half:])
    last = norm_rope(last, gains, pick(cosine), pick(sine), blocks)
    packed = (jnp.concatenate([pair01, pair23, last], axis=0) * 0.125).astype(BF16)
    to_chunks(q, (0,), packed, chunk)


def fresh_kernel(req_dev, meta, tok, gain, w, kg, table, after, fresh):
    del after
    b = pl.program_id(0)
    count = tok.shape[1]
    length = live_length(meta, lax.axis_index("req") * req_dev + b)
    out = jnp.dot(normalized(tok, gain), w[...], preferred_element_type=F32)
    cosine, sine = rotation(length, count, table)
    blocks = half_blocks()
    lanes = lane_iota(count)
    gains = jnp.concatenate([kg[...]] * 2, axis=1)
    for head in range(fresh.shape[1]):
        tile = out[:, head * 128 : head * 128 + 128]
        keys = norm_rope(tile, gains, cosine, sine, blocks)
        fresh[0, head] = jnp.where(lanes < 64, keys, tile).astype(BF16)


def split_heads(packed, count):
    half = count // 2
    wide = packed.astype(F32)
    lanes = lane_iota(count)
    tiles = [wide[:count], pltpu.roll(wide[:count], 64, 1)]
    tiles += [wide[count : 2 * count], pltpu.roll(wide[count : 2 * count], 64, 1)]
    last = wide[2 * count : 2 * count + half]
    tiles.append(jnp.concatenate([last, pltpu.roll(last, 64, 1)], axis=0))
    return [jnp.where(lanes < 64, tile, 0.0).astype(BF16) for tile in tiles]


def soft(scores, values):
    top = jnp.max(scores, axis=-1, keepdims=True)
    weights = jnp.exp(scores - top)
    total = jnp.sum(weights, axis=-1, keepdims=True)
    out = jnp.dot(weights.astype(BF16), values, preferred_element_type=F32)
    return out / total, top + jnp.log(total)


def local_kernel(groups, q, fresh, out):
    heads = 5
    count = fresh.shape[2]
    first = lax.axis_index("tp") * heads
    lanes = lane_iota(count)
    rows = lax.broadcasted_iota(jnp.int32, (count, count), 0)
    cols = lax.broadcasted_iota(jnp.int32, (count, count), 1)
    packed = q[...].reshape(-1, LANES)
    tiles = split_heads(packed, count)
    stats = jnp.zeros((count, LANES), F32)
    kept = []
    for head in range(heads):
        kv = fresh[0, (first + head) // groups]
        scores = lax.dot_general(
            tiles[head], kv, (((1,), (1,)), ((), ())), preferred_element_type=F32
        )
        scores = jnp.where(cols <= rows, scores, NEG)
        mixed, level = soft(scores, kv)
        stats = jnp.where(lanes == head, level, stats)
        kept.append(mixed)
    roll = lambda v: pltpu.roll(v, 64, 1)
    out[0, 0] = jnp.where(lanes < 64, roll(kept[0]), kept[1])
    out[0, 1] = jnp.where(lanes < 64, roll(kept[2]), kept[3])
    out[0, 2] = jnp.where(lanes < 64, roll(kept[4]), roll(stats))


def each(requests, step):
    if requests <= 32:
        for r in range(requests):
            step(r)
    else:
        pl.loop(0, requests)(step)


def route_query_kernel(requests, meta, src, dst):
    def step(r):
        @pl.when(live(meta, r))
        def _():
            dst[meta[1, r]] = src[r]

    each(requests, step)


def route_result_kernel(requests, meta, src, dst):
    def step(r):
        dst[r] = src[jnp.where(live(meta, r), meta[1, r], 0)]

    each(requests, step)


def row_kernel(requests, count, heads, groups, chunk, meta, q, stored, out, kv_sc, sem):
    span, kv_heads = kv_sc.shape[1], stored.shape[1]
    offset = lax.axis_index("tp") * heads
    first = offset // groups

    def fetch(number):
        source = stored.at[0, jnp.minimum(first + number, kv_heads - 1)]
        return pltpu.make_async_copy(source, kv_sc.at[number], sem.at[number])

    fetch(0).start()
    fetch(1).start()
    row = lax.axis_index("req")

    def find(r, length):
        mine = jnp.logical_and(live(meta, r), meta[1, r] == row)
        return jnp.where(mine, meta[2, r], length)

    length = lax.fori_loop(0, requests, find, 0)
    position = lax.broadcasted_iota(jnp.int32, (8, span), 1)
    bias = jnp.where(position < length, 0.0, NEG)[0:1]
    tiles = split_heads(q[...].reshape(-1, LANES), count)
    lanes = lane_iota(count)
    level = jnp.zeros((count, LANES), F32)
    kept = []
    for head in range(heads):
        if head < 2:
            fetch(head).wait()
        kv = kv_sc[(offset + head) // groups - first]
        scores = lax.dot_general(
            tiles[head], kv, (((1,), (1,)), ((), ())), preferred_element_type=F32
        )
        mixed, one = soft(scores + bias, kv)
        level = jnp.where(lanes == head, one, level)
        kept.append(mixed)
    roll = lambda v, n: pltpu.roll(v, n, 1)
    high = level.astype(BF16).astype(F32)
    mid = (level - high).astype(BF16).astype(F32)
    low = (level - high - mid).astype(BF16).astype(F32)
    stats = roll(high, 64) + roll(mid, 64 + heads) + roll(low, 64 + 2 * heads)
    tiles = [
        jnp.where(lanes < 64, roll(kept[0], 64), kept[1]),
        jnp.where(lanes < 64, roll(kept[2], 64), kept[3]),
        jnp.where(lanes < 64, roll(kept[4], 64), stats),
    ]
    to_chunks(out, (), jnp.concatenate(tiles, axis=0).astype(BF16), chunk)


def merge_kernel(req_dev, meta, far, near, mixed):
    heads = 5
    count = near.shape[2]
    b = pl.program_id(0)
    request = lax.axis_index("req") * req_dev + b
    lanes = lane_iota(count)
    roll = lambda v, n: pltpu.roll(v, n, 1)
    packed = far[...].reshape(-1, LANES)
    tiles = [packed[p * count : (p + 1) * count].astype(F32) for p in range(3)]
    stats = roll(tiles[2], 64) + roll(tiles[2], 64 - heads) + roll(tiles[2], 64 - 2 * heads)
    far_level = jnp.where(jnp.logical_and(live(meta, request), lanes < heads), stats, NEG)
    near_level = jnp.where(lanes < heads, roll(near[0, 2], 64), 0.0)
    top = jnp.maximum(far_level, near_level)
    far_part = jnp.exp(far_level - top)
    near_part = jnp.exp(near_level - top)
    share = far_part / (far_part + near_part)
    done = []
    for p in range(3):
        left = share[:, 2 * p : 2 * p + 1]
        right = share[:, 2 * p + 1 : 2 * p + 2] if 2 * p + 1 < heads else left
        weight = jnp.where(lanes < 64, left, right)
        done.append(weight * tiles[p] + (1.0 - weight) * near[0, p])
    half = count // 2
    last = jnp.where(lane_iota(half) < 64, done[2][:half], roll(done[2][half:], 64))
    mixed[0] = jnp.concatenate([done[0], done[1], last], axis=0).astype(BF16)


def project_kernel(block, m_a, m_b, w_a, w_b, base, out, lhs):
    count, width = out.shape[1:]
    half = count // 2
    lanes = lane_iota(half)
    for number, m in enumerate((m_a, m_b)):
        for p in range(2):
            col = number * 256 + p * 128
            lhs[:, col : col + 128] = m[0, p * count : (p + 1) * count]
    left = m_a[0, 2 * count :].astype(F32)
    right = m_b[0, 2 * count :].astype(F32)
    lhs[:half, 512:] = jnp.where(lanes < 64, left, pltpu.roll(right, 64, 1)).astype(BF16)
    lhs[half:, 512:] = jnp.where(lanes < 64, pltpu.roll(left, 64, 1), right).astype(BF16)
    for start in range(0, width, block):
        part = pl.ds(start, block)
        weights = jnp.concatenate(
            [w_a[:256, part], w_b[:256, part], w_a[256:, part], w_b[256:, part]], axis=0
        )
        total = base[0, :, part].astype(F32)
        total += jnp.dot(lhs[...], weights, preferred_element_type=F32)
        out[0, :, part] = total.astype(out.dtype)


def held(plane, here):
    apart = plane ^ here
    mid = jnp.logical_or(here == 1, here == 2)
    return jnp.where(apart < 2, apart, jnp.where(mid, 5 - apart, 2 + apart))


def cache_kernel(req_dev, span, meta, *refs):
    blocks, (mine, theirs, _, out, kept_sc, out_sc, sem, out_sem) = refs[:-8], refs[-8:]
    place, tp_place = lax.axis_index("req"), lax.axis_index("tp")
    side = place % 2
    kv_heads, segment = out.shape[1], out.shape[2]
    count = mine.shape[2]
    start = (side * lax.axis_size("tp") + tp_place) * segment
    skip = pl.multiple_of(start - jnp.minimum(start, span - segment), 16)
    first = (place // 2) * 2 * req_dev

    def fetch(number, action):
        row = jnp.where(live(meta, first + number), meta[1, first + number], 0)
        plane, which = row // 2, (row % 2) ^ side
        dst = kept_sc.at[number, :, pl.ds(0, segment), :]
        if len(blocks) == 1:
            action(pltpu.make_async_copy(blocks[0].at[plane, which], dst, sem.at[number]))
            return
        for step, block in enumerate(blocks):

            @pl.when(held(plane, place // 2) == step)
            def _():
                action(pltpu.make_async_copy(block.at[which], dst, sem.at[number]))

    def write(number):
        return pltpu.make_async_copy(out_sc.at[number], out.at[number], out_sem.at[number])

    for number in range(2 * req_dev):
        fetch(number, lambda copy: copy.start())
    rows = lax.broadcasted_iota(jnp.int32, (segment, count), 0)
    cols = lax.broadcasted_iota(jnp.int32, (segment, count), 1)
    for number in range(2 * req_dev):
        ahead = live_length(meta, first + number) - start
        shift = jnp.where(rows - cols == ahead, 1.0, 0.0).astype(BF16)
        local = number // req_dev == side
        place_of = number % req_dev
        new = jnp.concatenate(
            [jnp.where(local, mine[place_of, h], theirs[place_of, h]) for h in range(kv_heads)],
            axis=1,
        )
        moved = jnp.dot(shift, new, preferred_element_type=F32)
        old = lax.broadcasted_iota(jnp.int32, (segment, LANES), 0) < ahead
        fetch(number, lambda copy: copy.wait())
        for head in range(kv_heads):
            kept = kept_sc[number, head, pl.ds(skip, segment), :].astype(F32)
            part = moved[:, head * LANES : head * LANES + LANES]
            out_sc[number, head] = jnp.where(old, kept, part).astype(BF16)
        write(number).start()
    for number in range(2 * req_dev):
        write(number).wait()


def permuted(value, axis, mask):
    pairs = [(source, source ^ mask) for source in range(lax.axis_size(axis))]
    return lax.ppermute(value, axis, pairs)


def exchanged(value):
    return lax.all_to_all(value, "req", split_axis=0, concat_axis=0, tiled=True)


def full(shape):
    return pl.BlockSpec(shape, lambda *_: (0,) * len(shape))


def on_device(
    tokens,
    attn_gain,
    w_query,
    key_value_weight,
    w_out,
    q_gain,
    k_gain,
    stored,
    continuing,
    cache_row,
    cache_len,
):
    n_req = lax.axis_size("req")
    tp_count = lax.axis_size("tp")
    req_dev, count, width = tokens.shape
    head_dim = q_gain.shape[0]
    kv_heads = key_value_weight.shape[1] // (2 * head_dim)
    heads = w_query.shape[1] // head_dim
    groups = heads * tp_count // kv_heads
    span = stored.shape[2]
    requests = continuing.shape[0]
    segments = 2 * tp_count
    segment = (span + count) // segments
    q_rows = heads * head_dim * count // LANES
    o_rows = -(-heads * head_dim // LANES) * count
    q_chunk = -(-q_rows // (16 * n_req)) * 16
    o_chunk = -(-o_rows // (16 * n_req)) * 16

    table = jnp.asarray(angle_tables(head_dim, count, span))
    table_spec = full(table.shape)
    meta = jnp.stack([continuing, cache_row, cache_len])
    gain_row = attn_gain.reshape(1, width)
    q_gain_row = q_gain.reshape(1, head_dim)
    k_gain_row = k_gain.reshape(1, head_dim)
    w_query_rows = w_query.T
    any_spec = pl.BlockSpec(memory_space=pl.ANY)
    hbm_spec = pl.BlockSpec(memory_space=pltpu.HBM)
    vmem_spec = pl.BlockSpec(memory_space=pltpu.VMEM)
    token_spec = pl.BlockSpec((1, count, width), lambda b: (b, 0, 0))

    side = lax.axis_index("req") % 2
    tp_place = lax.axis_index("tp")

    def part(which):
        start = (which * tp_count + tp_place) * segment
        return lax.dynamic_slice_in_dim(stored[0], start, segment, 1)

    own_part, other_part = part(side), part(1 - side)
    partner_part = permuted(other_part, "req", 1)
    q = pl.pallas_call(
        functools.partial(query_kernel, req_dev, q_chunk),
        grid=(req_dev,),
        out_shape=jax.ShapeDtypeStruct((n_req, req_dev, q_chunk, LANES), BF16),
        in_specs=[
            SMEM,
            SMEM,
            token_spec,
            full((1, width)),
            full(w_query_rows.shape),
            full((1, head_dim)),
            table_spec,
        ],
        out_specs=pl.BlockSpec((n_req, 1, q_chunk, LANES), lambda b: (0, b, 0, 0)),
        compiler_params=params(60),
        cost_estimate=cost(2 * req_dev * count * width * 384, 6 << 20),
        name="query",
    )(continuing, cache_len, tokens, gain_row, w_query_rows, q_gain_row, table)
    q_mid = exchanged(q).reshape(requests, q_chunk, LANES)

    partner_part = lax.optimization_barrier((partner_part, q))[0]
    both = jnp.stack([own_part, partner_part])
    planes = n_req // 2
    hops = planes == 4

    def crossed(value, pairs):
        pairs = [(2 * a + parity, 2 * b + parity) for a, b in pairs for parity in range(2)]
        return lax.ppermute(value, "req", pairs)

    if hops:
        outer = [(z, z ^ 1) for z in range(planes)]
        beside = crossed(both, outer)
        middle = crossed(both, [(1, 2), (2, 1)])
    else:
        column = [list(range(parity, n_req, 2)) for parity in range(2)]
        blocks = [lax.all_gather(both, "req", axis_index_groups=column)]
        beside = middle = both

    w_x = permuted(w_out, "tp", tp_count // 2)
    w_c = permuted(w_out, "tp", 1)
    w_xc = permuted(w_x, "tp", 1)

    fresh = pl.pallas_call(
        functools.partial(fresh_kernel, req_dev),
        grid=(req_dev,),
        out_shape=jax.ShapeDtypeStruct((req_dev, kv_heads, count, LANES), BF16),
        in_specs=[
            SMEM,
            token_spec,
            full((1, width)),
            full(key_value_weight.shape),
            full((1, head_dim)),
            table_spec,
            any_spec,
        ],
        out_specs=pl.BlockSpec((1, kv_heads, count, LANES), lambda b: (b, 0, 0, 0)),
        compiler_params=params(),
        cost_estimate=HINT,
        name="fresh",
    )(meta, tokens, gain_row, key_value_weight, k_gain_row, table, q)

    q_out = pl.pallas_call(
        functools.partial(route_query_kernel, requests),
        out_shape=jax.ShapeDtypeStruct((n_req, q_chunk, LANES), BF16),
        in_specs=[SMEM, vmem_spec],
        out_specs=vmem_spec,
        compiler_params=params(),
        cost_estimate=cost(0, 1 << 20),
        name="route_query",
    )(meta, q_mid)
    q_row, beside, middle, _ = lax.optimization_barrier((exchanged(q_out), beside, middle, fresh))
    if hops:
        far_middle = crossed(beside, [(1, 2), (2, 1)])
        outward = crossed(middle, [(1, 0), (2, 3)])
    fresh_partner = permuted(fresh, "req", 1)

    near = pl.pallas_call(
        functools.partial(local_kernel, groups),
        grid=(req_dev,),
        out_shape=jax.ShapeDtypeStruct((req_dev, 3, count, LANES), F32),
        in_specs=[
            pl.BlockSpec((n_req, 1, q_chunk, LANES), lambda b: (0, b, 0, 0)),
            pl.BlockSpec((1, kv_heads, count, LANES), lambda b: (b, 0, 0, 0)),
        ],
        out_specs=pl.BlockSpec((1, 3, count, LANES), lambda b: (b, 0, 0, 0)),
        compiler_params=params(),
        cost_estimate=HINT,
        name="attend_new",
    )(q, fresh)

    far = pl.pallas_call(
        functools.partial(row_kernel, requests, count, heads, groups, o_chunk),
        out_shape=jax.ShapeDtypeStruct((n_req, o_chunk, LANES), BF16),
        in_specs=[SMEM, vmem_spec, any_spec],
        out_specs=vmem_spec,
        scratch_shapes=[
            pltpu.VMEM((2, span, LANES), BF16),
            pltpu.SemaphoreType.DMA((2,)),
        ],
        compiler_params=params(60),
        cost_estimate=cost(4 * heads * count * span * 256, 32 << 20),
        name="attend_row",
    )(meta, q_row, stored)

    far_mid = exchanged(far)
    if hops:
        far_mid = lax.optimization_barrier((far_mid, far_middle, outward, fresh_partner, near))[0]
        far_outward = crossed(far_middle, [(1, 0), (2, 3)])
        blocks = [both, beside, middle, far_middle, outward, far_outward]
    far_out = pl.pallas_call(
        functools.partial(route_result_kernel, requests),
        out_shape=jax.ShapeDtypeStruct((requests, o_chunk, LANES), BF16),
        in_specs=[SMEM, vmem_spec],
        out_specs=vmem_spec,
        compiler_params=params(),
        cost_estimate=cost(0, 1 << 20),
        name="route_result",
    )(meta, far_mid)
    far_home = exchanged(far_out.reshape(n_req, req_dev, o_chunk, LANES))

    mixed = pl.pallas_call(
        functools.partial(merge_kernel, req_dev),
        grid=(req_dev,),
        out_shape=jax.ShapeDtypeStruct((req_dev, q_rows, LANES), BF16),
        in_specs=[
            SMEM,
            pl.BlockSpec((n_req, 1, o_chunk, LANES), lambda b: (0, b, 0, 0)),
            pl.BlockSpec((1, 3, count, LANES), lambda b: (b, 0, 0, 0)),
        ],
        out_specs=pl.BlockSpec((1, q_rows, LANES), lambda b: (b, 0, 0)),
        compiler_params=params(),
        cost_estimate=HINT,
        name="merge",
    )(meta, far_home, near)

    m_x = permuted(mixed, "tp", tp_count // 2)
    m_c = permuted(mixed, "tp", 1)

    def project(m_a, m_b, w_a, w_b, base, dtype, name):
        m_spec = pl.BlockSpec((1, q_rows, LANES), lambda b: (b, 0, 0))
        return pl.pallas_call(
            functools.partial(project_kernel, 512),
            grid=(req_dev,),
            out_shape=jax.ShapeDtypeStruct(tokens.shape, dtype),
            in_specs=[m_spec] * 2 + [full(w_out.shape)] * 2 + [token_spec],
            out_specs=token_spec,
            scratch_shapes=[pltpu.VMEM((count, 640), BF16)],
            compiler_params=params(),
            cost_estimate=HINT,
            name=name,
        )(m_a, m_b, w_a, w_b, base)

    partial = project(mixed, m_c, w_out, w_c, tokens, F32, "project_chip")
    m_x = lax.optimization_barrier((m_x, partial))[0]
    m_xc = permuted(m_x, "tp", 1)
    layer = project(m_x, m_xc, w_x, w_xc, partial, BF16, "project_rest")

    cache = pl.pallas_call(
        functools.partial(cache_kernel, req_dev, span),
        in_specs=[SMEM] + [any_spec] * len(blocks) + [vmem_spec, vmem_spec, any_spec],
        out_specs=any_spec,
        scratch_shapes=[
            pltpu.VMEM((2 * req_dev, kv_heads, 2 * segment, LANES), BF16),
            pltpu.VMEM((2 * req_dev, kv_heads, segment, LANES), BF16),
            pltpu.SemaphoreType.DMA((2 * req_dev,)),
            pltpu.SemaphoreType.DMA((2 * req_dev,)),
        ],
        out_shape=jax.ShapeDtypeStruct((2 * req_dev, kv_heads, segment, LANES), BF16),
        compiler_params=params(60),
        cost_estimate=HINT,
        name="cache",
    )(meta, *blocks, fresh, fresh_partner, layer)
    return (layer, cache)


def solution(mesh):
    return jax.shard_map(
        on_device,
        mesh=mesh,
        in_specs=(
            P("req", None, None),
            P(),
            P(None, "tp"),
            P(),
            P("tp", None),
            P(),
            P(),
            P("req", None, None, None),
            P(),
            P(),
            P(),
        ),
        out_specs=(P("req", None, None), P("req", None, "tp", None)),
        check_vma=False,
    )
```

```python
import functools
import math

import jax
import jax.numpy as jnp
import numpy as np
from jax import lax
from jax.experimental import pallas as pl
from jax.experimental.pallas import tpu as pltpu
from jax.sharding import PartitionSpec as P

BF16 = jnp.bfloat16
F32 = jnp.float32
LANES = 128
EPS = 1e-06
NEG = -1e30
SMEM = pl.BlockSpec(memory_space=pltpu.SMEM)


HINT = pl.CostEstimate(flops=0, bytes_accessed=1024, transcendentals=0)


def cost(flops, moved):
    return pl.CostEstimate(flops=int(flops), bytes_accessed=int(moved), transcendentals=0)


def params(mib=20):
    return pltpu.CompilerParams(vmem_limit_bytes=mib << 20)


def lane_iota(rows):
    return lax.broadcasted_iota(jnp.int32, (rows, LANES), 1)


def angle_tables(head_dim, new_count, cache_span):
    half = head_dim // 2
    freq = np.exp(-math.log(10000.0) * np.arange(half, dtype=np.float64) * 2.0 / head_dim)
    freq = np.tile(freq.astype(np.float32).astype(np.float64), LANES // half)

    def pair(positions):
        angle = positions[:, None].astype(np.float64) * freq[None, :]
        return np.cos(angle).astype(np.float32), np.sin(angle).astype(np.float32)

    fine = pair(np.arange(new_count))
    coarse = pair(np.arange(cache_span // 16 + 8) * 16)
    small = pair(np.arange(16))
    return np.stack([np.concatenate(part) for part in zip(fine, small, coarse)])


def rotation(length, count, table):
    high = length // 16
    low = length - high * 16
    row = lambda which, place: table[which, pl.ds(place, 1), :]
    ch, sh = row(0, count + 16 + high), row(1, count + 16 + high)
    cl, sl = row(0, count + low), row(1, count + low)
    cb, sb = ch * cl - sh * sl, sh * cl + ch * sl
    ci, si = table[0, :count], table[1, :count]
    cosine = ci * cb - si * sb
    sine = si * cb + ci * sb
    lanes = lane_iota(ci.shape[0])
    return cosine, jnp.where(lanes % 64 < 32, -sine, sine)


def norm_rope(tile, gain, cosine, sine, blocks):
    square = tile * tile
    high = square.astype(BF16)
    low = (square - high.astype(F32)).astype(BF16)
    mean = jnp.dot(high, blocks, preferred_element_type=F32) + jnp.dot(
        low, blocks, preferred_element_type=F32
    )
    unit = tile * lax.rsqrt(mean + EPS) * gain
    lanes = lane_iota(tile.shape[0])
    other = jnp.where(lanes % 64 < 32, pltpu.roll(unit, 96, 1), pltpu.roll(unit, 32, 1))
    return unit * cosine + other * sine


def half_blocks():
    rows = lax.broadcasted_iota(jnp.int32, (LANES, LANES), 0)
    cols = lax.broadcasted_iota(jnp.int32, (LANES, LANES), 1)
    return jnp.where(rows // 64 == cols // 64, 1.0 / 64.0, 0.0).astype(BF16)


def live(meta, request):
    return meta[0, request] == 1


def live_length(meta, request):
    return jnp.where(live(meta, request), meta[2, request], 0)


def to_chunks(ref, lead, value, chunk):
    rows = value.shape[0]
    for start in range(0, rows, chunk):
        size = min(chunk, rows - start)
        ref[(start // chunk,) + lead + (pl.ds(0, size),)] = value[start : start + size]


def normalized(tok, gain):
    x = tok[0].astype(F32)
    mean = jnp.mean(x * x, axis=-1, keepdims=True)
    return (x * lax.rsqrt(mean + EPS) * gain[...]).astype(BF16)


def query_kernel(req_dev, chunk, cont, clen, tok, gain, w, qg, table, q):
    b = pl.program_id(0)
    count = tok.shape[1]
    half = count // 2
    request = lax.axis_index("req") * req_dev + b
    length = jnp.where(cont[request] == 1, clen[request], 0)
    out = lax.dot_general(
        normalized(tok, gain), w[...], (((1,), (1,)), ((), ())), preferred_element_type=F32
    )
    cosine, sine = rotation(length, count, table)
    blocks = half_blocks()
    gains = jnp.concatenate([qg[...]] * 2, axis=1)
    pair01 = norm_rope(out[:, :128], gains, cosine, sine, blocks)
    pair23 = norm_rope(out[:, 128:256], gains, cosine, sine, blocks)
    last = out[:, 256:320]
    last = jnp.concatenate([last[:half], last[half:]], axis=1)
    lanes = lane_iota(half)
    pick = lambda v: jnp.where(lanes < 64, v[:half], v[half:])
    last = norm_rope(last, gains, pick(cosine), pick(sine), blocks)
    packed = (jnp.concatenate([pair01, pair23, last], axis=0) * 0.125).astype(BF16)
    to_chunks(q, (0,), packed, chunk)


def fresh_kernel(req_dev, meta, tok, gain, w, kg, table, after, fresh):
    del after
    b = pl.program_id(0)
    count = tok.shape[1]
    length = live_length(meta, lax.axis_index("req") * req_dev + b)
    out = jnp.dot(normalized(tok, gain), w[...], preferred_element_type=F32)
    cosine, sine = rotation(length, count, table)
    blocks = half_blocks()
    lanes = lane_iota(count)
    gains = jnp.concatenate([kg[...]] * 2, axis=1)
    for head in range(fresh.shape[1]):
        tile = out[:, head * 128 : head * 128 + 128]
        keys = norm_rope(tile, gains, cosine, sine, blocks)
        fresh[0, head] = jnp.where(lanes < 64, keys, tile).astype(BF16)


def split_heads(packed, count):
    half = count // 2
    wide = packed.astype(F32)
    lanes = lane_iota(count)
    tiles = [wide[:count], pltpu.roll(wide[:count], 64, 1)]
    tiles += [wide[count : 2 * count], pltpu.roll(wide[count : 2 * count], 64, 1)]
    last = wide[2 * count : 2 * count + half]
    tiles.append(jnp.concatenate([last, pltpu.roll(last, 64, 1)], axis=0))
    return [jnp.where(lanes < 64, tile, 0.0).astype(BF16) for tile in tiles]


def soft(scores, values):
    top = jnp.max(scores, axis=-1, keepdims=True)
    weights = jnp.exp(scores - top)
    total = jnp.sum(weights, axis=-1, keepdims=True)
    out = jnp.dot(weights.astype(BF16), values, preferred_element_type=F32)
    return out / total, top + jnp.log(total)


def local_kernel(groups, q, fresh, out):
    heads = 5
    count = fresh.shape[2]
    first = lax.axis_index("tp") * heads
    lanes = lane_iota(count)
    rows = lax.broadcasted_iota(jnp.int32, (count, count), 0)
    cols = lax.broadcasted_iota(jnp.int32, (count, count), 1)
    packed = q[...].reshape(-1, LANES)
    tiles = split_heads(packed, count)
    stats = jnp.zeros((count, LANES), F32)
    kept = []
    for head in range(heads):
        kv = fresh[0, (first + head) // groups]
        scores = lax.dot_general(
            tiles[head], kv, (((1,), (1,)), ((), ())), preferred_element_type=F32
        )
        scores = jnp.where(cols <= rows, scores, NEG)
        mixed, level = soft(scores, kv)
        stats = jnp.where(lanes == head, level, stats)
        kept.append(mixed)
    roll = lambda v: pltpu.roll(v, 64, 1)
    out[0, 0] = jnp.where(lanes < 64, roll(kept[0]), kept[1])
    out[0, 1] = jnp.where(lanes < 64, roll(kept[2]), kept[3])
    out[0, 2] = jnp.where(lanes < 64, roll(kept[4]), roll(stats))


def each(requests, step):
    if requests <= 32:
        for r in range(requests):
            step(r)
    else:
        pl.loop(0, requests)(step)


def route_query_kernel(requests, meta, src, dst):
    def step(r):
        @pl.when(live(meta, r))
        def _():
            dst[meta[1, r]] = src[r]

    each(requests, step)


def route_result_kernel(requests, meta, src, dst):
    def step(r):
        dst[r] = src[jnp.where(live(meta, r), meta[1, r], 0)]

    each(requests, step)


def row_kernel(requests, count, heads, groups, chunk, meta, q, pair, out):
    span = pair.shape[1]
    offset = lax.axis_index("tp") * heads
    first = offset // groups

    row = lax.axis_index("req")

    def find(r, length):
        mine = jnp.logical_and(live(meta, r), meta[1, r] == row)
        return jnp.where(mine, meta[2, r], length)

    length = lax.fori_loop(0, requests, find, 0)
    position = lax.broadcasted_iota(jnp.int32, (8, span), 1)
    bias = jnp.where(position < length, 0.0, NEG)[0:1]
    tiles = split_heads(q[...].reshape(-1, LANES), count)
    lanes = lane_iota(count)
    level = jnp.zeros((count, LANES), F32)
    kept = []
    for head in range(heads):
        kv = pair[(offset + head) // groups - first]
        scores = lax.dot_general(
            tiles[head], kv, (((1,), (1,)), ((), ())), preferred_element_type=F32
        )
        mixed, one = soft(scores + bias, kv)
        level = jnp.where(lanes == head, one, level)
        kept.append(mixed)
    roll = lambda v, n: pltpu.roll(v, n, 1)
    high = level.astype(BF16).astype(F32)
    mid = (level - high).astype(BF16).astype(F32)
    low = (level - high - mid).astype(BF16).astype(F32)
    stats = roll(high, 64) + roll(mid, 64 + heads) + roll(low, 64 + 2 * heads)
    tiles = [
        jnp.where(lanes < 64, roll(kept[0], 64), kept[1]),
        jnp.where(lanes < 64, roll(kept[2], 64), kept[3]),
        jnp.where(lanes < 64, roll(kept[4], 64), stats),
    ]
    to_chunks(out, (), jnp.concatenate(tiles, axis=0).astype(BF16), chunk)


def merge_kernel(req_dev, meta, far, near, mixed):
    heads = 5
    count = near.shape[2]
    b = pl.program_id(0)
    request = lax.axis_index("req") * req_dev + b
    lanes = lane_iota(count)
    roll = lambda v, n: pltpu.roll(v, n, 1)
    packed = far[...].reshape(-1, LANES)
    tiles = [packed[p * count : (p + 1) * count].astype(F32) for p in range(3)]
    stats = roll(tiles[2], 64) + roll(tiles[2], 64 - heads) + roll(tiles[2], 64 - 2 * heads)
    far_level = jnp.where(jnp.logical_and(live(meta, request), lanes < heads), stats, NEG)
    near_level = jnp.where(lanes < heads, roll(near[0, 2], 64), 0.0)
    top = jnp.maximum(far_level, near_level)
    far_part = jnp.exp(far_level - top)
    near_part = jnp.exp(near_level - top)
    share = far_part / (far_part + near_part)
    done = []
    for p in range(3):
        left = share[:, 2 * p : 2 * p + 1]
        right = share[:, 2 * p + 1 : 2 * p + 2] if 2 * p + 1 < heads else left
        weight = jnp.where(lanes < 64, left, right)
        done.append(weight * tiles[p] + (1.0 - weight) * near[0, p])
    half = count // 2
    last = jnp.where(lane_iota(half) < 64, done[2][:half], roll(done[2][half:], 64))
    mixed[0] = jnp.concatenate([done[0], done[1], last], axis=0).astype(BF16)


def project_kernel(block, m_a, m_b, w_a, w_b, base, out, lhs):
    count, width = out.shape[1:]
    half = count // 2
    lanes = lane_iota(half)
    for number, m in enumerate((m_a, m_b)):
        for p in range(2):
            col = number * 256 + p * 128
            lhs[:, col : col + 128] = m[0, p * count : (p + 1) * count]
    left = m_a[0, 2 * count :].astype(F32)
    right = m_b[0, 2 * count :].astype(F32)
    lhs[:half, 512:] = jnp.where(lanes < 64, left, pltpu.roll(right, 64, 1)).astype(BF16)
    lhs[half:, 512:] = jnp.where(lanes < 64, pltpu.roll(left, 64, 1), right).astype(BF16)
    for start in range(0, width, block):
        part = pl.ds(start, block)
        weights = jnp.concatenate(
            [w_a[:256, part], w_b[:256, part], w_a[256:, part], w_b[256:, part]], axis=0
        )
        total = base[0, :, part].astype(F32)
        total += jnp.dot(lhs[...], weights, preferred_element_type=F32)
        out[0, :, part] = total.astype(out.dtype)


def held(plane, here):
    apart = plane ^ here
    mid = jnp.logical_or(here == 1, here == 2)
    return jnp.where(apart < 2, apart, jnp.where(mid, 5 - apart, 2 + apart))


def cache_kernel(req_dev, span, steps, meta, *refs):
    blocks, (mine, theirs, _, out, kept_sc, out_sc, sem, out_sem) = refs[:-8], refs[-8:]
    place, tp_place = lax.axis_index("req"), lax.axis_index("tp")
    side = place % 2
    kv_heads, segment = out.shape[1], out.shape[2]
    count = mine.shape[2]
    start = (side * lax.axis_size("tp") + tp_place) * segment
    skip = pl.multiple_of(start - jnp.minimum(start, span - segment), 16)
    first = (place // 2) * 2 * req_dev
    numbers = range(2 * req_dev)
    found = []
    for number in numbers:
        row = jnp.where(live(meta, first + number), meta[1, first + number], place)
        step = 0 if len(blocks[0].shape) == 5 else held(row // 2, place // 2)
        found.append((row // 2, (row % 2) ^ side, step))

    def here(number, action):
        wanted = functools.reduce(jnp.logical_or, [found[number][2] == step for step in steps])
        pl.when(wanted)(action)

    def fetch(number):
        plane, which, step = found[number]
        dst = kept_sc.at[number, :, pl.ds(0, segment), :]
        if len(blocks[0].shape) == 5:
            pltpu.make_async_copy(blocks[0].at[plane, which], dst, sem.at[number]).start()
            return
        for step_of, block in zip(steps, blocks):

            @pl.when(step == step_of)
            def _():
                pltpu.make_async_copy(block.at[which], dst, sem.at[number]).start()

    def write(number):
        return pltpu.make_async_copy(out_sc.at[number], out.at[number], out_sem.at[number])

    def fill(number):
        ahead = live_length(meta, first + number) - start
        rows = lax.broadcasted_iota(jnp.int32, (segment, count), 0)
        cols = lax.broadcasted_iota(jnp.int32, (segment, count), 1)
        shift = jnp.where(rows - cols == ahead, 1.0, 0.0).astype(BF16)
        local = number // req_dev == side
        place_of = number % req_dev
        new = jnp.concatenate(
            [jnp.where(local, mine[place_of, h], theirs[place_of, h]) for h in range(kv_heads)],
            axis=1,
        )
        moved = jnp.dot(shift, new, preferred_element_type=F32)
        old = lax.broadcasted_iota(jnp.int32, (segment, LANES), 0) < ahead
        dst = kept_sc.at[number, :, pl.ds(0, segment), :]
        pltpu.make_async_copy(dst, dst, sem.at[number]).wait()
        for head in range(kv_heads):
            kept = kept_sc[number, head, pl.ds(skip, segment), :].astype(F32)
            part = moved[:, head * LANES : head * LANES + LANES]
            out_sc[number, head] = jnp.where(old, kept, part).astype(BF16)
        write(number).start()

    for number in numbers:
        fetch(number)
    for number in numbers:
        here(number, functools.partial(fill, number))
    for number in numbers:
        here(number, lambda number=number: write(number).wait())


def permuted(value, axis, mask):
    pairs = [(source, source ^ mask) for source in range(lax.axis_size(axis))]
    return lax.ppermute(value, axis, pairs)


def exchanged(value):
    return lax.all_to_all(value, "req", split_axis=0, concat_axis=0, tiled=True)


def full(shape):
    return pl.BlockSpec(shape, lambda *_: (0,) * len(shape))


def on_device(
    tokens,
    attn_gain,
    w_query,
    key_value_weight,
    w_out,
    q_gain,
    k_gain,
    stored,
    continuing,
    cache_row,
    cache_len,
):
    n_req = lax.axis_size("req")
    tp_count = lax.axis_size("tp")
    req_dev, count, width = tokens.shape
    head_dim = q_gain.shape[0]
    kv_heads = key_value_weight.shape[1] // (2 * head_dim)
    heads = w_query.shape[1] // head_dim
    groups = heads * tp_count // kv_heads
    span = stored.shape[2]
    requests = continuing.shape[0]
    segments = 2 * tp_count
    segment = (span + count) // segments
    q_rows = heads * head_dim * count // LANES
    o_rows = -(-heads * head_dim // LANES) * count
    q_chunk = -(-q_rows // (16 * n_req)) * 16
    o_chunk = -(-o_rows // (16 * n_req)) * 16

    table = jnp.asarray(angle_tables(head_dim, count, span))
    table_spec = full(table.shape)
    meta = jnp.stack([continuing, cache_row, cache_len])
    gain_row = attn_gain.reshape(1, width)
    q_gain_row = q_gain.reshape(1, head_dim)
    k_gain_row = k_gain.reshape(1, head_dim)
    w_query_rows = w_query.T
    any_spec = pl.BlockSpec(memory_space=pl.ANY)
    hbm_spec = pl.BlockSpec(memory_space=pltpu.HBM)
    vmem_spec = pl.BlockSpec(memory_space=pltpu.VMEM)
    token_spec = pl.BlockSpec((1, count, width), lambda b: (b, 0, 0))

    side = lax.axis_index("req") % 2
    tp_place = lax.axis_index("tp")

    def part(source, which):
        start = (which * tp_count + tp_place) * segment
        return lax.dynamic_slice_in_dim(source[0], start, segment, 1)

    partner_part = permuted(part(stored, 1 - side), "req", 1)
    q = pl.pallas_call(
        functools.partial(query_kernel, req_dev, q_chunk),
        grid=(req_dev,),
        out_shape=jax.ShapeDtypeStruct((n_req, req_dev, q_chunk, LANES), BF16),
        in_specs=[
            SMEM,
            SMEM,
            token_spec,
            full((1, width)),
            full(w_query_rows.shape),
            full((1, head_dim)),
            table_spec,
        ],
        out_specs=pl.BlockSpec((n_req, 1, q_chunk, LANES), lambda b: (0, b, 0, 0)),
        compiler_params=params(60),
        cost_estimate=cost(2 * req_dev * count * width * 384, 6 << 20),
        name="query",
    )(continuing, cache_len, tokens, gain_row, w_query_rows, q_gain_row, table)
    q_mid = exchanged(q).reshape(requests, q_chunk, LANES)

    partner_part, later = lax.optimization_barrier((partner_part, stored, q))[:2]
    both = jnp.stack([part(later, side), partner_part])
    planes = n_req // 2
    hops = planes == 4

    def crossed(value, pairs):
        pairs = [(2 * a + parity, 2 * b + parity) for a, b in pairs for parity in range(2)]
        return lax.ppermute(value, "req", pairs)

    if hops:
        outer = [(z, z ^ 1) for z in range(planes)]
        beside = crossed(both, outer)
        middle = crossed(both, [(1, 2), (2, 1)])
    else:
        column = [list(range(parity, n_req, 2)) for parity in range(2)]
        blocks = [lax.all_gather(both, "req", axis_index_groups=column)]
        beside = middle = both

    w_x = permuted(w_out, "tp", tp_count // 2)
    w_c = permuted(w_out, "tp", 1)
    w_xc = permuted(w_x, "tp", 1)

    later = lax.optimization_barrier((stored, q_mid))[0]
    pair = lax.dynamic_slice_in_dim(later[0], tp_place * heads // groups, 2, 0)
    fresh = pl.pallas_call(
        functools.partial(fresh_kernel, req_dev),
        grid=(req_dev,),
        out_shape=jax.ShapeDtypeStruct((req_dev, kv_heads, count, LANES), BF16),
        in_specs=[
            SMEM,
            token_spec,
            full((1, width)),
            full(key_value_weight.shape),
            full((1, head_dim)),
            table_spec,
            any_spec,
        ],
        out_specs=pl.BlockSpec((1, kv_heads, count, LANES), lambda b: (b, 0, 0, 0)),
        compiler_params=params(),
        cost_estimate=HINT,
        name="fresh",
    )(meta, tokens, gain_row, key_value_weight, k_gain_row, table, pair)

    q_out = pl.pallas_call(
        functools.partial(route_query_kernel, requests),
        out_shape=jax.ShapeDtypeStruct((n_req, q_chunk, LANES), BF16),
        in_specs=[SMEM, vmem_spec],
        out_specs=vmem_spec,
        compiler_params=params(),
        cost_estimate=cost(0, 1 << 20),
        name="route_query",
    )(meta, q_mid)
    q_row, beside, middle, _ = lax.optimization_barrier((exchanged(q_out), beside, middle, fresh))
    if hops:
        far_middle = crossed(beside, [(1, 2), (2, 1)])
        outward = crossed(middle, [(1, 0), (2, 3)])
    fresh_partner = permuted(fresh, "req", 1)

    near = pl.pallas_call(
        functools.partial(local_kernel, groups),
        grid=(req_dev,),
        out_shape=jax.ShapeDtypeStruct((req_dev, 3, count, LANES), F32),
        in_specs=[
            pl.BlockSpec((n_req, 1, q_chunk, LANES), lambda b: (0, b, 0, 0)),
            pl.BlockSpec((1, kv_heads, count, LANES), lambda b: (b, 0, 0, 0)),
        ],
        out_specs=pl.BlockSpec((1, 3, count, LANES), lambda b: (b, 0, 0, 0)),
        compiler_params=params(),
        cost_estimate=HINT,
        name="attend_new",
    )(q, fresh)

    far = pl.pallas_call(
        functools.partial(row_kernel, requests, count, heads, groups, o_chunk),
        out_shape=jax.ShapeDtypeStruct((n_req, o_chunk, LANES), BF16),
        in_specs=[SMEM, vmem_spec, vmem_spec],
        out_specs=vmem_spec,
        compiler_params=params(40),
        cost_estimate=cost(4 * heads * count * span * 256, 32 << 20),
        name="attend_row",
    )(meta, q_row, pair)

    far_mid = exchanged(far)
    if hops:
        far_mid = lax.optimization_barrier((far_mid, far_middle, outward, fresh_partner, near))[0]
        far_outward = crossed(far_middle, [(1, 0), (2, 3)])
        blocks = [both, beside, middle, far_middle, outward, far_outward]
    def fill_cache(steps, blocks, after, aliases):
        return pl.pallas_call(
            functools.partial(cache_kernel, req_dev, span, steps),
            in_specs=[SMEM] + [any_spec] * len(blocks) + [vmem_spec, vmem_spec, any_spec],
            out_specs=any_spec,
            scratch_shapes=[
                pltpu.VMEM((2 * req_dev, kv_heads, 2 * segment, LANES), BF16),
                pltpu.VMEM((2 * req_dev, kv_heads, segment, LANES), BF16),
                pltpu.SemaphoreType.DMA((2 * req_dev,)),
                pltpu.SemaphoreType.DMA((2 * req_dev,)),
            ],
            out_shape=jax.ShapeDtypeStruct((2 * req_dev, kv_heads, segment, LANES), BF16),
            input_output_aliases=aliases,
            compiler_params=params(),
            cost_estimate=HINT,
            name="cache",
        )(meta, *blocks, fresh, fresh_partner, after)

    if hops:
        cache = fill_cache(tuple(range(5)), blocks[:5], far_mid, {})

    far_out = pl.pallas_call(
        functools.partial(route_result_kernel, requests),
        out_shape=jax.ShapeDtypeStruct((requests, o_chunk, LANES), BF16),
        in_specs=[SMEM, vmem_spec],
        out_specs=vmem_spec,
        compiler_params=params(),
        cost_estimate=cost(0, 1 << 20),
        name="route_result",
    )(meta, far_mid)
    far_home = exchanged(far_out.reshape(n_req, req_dev, o_chunk, LANES))
    if hops:
        far_home = lax.optimization_barrier((far_home, cache))[0]

    mixed = pl.pallas_call(
        functools.partial(merge_kernel, req_dev),
        grid=(req_dev,),
        out_shape=jax.ShapeDtypeStruct((req_dev, q_rows, LANES), BF16),
        in_specs=[
            SMEM,
            pl.BlockSpec((n_req, 1, o_chunk, LANES), lambda b: (0, b, 0, 0)),
            pl.BlockSpec((1, 3, count, LANES), lambda b: (b, 0, 0, 0)),
        ],
        out_specs=pl.BlockSpec((1, q_rows, LANES), lambda b: (b, 0, 0)),
        compiler_params=params(),
        cost_estimate=HINT,
        name="merge",
    )(meta, far_home, near)

    m_x = permuted(mixed, "tp", tp_count // 2)
    m_c = permuted(mixed, "tp", 1)

    def project(m_a, m_b, w_a, w_b, base, dtype, name):
        m_spec = pl.BlockSpec((1, q_rows, LANES), lambda b: (b, 0, 0))
        return pl.pallas_call(
            functools.partial(project_kernel, 512),
            grid=(req_dev,),
            out_shape=jax.ShapeDtypeStruct(tokens.shape, dtype),
            in_specs=[m_spec] * 2 + [full(w_out.shape)] * 2 + [token_spec],
            out_specs=token_spec,
            scratch_shapes=[pltpu.VMEM((count, 640), BF16)],
            compiler_params=params(),
            cost_estimate=HINT,
            name=name,
        )(m_a, m_b, w_a, w_b, base)

    partial = project(mixed, m_c, w_out, w_c, tokens, F32, "project_chip")
    m_x = lax.optimization_barrier((m_x, partial))[0]
    m_xc = permuted(m_x, "tp", 1)
    layer = project(m_x, m_xc, w_x, w_xc, partial, BF16, "project_rest")

    if hops:
        cache = fill_cache((5,), [far_outward], cache, {4: 0})
    else:
        cache = fill_cache((0,), blocks, layer, {})
    return (layer, cache)


def solution(mesh):
    return jax.shard_map(
        on_device,
        mesh=mesh,
        in_specs=(
            P("req", None, None),
            P(),
            P(None, "tp"),
            P(),
            P("tp", None),
            P(),
            P(),
            P("req", None, None, None),
            P(),
            P(),
            P(),
        ),
        out_specs=(P("req", None, None), P("req", None, "tp", None)),
        check_vma=False,
    )
```

```python
import functools
import math

import jax
import jax.numpy as jnp
import numpy as np
from jax import lax
from jax.experimental import pallas as pl
from jax.experimental.pallas import tpu as pltpu
from jax.sharding import PartitionSpec as P

BF16 = jnp.bfloat16
F32 = jnp.float32
LANES = 128
EPS = 1e-06
NEG = -1e30
SMEM = pl.BlockSpec(memory_space=pltpu.SMEM)


HINT = pl.CostEstimate(flops=0, bytes_accessed=1024, transcendentals=0)


def cost(flops, moved):
    return pl.CostEstimate(flops=int(flops), bytes_accessed=int(moved), transcendentals=0)


def params(mib=20):
    return pltpu.CompilerParams(vmem_limit_bytes=mib << 20)


def lane_iota(rows):
    return lax.broadcasted_iota(jnp.int32, (rows, LANES), 1)


def angle_tables(head_dim, new_count, cache_span):
    half = head_dim // 2
    freq = np.exp(-math.log(10000.0) * np.arange(half, dtype=np.float64) * 2.0 / head_dim)
    freq = np.tile(freq.astype(np.float32).astype(np.float64), LANES // half)

    def pair(positions):
        angle = positions[:, None].astype(np.float64) * freq[None, :]
        return np.cos(angle).astype(np.float32), np.sin(angle).astype(np.float32)

    fine = pair(np.arange(new_count))
    coarse = pair(np.arange(cache_span // 16 + 8) * 16)
    small = pair(np.arange(16))
    return np.stack([np.concatenate(part) for part in zip(fine, small, coarse)])


def rotation(length, count, table):
    high = length // 16
    low = length - high * 16
    row = lambda which, place: table[which, pl.ds(place, 1), :]
    ch, sh = row(0, count + 16 + high), row(1, count + 16 + high)
    cl, sl = row(0, count + low), row(1, count + low)
    cb, sb = ch * cl - sh * sl, sh * cl + ch * sl
    ci, si = table[0, :count], table[1, :count]
    cosine = ci * cb - si * sb
    sine = si * cb + ci * sb
    lanes = lane_iota(ci.shape[0])
    return cosine, jnp.where(lanes % 64 < 32, -sine, sine)


def norm_rope(tile, gain, cosine, sine, blocks):
    square = tile * tile
    high = square.astype(BF16)
    low = (square - high.astype(F32)).astype(BF16)
    mean = jnp.dot(high, blocks, preferred_element_type=F32) + jnp.dot(
        low, blocks, preferred_element_type=F32
    )
    unit = tile * lax.rsqrt(mean + EPS) * gain
    lanes = lane_iota(tile.shape[0])
    other = jnp.where(lanes % 64 < 32, pltpu.roll(unit, 96, 1), pltpu.roll(unit, 32, 1))
    return unit * cosine + other * sine


def half_blocks():
    rows = lax.broadcasted_iota(jnp.int32, (LANES, LANES), 0)
    cols = lax.broadcasted_iota(jnp.int32, (LANES, LANES), 1)
    return jnp.where(rows // 64 == cols // 64, 1.0 / 64.0, 0.0).astype(BF16)


def live(meta, request):
    return meta[0, request] == 1


def live_length(meta, request):
    return jnp.where(live(meta, request), meta[2, request], 0)


def to_chunks(ref, lead, value, chunk):
    rows = value.shape[0]
    for start in range(0, rows, chunk):
        size = min(chunk, rows - start)
        ref[(start // chunk,) + lead + (pl.ds(0, size),)] = value[start : start + size]


def normalized(tok, gain):
    x = tok[0].astype(F32)
    mean = jnp.mean(x * x, axis=-1, keepdims=True)
    return (x * lax.rsqrt(mean + EPS) * gain[...]).astype(BF16)


def query_kernel(req_dev, chunk, cont, clen, tok, gain, w, qg, table, q):
    b = pl.program_id(0)
    count = tok.shape[1]
    half = count // 2
    request = lax.axis_index("req") * req_dev + b
    length = jnp.where(cont[request] == 1, clen[request], 0)
    out = lax.dot_general(
        normalized(tok, gain), w[...], (((1,), (1,)), ((), ())), preferred_element_type=F32
    )
    cosine, sine = rotation(length, count, table)
    blocks = half_blocks()
    gains = jnp.concatenate([qg[...]] * 2, axis=1)
    pair01 = norm_rope(out[:, :128], gains, cosine, sine, blocks)
    pair23 = norm_rope(out[:, 128:256], gains, cosine, sine, blocks)
    last = out[:, 256:320]
    last = jnp.concatenate([last[:half], last[half:]], axis=1)
    lanes = lane_iota(half)
    pick = lambda v: jnp.where(lanes < 64, v[:half], v[half:])
    last = norm_rope(last, gains, pick(cosine), pick(sine), blocks)
    packed = (jnp.concatenate([pair01, pair23, last], axis=0) * 0.125).astype(BF16)
    to_chunks(q, (0,), packed, chunk)


def fresh_kernel(req_dev, meta, tok, gain, w, kg, table, after, fresh):
    del after
    b = pl.program_id(0)
    count = tok.shape[1]
    length = live_length(meta, lax.axis_index("req") * req_dev + b)
    out = jnp.dot(normalized(tok, gain), w[...], preferred_element_type=F32)
    cosine, sine = rotation(length, count, table)
    blocks = half_blocks()
    lanes = lane_iota(count)
    gains = jnp.concatenate([kg[...]] * 2, axis=1)
    for head in range(fresh.shape[1]):
        tile = out[:, head * 128 : head * 128 + 128]
        keys = norm_rope(tile, gains, cosine, sine, blocks)
        fresh[0, head] = jnp.where(lanes < 64, keys, tile).astype(BF16)


def split_heads(packed, count):
    half = count // 2
    wide = packed.astype(F32)
    lanes = lane_iota(count)
    tiles = [wide[:count], pltpu.roll(wide[:count], 64, 1)]
    tiles += [wide[count : 2 * count], pltpu.roll(wide[count : 2 * count], 64, 1)]
    last = wide[2 * count : 2 * count + half]
    tiles.append(jnp.concatenate([last, pltpu.roll(last, 64, 1)], axis=0))
    return [jnp.where(lanes < 64, tile, 0.0).astype(BF16) for tile in tiles]


def soft(scores, values):
    top = jnp.max(scores, axis=-1, keepdims=True)
    weights = jnp.exp(scores - top)
    total = jnp.sum(weights, axis=-1, keepdims=True)
    out = jnp.dot(weights.astype(BF16), values, preferred_element_type=F32)
    return out / total, top + jnp.log(total)


def local_kernel(groups, q, fresh, out):
    heads = 5
    count = fresh.shape[2]
    first = lax.axis_index("tp") * heads
    lanes = lane_iota(count)
    rows = lax.broadcasted_iota(jnp.int32, (count, count), 0)
    cols = lax.broadcasted_iota(jnp.int32, (count, count), 1)
    packed = q[...].reshape(-1, LANES)
    tiles = split_heads(packed, count)
    stats = jnp.zeros((count, LANES), F32)
    kept = []
    for head in range(heads):
        kv = fresh[0, (first + head) // groups]
        scores = lax.dot_general(
            tiles[head], kv, (((1,), (1,)), ((), ())), preferred_element_type=F32
        )
        scores = jnp.where(cols <= rows, scores, NEG)
        mixed, level = soft(scores, kv)
        stats = jnp.where(lanes == head, level, stats)
        kept.append(mixed)
    roll = lambda v: pltpu.roll(v, 64, 1)
    out[0, 0] = jnp.where(lanes < 64, roll(kept[0]), kept[1])
    out[0, 1] = jnp.where(lanes < 64, roll(kept[2]), kept[3])
    out[0, 2] = jnp.where(lanes < 64, roll(kept[4]), roll(stats))


def each(requests, step):
    if requests <= 32:
        for r in range(requests):
            step(r)
    else:
        pl.loop(0, requests)(step)


def route_query_kernel(requests, meta, src, dst):
    def step(r):
        @pl.when(live(meta, r))
        def _():
            dst[meta[1, r]] = src[r]

    each(requests, step)


def route_result_kernel(requests, meta, src, dst):
    def step(r):
        dst[r] = src[jnp.where(live(meta, r), meta[1, r], 0)]

    each(requests, step)


def row_kernel(requests, count, heads, groups, chunk, meta, q, pair, out):
    span = pair.shape[1]
    offset = lax.axis_index("tp") * heads
    first = offset // groups

    row = lax.axis_index("req")

    def find(r, length):
        mine = jnp.logical_and(live(meta, r), meta[1, r] == row)
        return jnp.where(mine, meta[2, r], length)

    length = lax.fori_loop(0, requests, find, 0)
    position = lax.broadcasted_iota(jnp.int32, (8, span), 1)
    bias = jnp.where(position < length, 0.0, NEG)[0:1]
    tiles = split_heads(q[...].reshape(-1, LANES), count)
    lanes = lane_iota(count)
    level = jnp.zeros((count, LANES), F32)
    kept = []
    for head in range(heads):
        kv = pair[(offset + head) // groups - first]
        scores = lax.dot_general(
            tiles[head], kv, (((1,), (1,)), ((), ())), preferred_element_type=F32
        )
        mixed, one = soft(scores + bias, kv)
        level = jnp.where(lanes == head, one, level)
        kept.append(mixed)
    roll = lambda v, n: pltpu.roll(v, n, 1)
    high = level.astype(BF16).astype(F32)
    mid = (level - high).astype(BF16).astype(F32)
    low = (level - high - mid).astype(BF16).astype(F32)
    stats = roll(high, 64) + roll(mid, 64 + heads) + roll(low, 64 + 2 * heads)
    tiles = [
        jnp.where(lanes < 64, roll(kept[0], 64), kept[1]),
        jnp.where(lanes < 64, roll(kept[2], 64), kept[3]),
        jnp.where(lanes < 64, roll(kept[4], 64), stats),
    ]
    to_chunks(out, (), jnp.concatenate(tiles, axis=0).astype(BF16), chunk)


def merge_kernel(req_dev, meta, far, near, mixed):
    heads = 5
    count = near.shape[2]
    b = pl.program_id(0)
    request = lax.axis_index("req") * req_dev + b
    lanes = lane_iota(count)
    roll = lambda v, n: pltpu.roll(v, n, 1)
    packed = far[...].reshape(-1, LANES)
    tiles = [packed[p * count : (p + 1) * count].astype(F32) for p in range(3)]
    stats = roll(tiles[2], 64) + roll(tiles[2], 64 - heads) + roll(tiles[2], 64 - 2 * heads)
    far_level = jnp.where(jnp.logical_and(live(meta, request), lanes < heads), stats, NEG)
    near_level = jnp.where(lanes < heads, roll(near[0, 2], 64), 0.0)
    top = jnp.maximum(far_level, near_level)
    far_part = jnp.exp(far_level - top)
    near_part = jnp.exp(near_level - top)
    share = far_part / (far_part + near_part)
    done = []
    for p in range(3):
        left = share[:, 2 * p : 2 * p + 1]
        right = share[:, 2 * p + 1 : 2 * p + 2] if 2 * p + 1 < heads else left
        weight = jnp.where(lanes < 64, left, right)
        done.append(weight * tiles[p] + (1.0 - weight) * near[0, p])
    half = count // 2
    last = jnp.where(lane_iota(half) < 64, done[2][:half], roll(done[2][half:], 64))
    mixed[0] = jnp.concatenate([done[0], done[1], last], axis=0).astype(BF16)


def project_kernel(block, m_a, m_b, w_a, w_b, base, out, lhs):
    count, width = out.shape[1:]
    half = count // 2
    lanes = lane_iota(half)
    for number, m in enumerate((m_a, m_b)):
        for p in range(2):
            col = number * 256 + p * 128
            lhs[:, col : col + 128] = m[0, p * count : (p + 1) * count]
    left = m_a[0, 2 * count :].astype(F32)
    right = m_b[0, 2 * count :].astype(F32)
    lhs[:half, 512:] = jnp.where(lanes < 64, left, pltpu.roll(right, 64, 1)).astype(BF16)
    lhs[half:, 512:] = jnp.where(lanes < 64, pltpu.roll(left, 64, 1), right).astype(BF16)
    for start in range(0, width, block):
        part = pl.ds(start, block)
        weights = jnp.concatenate(
            [w_a[:256, part], w_b[:256, part], w_a[256:, part], w_b[256:, part]], axis=0
        )
        total = base[0, :, part].astype(F32)
        total += jnp.dot(lhs[...], weights, preferred_element_type=F32)
        out[0, :, part] = total.astype(out.dtype)


def held(plane, here):
    apart = plane ^ here
    mid = jnp.logical_or(here == 1, here == 2)
    return jnp.where(apart < 2, apart, jnp.where(mid, 5 - apart, 2 + apart))


def cache_kernel(req_dev, span, steps, meta, *refs):
    blocks, (mine, theirs, _, out, kept_sc, out_sc, sem, out_sem) = refs[:-8], refs[-8:]
    place, tp_place = lax.axis_index("req"), lax.axis_index("tp")
    side = place % 2
    kv_heads, segment = out.shape[1], out.shape[2]
    count = mine.shape[2]
    start = (side * lax.axis_size("tp") + tp_place) * segment
    skip = pl.multiple_of(start - jnp.minimum(start, span - segment), 16)
    first = (place // 2) * 2 * req_dev
    numbers = range(2 * req_dev)
    found = []
    for number in numbers:
        row = jnp.where(live(meta, first + number), meta[1, first + number], place)
        step = 0 if len(blocks[0].shape) == 5 else held(row // 2, place // 2)
        found.append((row // 2, (row % 2) ^ side, step))

    def here(number, action):
        wanted = functools.reduce(jnp.logical_or, [found[number][2] == step for step in steps])
        pl.when(wanted)(action)

    def fetch(number):
        plane, which, step = found[number]
        dst = kept_sc.at[number, :, pl.ds(0, segment), :]
        if len(blocks[0].shape) == 5:
            pltpu.make_async_copy(blocks[0].at[plane, which], dst, sem.at[number]).start()
            return
        for step_of, block in zip(steps, blocks):

            @pl.when(step == step_of)
            def _():
                pltpu.make_async_copy(block.at[which], dst, sem.at[number]).start()

    def write(number):
        return pltpu.make_async_copy(out_sc.at[number], out.at[number], out_sem.at[number])

    def fill(number):
        ahead = live_length(meta, first + number) - start
        rows = lax.broadcasted_iota(jnp.int32, (segment, count), 0)
        cols = lax.broadcasted_iota(jnp.int32, (segment, count), 1)
        shift = jnp.where(rows - cols == ahead, 1.0, 0.0).astype(BF16)
        local = number // req_dev == side
        place_of = number % req_dev
        new = jnp.concatenate(
            [jnp.where(local, mine[place_of, h], theirs[place_of, h]) for h in range(kv_heads)],
            axis=1,
        )
        moved = jnp.dot(shift, new, preferred_element_type=F32)
        old = lax.broadcasted_iota(jnp.int32, (segment, LANES), 0) < ahead
        dst = kept_sc.at[number, :, pl.ds(0, segment), :]
        pltpu.make_async_copy(dst, dst, sem.at[number]).wait()
        for head in range(kv_heads):
            kept = kept_sc[number, head, pl.ds(skip, segment), :].astype(F32)
            part = moved[:, head * LANES : head * LANES + LANES]
            out_sc[number, head] = jnp.where(old, kept, part).astype(BF16)
        write(number).start()

    for number in numbers:
        fetch(number)
    for number in numbers:
        here(number, functools.partial(fill, number))
    for number in numbers:
        here(number, lambda number=number: write(number).wait())


def permuted(value, axis, mask):
    pairs = [(source, source ^ mask) for source in range(lax.axis_size(axis))]
    return lax.ppermute(value, axis, pairs)


def exchanged(value):
    return lax.all_to_all(value, "req", split_axis=0, concat_axis=0, tiled=True)


def full(shape):
    return pl.BlockSpec(shape, lambda *_: (0,) * len(shape))


def on_device(
    tokens,
    attn_gain,
    w_query,
    key_value_weight,
    w_out,
    q_gain,
    k_gain,
    stored,
    continuing,
    cache_row,
    cache_len,
):
    n_req = lax.axis_size("req")
    tp_count = lax.axis_size("tp")
    req_dev, count, width = tokens.shape
    head_dim = q_gain.shape[0]
    kv_heads = key_value_weight.shape[1] // (2 * head_dim)
    heads = w_query.shape[1] // head_dim
    groups = heads * tp_count // kv_heads
    span = stored.shape[2]
    requests = continuing.shape[0]
    segments = 2 * tp_count
    segment = (span + count) // segments
    q_rows = heads * head_dim * count // LANES
    o_rows = -(-heads * head_dim // LANES) * count
    q_chunk = -(-q_rows // (16 * n_req)) * 16
    o_chunk = -(-o_rows // (16 * n_req)) * 16

    table = jnp.asarray(angle_tables(head_dim, count, span))
    table_spec = full(table.shape)
    meta = jnp.stack([continuing, cache_row, cache_len])
    gain_row = attn_gain.reshape(1, width)
    q_gain_row = q_gain.reshape(1, head_dim)
    k_gain_row = k_gain.reshape(1, head_dim)
    w_query_rows = w_query.T
    any_spec = pl.BlockSpec(memory_space=pl.ANY)
    hbm_spec = pl.BlockSpec(memory_space=pltpu.HBM)
    vmem_spec = pl.BlockSpec(memory_space=pltpu.VMEM)
    token_spec = pl.BlockSpec((1, count, width), lambda b: (b, 0, 0))

    side = lax.axis_index("req") % 2
    tp_place = lax.axis_index("tp")

    def part(source, which):
        start = (which * tp_count + tp_place) * segment
        return lax.dynamic_slice_in_dim(source[0], start, segment, 1)

    partner_part = permuted(part(stored, 1 - side), "req", 1)
    q = pl.pallas_call(
        functools.partial(query_kernel, req_dev, q_chunk),
        grid=(req_dev,),
        out_shape=jax.ShapeDtypeStruct((n_req, req_dev, q_chunk, LANES), BF16),
        in_specs=[
            SMEM,
            SMEM,
            token_spec,
            full((1, width)),
            full(w_query_rows.shape),
            full((1, head_dim)),
            table_spec,
        ],
        out_specs=pl.BlockSpec((n_req, 1, q_chunk, LANES), lambda b: (0, b, 0, 0)),
        compiler_params=params(60),
        cost_estimate=cost(2 * req_dev * count * width * 384, 6 << 20),
        name="query",
    )(continuing, cache_len, tokens, gain_row, w_query_rows, q_gain_row, table)
    q_mid = exchanged(q).reshape(requests, q_chunk, LANES)

    partner_part, later = lax.optimization_barrier((partner_part, stored, q))[:2]
    both = jnp.stack([part(later, side), partner_part])
    planes = n_req // 2
    hops = planes == 4

    def crossed(value, pairs):
        pairs = [(2 * a + parity, 2 * b + parity) for a, b in pairs for parity in range(2)]
        return lax.ppermute(value, "req", pairs)

    if hops:
        outer = [(z, z ^ 1) for z in range(planes)]
        beside = crossed(both, outer)
        middle = crossed(both, [(1, 2), (2, 1)])
    else:
        column = [list(range(parity, n_req, 2)) for parity in range(2)]
        blocks = [lax.all_gather(both, "req", axis_index_groups=column)]
        beside = middle = both

    w_x = permuted(w_out, "tp", tp_count // 2)
    w_c = permuted(w_out, "tp", 1)
    w_xc = permuted(w_x, "tp", 1)

    later = lax.optimization_barrier((stored, q_mid))[0]
    pair = lax.dynamic_slice_in_dim(later[0], tp_place * heads // groups, 2, 0)
    fresh = pl.pallas_call(
        functools.partial(fresh_kernel, req_dev),
        grid=(req_dev,),
        out_shape=jax.ShapeDtypeStruct((req_dev, kv_heads, count, LANES), BF16),
        in_specs=[
            SMEM,
            token_spec,
            full((1, width)),
            full(key_value_weight.shape),
            full((1, head_dim)),
            table_spec,
            any_spec,
        ],
        out_specs=pl.BlockSpec((1, kv_heads, count, LANES), lambda b: (b, 0, 0, 0)),
        compiler_params=params(),
        cost_estimate=HINT,
        name="fresh",
    )(meta, tokens, gain_row, key_value_weight, k_gain_row, table, pair)

    q_out = pl.pallas_call(
        functools.partial(route_query_kernel, requests),
        out_shape=jax.ShapeDtypeStruct((n_req, q_chunk, LANES), BF16),
        in_specs=[SMEM, vmem_spec],
        out_specs=vmem_spec,
        compiler_params=params(),
        cost_estimate=cost(0, 1 << 20),
        name="route_query",
    )(meta, q_mid)
    q_row, beside, middle, _ = lax.optimization_barrier((exchanged(q_out), beside, middle, fresh))
    if hops:
        far_middle = crossed(beside, [(1, 2), (2, 1)])
        outward = crossed(middle, outer)
    fresh_partner = permuted(fresh, "req", 1)

    near = pl.pallas_call(
        functools.partial(local_kernel, groups),
        grid=(req_dev,),
        out_shape=jax.ShapeDtypeStruct((req_dev, 3, count, LANES), F32),
        in_specs=[
            pl.BlockSpec((n_req, 1, q_chunk, LANES), lambda b: (0, b, 0, 0)),
            pl.BlockSpec((1, kv_heads, count, LANES), lambda b: (b, 0, 0, 0)),
        ],
        out_specs=pl.BlockSpec((1, 3, count, LANES), lambda b: (b, 0, 0, 0)),
        compiler_params=params(),
        cost_estimate=HINT,
        name="attend_new",
    )(q, fresh)

    far = pl.pallas_call(
        functools.partial(row_kernel, requests, count, heads, groups, o_chunk),
        out_shape=jax.ShapeDtypeStruct((n_req, o_chunk, LANES), BF16),
        in_specs=[SMEM, vmem_spec, vmem_spec],
        out_specs=vmem_spec,
        compiler_params=params(40),
        cost_estimate=cost(4 * heads * count * span * 256, 32 << 20),
        name="attend_row",
    )(meta, q_row, pair)

    far_mid = exchanged(far)
    if hops:
        far_mid = lax.optimization_barrier((far_mid, far_middle, outward, fresh_partner, near))[0]
        far_outward = crossed(far_middle, outer)
        blocks = [both, beside, middle, far_middle, outward, far_outward]
    def fill_cache(steps, blocks, after, aliases):
        return pl.pallas_call(
            functools.partial(cache_kernel, req_dev, span, steps),
            in_specs=[SMEM] + [any_spec] * len(blocks) + [vmem_spec, vmem_spec, any_spec],
            out_specs=any_spec,
            scratch_shapes=[
                pltpu.VMEM((2 * req_dev, kv_heads, 2 * segment, LANES), BF16),
                pltpu.VMEM((2 * req_dev, kv_heads, segment, LANES), BF16),
                pltpu.SemaphoreType.DMA((2 * req_dev,)),
                pltpu.SemaphoreType.DMA((2 * req_dev,)),
            ],
            out_shape=jax.ShapeDtypeStruct((2 * req_dev, kv_heads, segment, LANES), BF16),
            input_output_aliases=aliases,
            compiler_params=params(),
            cost_estimate=HINT,
            name="cache",
        )(meta, *blocks, fresh, fresh_partner, after)

    if hops:
        cache = fill_cache(tuple(range(5)), blocks[:5], far_mid, {})

    far_out = pl.pallas_call(
        functools.partial(route_result_kernel, requests),
        out_shape=jax.ShapeDtypeStruct((requests, o_chunk, LANES), BF16),
        in_specs=[SMEM, vmem_spec],
        out_specs=vmem_spec,
        compiler_params=params(),
        cost_estimate=cost(0, 1 << 20),
        name="route_result",
    )(meta, far_mid)
    far_home = exchanged(far_out.reshape(n_req, req_dev, o_chunk, LANES))
    if hops:
        far_home = lax.optimization_barrier((far_home, cache))[0]

    mixed = pl.pallas_call(
        functools.partial(merge_kernel, req_dev),
        grid=(req_dev,),
        out_shape=jax.ShapeDtypeStruct((req_dev, q_rows, LANES), BF16),
        in_specs=[
            SMEM,
            pl.BlockSpec((n_req, 1, o_chunk, LANES), lambda b: (0, b, 0, 0)),
            pl.BlockSpec((1, 3, count, LANES), lambda b: (b, 0, 0, 0)),
        ],
        out_specs=pl.BlockSpec((1, q_rows, LANES), lambda b: (b, 0, 0)),
        compiler_params=params(),
        cost_estimate=HINT,
        name="merge",
    )(meta, far_home, near)

    m_x = permuted(mixed, "tp", tp_count // 2)
    m_c = permuted(mixed, "tp", 1)

    def project(m_a, m_b, w_a, w_b, base, dtype, name):
        m_spec = pl.BlockSpec((1, q_rows, LANES), lambda b: (b, 0, 0))
        return pl.pallas_call(
            functools.partial(project_kernel, 512),
            grid=(req_dev,),
            out_shape=jax.ShapeDtypeStruct(tokens.shape, dtype),
            in_specs=[m_spec] * 2 + [full(w_out.shape)] * 2 + [token_spec],
            out_specs=token_spec,
            scratch_shapes=[pltpu.VMEM((count, 640), BF16)],
            compiler_params=params(),
            cost_estimate=HINT,
            name=name,
        )(m_a, m_b, w_a, w_b, base)

    partial = project(mixed, m_c, w_out, w_c, tokens, F32, "project_chip")
    m_x = lax.optimization_barrier((m_x, partial))[0]
    m_xc = permuted(m_x, "tp", 1)
    layer = project(m_x, m_xc, w_x, w_xc, partial, BF16, "project_rest")

    if hops:
        cache = fill_cache((5,), [far_outward], cache, {4: 0})
    else:
        cache = fill_cache((0,), blocks, layer, {})
    return (layer, cache)


def solution(mesh):
    return jax.shard_map(
        on_device,
        mesh=mesh,
        in_specs=(
            P("req", None, None),
            P(),
            P(None, "tp"),
            P(),
            P("tp", None),
            P(),
            P(),
            P("req", None, None, None),
            P(),
            P(),
            P(),
        ),
        out_specs=(P("req", None, None), P("req", None, "tp", None)),
        check_vma=False,
    )
```

```python
import functools
import math

import jax
import jax.numpy as jnp
import numpy as np
from jax import lax
from jax.experimental import pallas as pl
from jax.experimental.pallas import tpu as pltpu
from jax.sharding import PartitionSpec as P

BF16 = jnp.bfloat16
F32 = jnp.float32
LANES = 128
EPS = 1e-06
NEG = -1e30
SMEM = pl.BlockSpec(memory_space=pltpu.SMEM)


HINT = pl.CostEstimate(flops=0, bytes_accessed=1024, transcendentals=0)


def cost(flops, moved):
    return pl.CostEstimate(flops=int(flops), bytes_accessed=int(moved), transcendentals=0)


def params(mib=20):
    return pltpu.CompilerParams(vmem_limit_bytes=mib << 20)


def lane_iota(rows):
    return lax.broadcasted_iota(jnp.int32, (rows, LANES), 1)


def angle_tables(head_dim, new_count, cache_span):
    half = head_dim // 2
    freq = np.exp(-math.log(10000.0) * np.arange(half, dtype=np.float64) * 2.0 / head_dim)
    freq = np.tile(freq.astype(np.float32).astype(np.float64), LANES // half)

    def pair(positions):
        angle = positions[:, None].astype(np.float64) * freq[None, :]
        return np.cos(angle).astype(np.float32), np.sin(angle).astype(np.float32)

    fine = pair(np.arange(new_count))
    coarse = pair(np.arange(cache_span // 16 + 8) * 16)
    small = pair(np.arange(16))
    return np.stack([np.concatenate(part) for part in zip(fine, small, coarse)])


def rotation(length, count, table):
    high = length // 16
    low = length - high * 16
    row = lambda which, place: table[which, pl.ds(place, 1), :]
    ch, sh = row(0, count + 16 + high), row(1, count + 16 + high)
    cl, sl = row(0, count + low), row(1, count + low)
    cb, sb = ch * cl - sh * sl, sh * cl + ch * sl
    ci, si = table[0, :count], table[1, :count]
    cosine = ci * cb - si * sb
    sine = si * cb + ci * sb
    lanes = lane_iota(ci.shape[0])
    return cosine, jnp.where(lanes % 64 < 32, -sine, sine)


def norm_rope(tile, gain, cosine, sine, blocks):
    square = tile * tile
    high = square.astype(BF16)
    low = (square - high.astype(F32)).astype(BF16)
    mean = jnp.dot(high, blocks, preferred_element_type=F32) + jnp.dot(
        low, blocks, preferred_element_type=F32
    )
    unit = tile * lax.rsqrt(mean + EPS) * gain
    lanes = lane_iota(tile.shape[0])
    other = jnp.where(lanes % 64 < 32, pltpu.roll(unit, 96, 1), pltpu.roll(unit, 32, 1))
    return unit * cosine + other * sine


def half_blocks():
    rows = lax.broadcasted_iota(jnp.int32, (LANES, LANES), 0)
    cols = lax.broadcasted_iota(jnp.int32, (LANES, LANES), 1)
    return jnp.where(rows // 64 == cols // 64, 1.0 / 64.0, 0.0).astype(BF16)


def live(meta, request):
    return meta[0, request] == 1


def live_length(meta, request):
    return jnp.where(live(meta, request), meta[2, request], 0)


def to_chunks(ref, lead, value, chunk):
    rows = value.shape[0]
    for start in range(0, rows, chunk):
        size = min(chunk, rows - start)
        ref[(start // chunk,) + lead + (pl.ds(0, size),)] = value[start : start + size]


def normalized(tok, gain):
    x = tok[0].astype(F32)
    mean = jnp.mean(x * x, axis=-1, keepdims=True)
    return (x * lax.rsqrt(mean + EPS) * gain[...]).astype(BF16)


def query_kernel(req_dev, chunk, cont, clen, tok, gain, w, qg, table, q):
    b = pl.program_id(0)
    count = tok.shape[1]
    half = count // 2
    request = lax.axis_index("req") * req_dev + b
    length = jnp.where(cont[request] == 1, clen[request], 0)
    out = lax.dot_general(
        normalized(tok, gain), w[...], (((1,), (1,)), ((), ())), preferred_element_type=F32
    )
    cosine, sine = rotation(length, count, table)
    blocks = half_blocks()
    gains = jnp.concatenate([qg[...]] * 2, axis=1)
    pair01 = norm_rope(out[:, :128], gains, cosine, sine, blocks)
    pair23 = norm_rope(out[:, 128:256], gains, cosine, sine, blocks)
    last = out[:, 256:320]
    last = jnp.concatenate([last[:half], last[half:]], axis=1)
    lanes = lane_iota(half)
    pick = lambda v: jnp.where(lanes < 64, v[:half], v[half:])
    last = norm_rope(last, gains, pick(cosine), pick(sine), blocks)
    packed = (jnp.concatenate([pair01, pair23, last], axis=0) * 0.125).astype(BF16)
    to_chunks(q, (0,), packed, chunk)


def fresh_kernel(req_dev, meta, tok, gain, w, kg, table, after, fresh):
    del after
    b = pl.program_id(0)
    count = tok.shape[1]
    length = live_length(meta, lax.axis_index("req") * req_dev + b)
    out = jnp.dot(normalized(tok, gain), w[...], preferred_element_type=F32)
    cosine, sine = rotation(length, count, table)
    blocks = half_blocks()
    lanes = lane_iota(count)
    gains = jnp.concatenate([kg[...]] * 2, axis=1)
    for head in range(fresh.shape[1]):
        tile = out[:, head * 128 : head * 128 + 128]
        keys = norm_rope(tile, gains, cosine, sine, blocks)
        fresh[0, head] = jnp.where(lanes < 64, keys, tile).astype(BF16)


def split_heads(packed, count):
    half = count // 2
    wide = packed.astype(F32)
    lanes = lane_iota(count)
    tiles = [wide[:count], pltpu.roll(wide[:count], 64, 1)]
    tiles += [wide[count : 2 * count], pltpu.roll(wide[count : 2 * count], 64, 1)]
    last = wide[2 * count : 2 * count + half]
    tiles.append(jnp.concatenate([last, pltpu.roll(last, 64, 1)], axis=0))
    return [jnp.where(lanes < 64, tile, 0.0).astype(BF16) for tile in tiles]


def soft(scores, values):
    top = jnp.max(scores, axis=-1, keepdims=True)
    weights = jnp.exp(scores - top)
    total = jnp.sum(weights, axis=-1, keepdims=True)
    out = jnp.dot(weights.astype(BF16), values, preferred_element_type=F32)
    return out / total, top + jnp.log(total)


def local_kernel(groups, q, fresh, out):
    heads = 5
    count = fresh.shape[2]
    first = lax.axis_index("tp") * heads
    lanes = lane_iota(count)
    rows = lax.broadcasted_iota(jnp.int32, (count, count), 0)
    cols = lax.broadcasted_iota(jnp.int32, (count, count), 1)
    packed = q[...].reshape(-1, LANES)
    tiles = split_heads(packed, count)
    stats = jnp.zeros((count, LANES), F32)
    kept = []
    for head in range(heads):
        kv = fresh[0, (first + head) // groups]
        scores = lax.dot_general(
            tiles[head], kv, (((1,), (1,)), ((), ())), preferred_element_type=F32
        )
        scores = jnp.where(cols <= rows, scores, NEG)
        mixed, level = soft(scores, kv)
        stats = jnp.where(lanes == head, level, stats)
        kept.append(mixed)
    roll = lambda v: pltpu.roll(v, 64, 1)
    out[0, 0] = jnp.where(lanes < 64, roll(kept[0]), kept[1])
    out[0, 1] = jnp.where(lanes < 64, roll(kept[2]), kept[3])
    out[0, 2] = jnp.where(lanes < 64, roll(kept[4]), roll(stats))


def each(requests, step):
    if requests <= 32:
        for r in range(requests):
            step(r)
    else:
        pl.loop(0, requests)(step)


def route_query_kernel(requests, meta, src, dst):
    def step(r):
        @pl.when(live(meta, r))
        def _():
            dst[meta[1, r]] = src[r]

    each(requests, step)


def route_result_kernel(requests, meta, src, dst):
    def step(r):
        dst[r] = src[jnp.where(live(meta, r), meta[1, r], 0)]

    each(requests, step)


def row_kernel(requests, count, heads, groups, chunk, meta, q, pair, out):
    span = pair.shape[1]
    offset = lax.axis_index("tp") * heads
    first = offset // groups

    row = lax.axis_index("req")

    def find(r, length):
        mine = jnp.logical_and(live(meta, r), meta[1, r] == row)
        return jnp.where(mine, meta[2, r], length)

    length = lax.fori_loop(0, requests, find, 0)
    position = lax.broadcasted_iota(jnp.int32, (8, span), 1)
    bias = jnp.where(position < length, 0.0, NEG)[0:1]
    tiles = split_heads(q[...].reshape(-1, LANES), count)
    lanes = lane_iota(count)
    level = jnp.zeros((count, LANES), F32)
    kept = []
    for head in range(heads):
        kv = pair[(offset + head) // groups - first]
        scores = lax.dot_general(
            tiles[head], kv, (((1,), (1,)), ((), ())), preferred_element_type=F32
        )
        mixed, one = soft(scores + bias, kv)
        level = jnp.where(lanes == head, one, level)
        kept.append(mixed)
    roll = lambda v, n: pltpu.roll(v, n, 1)
    high = level.astype(BF16).astype(F32)
    mid = (level - high).astype(BF16).astype(F32)
    low = (level - high - mid).astype(BF16).astype(F32)
    stats = roll(high, 64) + roll(mid, 64 + heads) + roll(low, 64 + 2 * heads)
    tiles = [
        jnp.where(lanes < 64, roll(kept[0], 64), kept[1]),
        jnp.where(lanes < 64, roll(kept[2], 64), kept[3]),
        jnp.where(lanes < 64, roll(kept[4], 64), stats),
    ]
    to_chunks(out, (), jnp.concatenate(tiles, axis=0).astype(BF16), chunk)


def merge_kernel(req_dev, meta, far, near, mixed):
    heads = 5
    count = near.shape[2]
    b = pl.program_id(0)
    request = lax.axis_index("req") * req_dev + b
    lanes = lane_iota(count)
    roll = lambda v, n: pltpu.roll(v, n, 1)
    packed = far[...].reshape(-1, LANES)
    tiles = [packed[p * count : (p + 1) * count].astype(F32) for p in range(3)]
    stats = roll(tiles[2], 64) + roll(tiles[2], 64 - heads) + roll(tiles[2], 64 - 2 * heads)
    far_level = jnp.where(jnp.logical_and(live(meta, request), lanes < heads), stats, NEG)
    near_level = jnp.where(lanes < heads, roll(near[0, 2], 64), 0.0)
    top = jnp.maximum(far_level, near_level)
    far_part = jnp.exp(far_level - top)
    near_part = jnp.exp(near_level - top)
    share = far_part / (far_part + near_part)
    done = []
    for p in range(3):
        left = share[:, 2 * p : 2 * p + 1]
        right = share[:, 2 * p + 1 : 2 * p + 2] if 2 * p + 1 < heads else left
        weight = jnp.where(lanes < 64, left, right)
        done.append(weight * tiles[p] + (1.0 - weight) * near[0, p])
    half = count // 2
    last = jnp.where(lane_iota(half) < 64, done[2][:half], roll(done[2][half:], 64))
    mixed[0] = jnp.concatenate([done[0], done[1], last], axis=0).astype(BF16)


def project_kernel(block, m_a, m_b, *refs):
    ws, (base, out, lhs) = refs[:-3], refs[-3:]
    count, width = out.shape[1:]
    half = count // 2
    lanes = lane_iota(half)
    for number, m in enumerate((m_a, m_b)):
        for p in range(2):
            col = number * 256 + p * 128
            lhs[:, col : col + 128] = m[0, p * count : (p + 1) * count]
    left = m_a[0, 2 * count :].astype(F32)
    right = m_b[0, 2 * count :].astype(F32)
    lhs[:half, 512:] = jnp.where(lanes < 64, left, pltpu.roll(right, 64, 1)).astype(BF16)
    lhs[half:, 512:] = jnp.where(lanes < 64, pltpu.roll(left, 64, 1), right).astype(BF16)
    for start in range(0, width, block):
        part = pl.ds(start, block)
        if len(ws) == 1:
            weights = ws[0][:, part]
        else:
            weights = jnp.concatenate(
                [w[rows, part] for rows in (pl.ds(0, 256), pl.ds(256, 64)) for w in ws], axis=0
            )
        total = base[0, :, part].astype(F32)
        total += jnp.dot(lhs[...], weights, preferred_element_type=F32)
        out[0, :, part] = total.astype(out.dtype)


def stage_kernel(w_a, w_b, after, out, sem):
    del after
    copies, place = [], 0
    for rows in (pl.ds(0, 256), pl.ds(256, 64)):
        for w in (w_a, w_b):
            dst = out.at[pl.ds(place, rows.size), :]
            copies.append(pltpu.make_async_copy(w.at[rows, :], dst, sem.at[len(copies)]))
            place += rows.size
    for copy in copies:
        copy.start()
    for copy in copies:
        copy.wait()


def held(plane, here):
    apart = plane ^ here
    mid = jnp.logical_or(here == 1, here == 2)
    return jnp.where(apart < 2, apart, jnp.where(mid, 5 - apart, 2 + apart))


def cache_kernel(req_dev, span, steps, meta, *refs):
    blocks, (mine, theirs, _, out, kept_sc, out_sc, sem, out_sem) = refs[:-8], refs[-8:]
    place, tp_place = lax.axis_index("req"), lax.axis_index("tp")
    side = place % 2
    kv_heads, segment = out.shape[1], out.shape[2]
    count = mine.shape[2]
    start = (side * lax.axis_size("tp") + tp_place) * segment
    skip = pl.multiple_of(start - jnp.minimum(start, span - segment), 16)
    first = (place // 2) * 2 * req_dev
    numbers = range(2 * req_dev)
    found = []
    for number in numbers:
        row = jnp.where(live(meta, first + number), meta[1, first + number], place)
        step = 0 if len(blocks[0].shape) == 5 else held(row // 2, place // 2)
        found.append((row // 2, (row % 2) ^ side, step))

    def here(number, action):
        wanted = functools.reduce(jnp.logical_or, [found[number][2] == step for step in steps])
        pl.when(wanted)(action)

    def fetch(number):
        plane, which, step = found[number]
        dst = kept_sc.at[number, :, pl.ds(0, segment), :]
        if len(blocks[0].shape) == 5:
            pltpu.make_async_copy(blocks[0].at[plane, which], dst, sem.at[number]).start()
            return
        for step_of, block in zip(steps, blocks):

            @pl.when(step == step_of)
            def _():
                pltpu.make_async_copy(block.at[which], dst, sem.at[number]).start()

    def write(number):
        return pltpu.make_async_copy(out_sc.at[number], out.at[number], out_sem.at[number])

    def fill(number):
        ahead = live_length(meta, first + number) - start
        rows = lax.broadcasted_iota(jnp.int32, (segment, count), 0)
        cols = lax.broadcasted_iota(jnp.int32, (segment, count), 1)
        shift = jnp.where(rows - cols == ahead, 1.0, 0.0).astype(BF16)
        local = number // req_dev == side
        place_of = number % req_dev
        new = jnp.concatenate(
            [jnp.where(local, mine[place_of, h], theirs[place_of, h]) for h in range(kv_heads)],
            axis=1,
        )
        moved = jnp.dot(shift, new, preferred_element_type=F32)
        old = lax.broadcasted_iota(jnp.int32, (segment, LANES), 0) < ahead
        dst = kept_sc.at[number, :, pl.ds(0, segment), :]
        pltpu.make_async_copy(dst, dst, sem.at[number]).wait()
        for head in range(kv_heads):
            kept = kept_sc[number, head, pl.ds(skip, segment), :].astype(F32)
            part = moved[:, head * LANES : head * LANES + LANES]
            out_sc[number, head] = jnp.where(old, kept, part).astype(BF16)
        write(number).start()

    for number in numbers:
        fetch(number)
    for number in numbers:
        here(number, functools.partial(fill, number))
    for number in numbers:
        here(number, lambda number=number: write(number).wait())


def permuted(value, axis, mask):
    pairs = [(source, source ^ mask) for source in range(lax.axis_size(axis))]
    return lax.ppermute(value, axis, pairs)


def exchanged(value):
    return lax.all_to_all(value, "req", split_axis=0, concat_axis=0, tiled=True)


def full(shape):
    return pl.BlockSpec(shape, lambda *_: (0,) * len(shape))


def on_device(
    tokens,
    attn_gain,
    w_query,
    key_value_weight,
    w_out,
    q_gain,
    k_gain,
    stored,
    continuing,
    cache_row,
    cache_len,
):
    n_req = lax.axis_size("req")
    tp_count = lax.axis_size("tp")
    req_dev, count, width = tokens.shape
    head_dim = q_gain.shape[0]
    kv_heads = key_value_weight.shape[1] // (2 * head_dim)
    heads = w_query.shape[1] // head_dim
    groups = heads * tp_count // kv_heads
    span = stored.shape[2]
    requests = continuing.shape[0]
    segments = 2 * tp_count
    segment = (span + count) // segments
    q_rows = heads * head_dim * count // LANES
    o_rows = -(-heads * head_dim // LANES) * count
    q_chunk = -(-q_rows // (16 * n_req)) * 16
    o_chunk = -(-o_rows // (16 * n_req)) * 16

    table = jnp.asarray(angle_tables(head_dim, count, span))
    table_spec = full(table.shape)
    meta = jnp.stack([continuing, cache_row, cache_len])
    gain_row = attn_gain.reshape(1, width)
    q_gain_row = q_gain.reshape(1, head_dim)
    k_gain_row = k_gain.reshape(1, head_dim)
    w_query_rows = w_query.T
    any_spec = pl.BlockSpec(memory_space=pl.ANY)
    hbm_spec = pl.BlockSpec(memory_space=pltpu.HBM)
    vmem_spec = pl.BlockSpec(memory_space=pltpu.VMEM)
    token_spec = pl.BlockSpec((1, count, width), lambda b: (b, 0, 0))

    side = lax.axis_index("req") % 2
    tp_place = lax.axis_index("tp")

    def part(source, which):
        start = (which * tp_count + tp_place) * segment
        return lax.dynamic_slice_in_dim(source[0], start, segment, 1)

    partner_part = permuted(part(stored, 1 - side), "req", 1)
    q = pl.pallas_call(
        functools.partial(query_kernel, req_dev, q_chunk),
        grid=(req_dev,),
        out_shape=jax.ShapeDtypeStruct((n_req, req_dev, q_chunk, LANES), BF16),
        in_specs=[
            SMEM,
            SMEM,
            token_spec,
            full((1, width)),
            full(w_query_rows.shape),
            full((1, head_dim)),
            table_spec,
        ],
        out_specs=pl.BlockSpec((n_req, 1, q_chunk, LANES), lambda b: (0, b, 0, 0)),
        compiler_params=params(60),
        cost_estimate=cost(2 * req_dev * count * width * 384, 6 << 20),
        name="query",
    )(continuing, cache_len, tokens, gain_row, w_query_rows, q_gain_row, table)
    q_mid = exchanged(q).reshape(requests, q_chunk, LANES)

    partner_part, later = lax.optimization_barrier((partner_part, stored, q))[:2]
    both = jnp.stack([part(later, side), partner_part])
    planes = n_req // 2
    hops = planes == 4

    def crossed(value, pairs):
        pairs = [(2 * a + parity, 2 * b + parity) for a, b in pairs for parity in range(2)]
        return lax.ppermute(value, "req", pairs)

    if hops:
        outer = [(z, z ^ 1) for z in range(planes)]
        beside = crossed(both, outer)
        middle = crossed(both, [(1, 2), (2, 1)])
    else:
        column = [list(range(parity, n_req, 2)) for parity in range(2)]
        blocks = [lax.all_gather(both, "req", axis_index_groups=column)]
        beside = middle = both

    w_x = permuted(w_out, "tp", tp_count // 2)
    w_c = permuted(w_out, "tp", 1)
    w_xc = permuted(w_x, "tp", 1)

    later = lax.optimization_barrier((stored, q_mid))[0]
    pair = lax.dynamic_slice_in_dim(later[0], tp_place * heads // groups, 2, 0)
    fresh = pl.pallas_call(
        functools.partial(fresh_kernel, req_dev),
        grid=(req_dev,),
        out_shape=jax.ShapeDtypeStruct((req_dev, kv_heads, count, LANES), BF16),
        in_specs=[
            SMEM,
            token_spec,
            full((1, width)),
            full(key_value_weight.shape),
            full((1, head_dim)),
            table_spec,
            any_spec,
        ],
        out_specs=pl.BlockSpec((1, kv_heads, count, LANES), lambda b: (b, 0, 0, 0)),
        compiler_params=params(),
        cost_estimate=HINT,
        name="fresh",
    )(meta, tokens, gain_row, key_value_weight, k_gain_row, table, pair)

    q_out = pl.pallas_call(
        functools.partial(route_query_kernel, requests),
        out_shape=jax.ShapeDtypeStruct((n_req, q_chunk, LANES), BF16),
        in_specs=[SMEM, vmem_spec],
        out_specs=vmem_spec,
        compiler_params=params(),
        cost_estimate=cost(0, 1 << 20),
        name="route_query",
    )(meta, q_mid)
    q_row, beside, middle, _ = lax.optimization_barrier((exchanged(q_out), beside, middle, fresh))
    if hops:
        far_middle = crossed(beside, [(1, 2), (2, 1)])
        outward = crossed(middle, outer)
    fresh_partner = permuted(fresh, "req", 1)

    near = pl.pallas_call(
        functools.partial(local_kernel, groups),
        grid=(req_dev,),
        out_shape=jax.ShapeDtypeStruct((req_dev, 3, count, LANES), F32),
        in_specs=[
            pl.BlockSpec((n_req, 1, q_chunk, LANES), lambda b: (0, b, 0, 0)),
            pl.BlockSpec((1, kv_heads, count, LANES), lambda b: (b, 0, 0, 0)),
        ],
        out_specs=pl.BlockSpec((1, 3, count, LANES), lambda b: (b, 0, 0, 0)),
        compiler_params=params(),
        cost_estimate=HINT,
        name="attend_new",
    )(q, fresh)

    far = pl.pallas_call(
        functools.partial(row_kernel, requests, count, heads, groups, o_chunk),
        out_shape=jax.ShapeDtypeStruct((n_req, o_chunk, LANES), BF16),
        in_specs=[SMEM, vmem_spec, vmem_spec],
        out_specs=vmem_spec,
        compiler_params=params(40),
        cost_estimate=cost(4 * heads * count * span * 256, 32 << 20),
        name="attend_row",
    )(meta, q_row, pair)

    far_mid = exchanged(far)
    if hops:
        far_mid = lax.optimization_barrier((far_mid, far_middle, outward, fresh_partner, near))[0]
        far_outward = crossed(far_middle, outer)
        blocks = [both, beside, middle, far_middle, outward, far_outward]
    def fill_cache(steps, blocks, after, aliases):
        return pl.pallas_call(
            functools.partial(cache_kernel, req_dev, span, steps),
            in_specs=[SMEM] + [any_spec] * len(blocks) + [vmem_spec, vmem_spec, any_spec],
            out_specs=any_spec,
            scratch_shapes=[
                pltpu.VMEM((2 * req_dev, kv_heads, 2 * segment, LANES), BF16),
                pltpu.VMEM((2 * req_dev, kv_heads, segment, LANES), BF16),
                pltpu.SemaphoreType.DMA((2 * req_dev,)),
                pltpu.SemaphoreType.DMA((2 * req_dev,)),
            ],
            out_shape=jax.ShapeDtypeStruct((2 * req_dev, kv_heads, segment, LANES), BF16),
            input_output_aliases=aliases,
            compiler_params=params(),
            cost_estimate=HINT,
            name="cache",
        )(meta, *blocks, fresh, fresh_partner, after)

    if hops:
        cache = fill_cache(tuple(range(5)), blocks[:5], far_mid, {})

    far_out = pl.pallas_call(
        functools.partial(route_result_kernel, requests),
        out_shape=jax.ShapeDtypeStruct((requests, o_chunk, LANES), BF16),
        in_specs=[SMEM, vmem_spec],
        out_specs=vmem_spec,
        compiler_params=params(),
        cost_estimate=cost(0, 1 << 20),
        name="route_result",
    )(meta, far_mid)
    far_home = exchanged(far_out.reshape(n_req, req_dev, o_chunk, LANES))
    if hops:
        far_home = lax.optimization_barrier((far_home, cache))[0]

    mixed = pl.pallas_call(
        functools.partial(merge_kernel, req_dev),
        grid=(req_dev,),
        out_shape=jax.ShapeDtypeStruct((req_dev, q_rows, LANES), BF16),
        in_specs=[
            SMEM,
            pl.BlockSpec((n_req, 1, o_chunk, LANES), lambda b: (0, b, 0, 0)),
            pl.BlockSpec((1, 3, count, LANES), lambda b: (b, 0, 0, 0)),
        ],
        out_specs=pl.BlockSpec((1, q_rows, LANES), lambda b: (b, 0, 0)),
        compiler_params=params(),
        cost_estimate=HINT,
        name="merge",
    )(meta, far_home, near)

    m_x = permuted(mixed, "tp", tp_count // 2)
    m_c = permuted(mixed, "tp", 1)

    def project(m_a, m_b, ws, base, dtype, name):
        m_spec = pl.BlockSpec((1, q_rows, LANES), lambda b: (b, 0, 0))
        return pl.pallas_call(
            functools.partial(project_kernel, 512),
            grid=(req_dev,),
            out_shape=jax.ShapeDtypeStruct(tokens.shape, dtype),
            in_specs=[m_spec] * 2 + [full(w.shape) for w in ws] + [token_spec],
            out_specs=token_spec,
            scratch_shapes=[pltpu.VMEM((count, 640), BF16)],
            compiler_params=params(),
            cost_estimate=HINT,
            name=name,
        )(m_a, m_b, *ws, base)

    partial = project(mixed, m_c, (w_out, w_c), tokens, F32, "project_chip")
    staged = pl.pallas_call(
        stage_kernel,
        out_shape=jax.ShapeDtypeStruct((2 * w_out.shape[0], width), BF16),
        in_specs=[any_spec] * 3,
        out_specs=vmem_spec,
        scratch_shapes=[pltpu.SemaphoreType.DMA((4,))],
        compiler_params=params(),
        cost_estimate=HINT,
        name="stage",
    )(w_x, w_xc, partial)
    m_x = lax.optimization_barrier((m_x, partial, staged))[0]
    m_xc = permuted(m_x, "tp", 1)
    layer = project(m_x, m_xc, (staged,), partial, BF16, "project_rest")

    if hops:
        cache = fill_cache((5,), [far_outward], cache, {4: 0})
    else:
        cache = fill_cache((0,), blocks, layer, {})
    return (layer, cache)


def solution(mesh):
    return jax.shard_map(
        on_device,
        mesh=mesh,
        in_specs=(
            P("req", None, None),
            P(),
            P(None, "tp"),
            P(),
            P("tp", None),
            P(),
            P(),
            P("req", None, None, None),
            P(),
            P(),
            P(),
        ),
        out_specs=(P("req", None, None), P("req", None, "tp", None)),
        check_vma=False,
    )
```

```python
import functools
import math

import jax
import jax.numpy as jnp
import numpy as np
from jax import lax
from jax.experimental import pallas as pl
from jax.experimental.pallas import tpu as pltpu
from jax.sharding import PartitionSpec as P

BF16 = jnp.bfloat16
F32 = jnp.float32
LANES = 128
EPS = 1e-06
NEG = -1e30
SMEM = pl.BlockSpec(memory_space=pltpu.SMEM)


HINT = pl.CostEstimate(flops=0, bytes_accessed=1024, transcendentals=0)


def cost(flops, moved):
    return pl.CostEstimate(flops=int(flops), bytes_accessed=int(moved), transcendentals=0)


def params(mib=20):
    return pltpu.CompilerParams(vmem_limit_bytes=mib << 20)


def lane_iota(rows):
    return lax.broadcasted_iota(jnp.int32, (rows, LANES), 1)


def angle_tables(head_dim, new_count, cache_span):
    half = head_dim // 2
    freq = np.exp(-math.log(10000.0) * np.arange(half, dtype=np.float64) * 2.0 / head_dim)
    freq = np.tile(freq.astype(np.float32).astype(np.float64), LANES // half)

    def pair(positions):
        angle = positions[:, None].astype(np.float64) * freq[None, :]
        return np.cos(angle).astype(np.float32), np.sin(angle).astype(np.float32)

    fine = pair(np.arange(new_count))
    coarse = pair(np.arange(cache_span // 16 + 8) * 16)
    small = pair(np.arange(16))
    return np.stack([np.concatenate(part) for part in zip(fine, small, coarse)])


def rotation(length, count, table):
    high = length // 16
    low = length - high * 16
    row = lambda which, place: table[which, pl.ds(place, 1), :]
    ch, sh = row(0, count + 16 + high), row(1, count + 16 + high)
    cl, sl = row(0, count + low), row(1, count + low)
    cb, sb = ch * cl - sh * sl, sh * cl + ch * sl
    ci, si = table[0, :count], table[1, :count]
    cosine = ci * cb - si * sb
    sine = si * cb + ci * sb
    lanes = lane_iota(ci.shape[0])
    return cosine, jnp.where(lanes % 64 < 32, -sine, sine)


def norm_rope(tile, gain, cosine, sine, blocks):
    square = tile * tile
    high = square.astype(BF16)
    low = (square - high.astype(F32)).astype(BF16)
    mean = jnp.dot(high, blocks, preferred_element_type=F32) + jnp.dot(
        low, blocks, preferred_element_type=F32
    )
    unit = tile * lax.rsqrt(mean + EPS) * gain
    lanes = lane_iota(tile.shape[0])
    other = jnp.where(lanes % 64 < 32, pltpu.roll(unit, 96, 1), pltpu.roll(unit, 32, 1))
    return unit * cosine + other * sine


def half_blocks():
    rows = lax.broadcasted_iota(jnp.int32, (LANES, LANES), 0)
    cols = lax.broadcasted_iota(jnp.int32, (LANES, LANES), 1)
    return jnp.where(rows // 64 == cols // 64, 1.0 / 64.0, 0.0).astype(BF16)


def live(meta, request):
    return meta[0, request] == 1


def live_length(meta, request):
    return jnp.where(live(meta, request), meta[2, request], 0)


def to_chunks(ref, lead, value, chunk):
    rows = value.shape[0]
    for start in range(0, rows, chunk):
        size = min(chunk, rows - start)
        ref[(start // chunk,) + lead + (pl.ds(0, size),)] = value[start : start + size]


def normalized(tok, gain):
    x = tok[0].astype(F32)
    mean = jnp.mean(x * x, axis=-1, keepdims=True)
    return (x * lax.rsqrt(mean + EPS) * gain[...]).astype(BF16)


def query_kernel(req_dev, chunk, cont, clen, tok, gain, w, qg, table, q):
    b = pl.program_id(0)
    count = tok.shape[1]
    half = count // 2
    request = lax.axis_index("req") * req_dev + b
    length = jnp.where(cont[request] == 1, clen[request], 0)
    out = lax.dot_general(
        normalized(tok, gain), w[...], (((1,), (1,)), ((), ())), preferred_element_type=F32
    )
    cosine, sine = rotation(length, count, table)
    blocks = half_blocks()
    gains = jnp.concatenate([qg[...]] * 2, axis=1)
    pair01 = norm_rope(out[:, :128], gains, cosine, sine, blocks)
    pair23 = norm_rope(out[:, 128:256], gains, cosine, sine, blocks)
    last = out[:, 256:320]
    last = jnp.concatenate([last[:half], last[half:]], axis=1)
    lanes = lane_iota(half)
    pick = lambda v: jnp.where(lanes < 64, v[:half], v[half:])
    last = norm_rope(last, gains, pick(cosine), pick(sine), blocks)
    packed = (jnp.concatenate([pair01, pair23, last], axis=0) * 0.125).astype(BF16)
    to_chunks(q, (0,), packed, chunk)


def fresh_kernel(req_dev, meta, tok, gain, w, kg, table, after, fresh):
    del after
    b = pl.program_id(0)
    count = tok.shape[1]
    length = live_length(meta, lax.axis_index("req") * req_dev + b)
    out = jnp.dot(normalized(tok, gain), w[...], preferred_element_type=F32)
    cosine, sine = rotation(length, count, table)
    blocks = half_blocks()
    lanes = lane_iota(count)
    gains = jnp.concatenate([kg[...]] * 2, axis=1)
    for head in range(fresh.shape[1]):
        tile = out[:, head * 128 : head * 128 + 128]
        keys = norm_rope(tile, gains, cosine, sine, blocks)
        fresh[0, head] = jnp.where(lanes < 64, keys, tile).astype(BF16)


def split_heads(packed, count):
    half = count // 2
    wide = packed.astype(F32)
    lanes = lane_iota(count)
    tiles = [wide[:count], pltpu.roll(wide[:count], 64, 1)]
    tiles += [wide[count : 2 * count], pltpu.roll(wide[count : 2 * count], 64, 1)]
    last = wide[2 * count : 2 * count + half]
    tiles.append(jnp.concatenate([last, pltpu.roll(last, 64, 1)], axis=0))
    return [jnp.where(lanes < 64, tile, 0.0).astype(BF16) for tile in tiles]


def soft(scores, values):
    top = jnp.max(scores, axis=-1, keepdims=True)
    weights = jnp.exp(scores - top)
    total = jnp.sum(weights, axis=-1, keepdims=True)
    out = jnp.dot(weights.astype(BF16), values, preferred_element_type=F32)
    return out / total, top + jnp.log(total)


def local_kernel(groups, q, fresh, out):
    heads = 5
    count = fresh.shape[2]
    first = lax.axis_index("tp") * heads
    lanes = lane_iota(count)
    rows = lax.broadcasted_iota(jnp.int32, (count, count), 0)
    cols = lax.broadcasted_iota(jnp.int32, (count, count), 1)
    packed = q[...].reshape(-1, LANES)
    tiles = split_heads(packed, count)
    stats = jnp.zeros((count, LANES), F32)
    kept = []
    for head in range(heads):
        kv = fresh[0, (first + head) // groups]
        scores = lax.dot_general(
            tiles[head], kv, (((1,), (1,)), ((), ())), preferred_element_type=F32
        )
        scores = jnp.where(cols <= rows, scores, NEG)
        mixed, level = soft(scores, kv)
        stats = jnp.where(lanes == head, level, stats)
        kept.append(mixed)
    roll = lambda v: pltpu.roll(v, 64, 1)
    out[0, 0] = jnp.where(lanes < 64, roll(kept[0]), kept[1])
    out[0, 1] = jnp.where(lanes < 64, roll(kept[2]), kept[3])
    out[0, 2] = jnp.where(lanes < 64, roll(kept[4]), roll(stats))


def each(requests, step):
    if requests <= 32:
        for r in range(requests):
            step(r)
    else:
        pl.loop(0, requests)(step)


def route_query_kernel(requests, meta, src, dst):
    def step(r):
        @pl.when(live(meta, r))
        def _():
            dst[meta[1, r]] = src[r]

    each(requests, step)


def route_result_kernel(requests, meta, src, dst):
    def step(r):
        dst[r] = src[jnp.where(live(meta, r), meta[1, r], 0)]

    each(requests, step)


def row_kernel(requests, count, heads, groups, chunk, meta, q, pair, out):
    span = pair.shape[1]
    offset = lax.axis_index("tp") * heads
    first = offset // groups

    row = lax.axis_index("req")

    def find(r, length):
        mine = jnp.logical_and(live(meta, r), meta[1, r] == row)
        return jnp.where(mine, meta[2, r], length)

    length = lax.fori_loop(0, requests, find, 0)
    position = lax.broadcasted_iota(jnp.int32, (8, span), 1)
    bias = jnp.where(position < length, 0.0, NEG)[0:1]
    tiles = split_heads(q[...].reshape(-1, LANES), count)
    lanes = lane_iota(count)
    level = jnp.zeros((count, LANES), F32)
    kept = []
    for head in range(heads):
        kv = pair[(offset + head) // groups - first]
        scores = lax.dot_general(
            tiles[head], kv, (((1,), (1,)), ((), ())), preferred_element_type=F32
        )
        mixed, one = soft(scores + bias, kv)
        level = jnp.where(lanes == head, one, level)
        kept.append(mixed)
    roll = lambda v, n: pltpu.roll(v, n, 1)
    high = level.astype(BF16).astype(F32)
    mid = (level - high).astype(BF16).astype(F32)
    low = (level - high - mid).astype(BF16).astype(F32)
    stats = roll(high, 64) + roll(mid, 64 + heads) + roll(low, 64 + 2 * heads)
    tiles = [
        jnp.where(lanes < 64, roll(kept[0], 64), kept[1]),
        jnp.where(lanes < 64, roll(kept[2], 64), kept[3]),
        jnp.where(lanes < 64, roll(kept[4], 64), stats),
    ]
    to_chunks(out, (), jnp.concatenate(tiles, axis=0).astype(BF16), chunk)


def merge_kernel(req_dev, meta, far, near, mixed):
    heads = 5
    count = near.shape[2]
    b = pl.program_id(0)
    request = lax.axis_index("req") * req_dev + b
    lanes = lane_iota(count)
    roll = lambda v, n: pltpu.roll(v, n, 1)
    packed = far[...].reshape(-1, LANES)
    tiles = [packed[p * count : (p + 1) * count].astype(F32) for p in range(3)]
    stats = roll(tiles[2], 64) + roll(tiles[2], 64 - heads) + roll(tiles[2], 64 - 2 * heads)
    far_level = jnp.where(jnp.logical_and(live(meta, request), lanes < heads), stats, NEG)
    near_level = jnp.where(lanes < heads, roll(near[0, 2], 64), 0.0)
    top = jnp.maximum(far_level, near_level)
    far_part = jnp.exp(far_level - top)
    near_part = jnp.exp(near_level - top)
    share = far_part / (far_part + near_part)
    done = []
    for p in range(3):
        left = share[:, 2 * p : 2 * p + 1]
        right = share[:, 2 * p + 1 : 2 * p + 2] if 2 * p + 1 < heads else left
        weight = jnp.where(lanes < 64, left, right)
        done.append(weight * tiles[p] + (1.0 - weight) * near[0, p])
    half = count // 2
    last = jnp.where(lane_iota(half) < 64, done[2][:half], roll(done[2][half:], 64))
    mixed[0] = jnp.concatenate([done[0], done[1], last], axis=0).astype(BF16)


def project_kernel(block, m_a, m_b, *refs):
    ws, (base, out, lhs) = refs[:-3], refs[-3:]
    count, width = out.shape[1:]
    half = count // 2
    lanes = lane_iota(half)
    for number, m in enumerate((m_a, m_b)):
        for p in range(2):
            col = number * 256 + p * 128
            lhs[:, col : col + 128] = m[0, p * count : (p + 1) * count]
    left = m_a[0, 2 * count :].astype(F32)
    right = m_b[0, 2 * count :].astype(F32)
    lhs[:half, 512:] = jnp.where(lanes < 64, left, pltpu.roll(right, 64, 1)).astype(BF16)
    lhs[half:, 512:] = jnp.where(lanes < 64, pltpu.roll(left, 64, 1), right).astype(BF16)
    for start in range(0, width, block):
        part = pl.ds(start, block)
        if len(ws) == 1:
            weights = ws[0][:, part]
        else:
            weights = jnp.concatenate(
                [w[rows, part] for rows in (pl.ds(0, 256), pl.ds(256, 64)) for w in ws], axis=0
            )
        total = base[0, :, part].astype(F32)
        total += jnp.dot(lhs[...], weights, preferred_element_type=F32)
        out[0, :, part] = total.astype(out.dtype)


def stage_kernel(w_a, w_b, after, out, sem):
    del after
    copies, place = [], 0
    for rows in (pl.ds(0, 256), pl.ds(256, 64)):
        for w in (w_a, w_b):
            dst = out.at[pl.ds(place, rows.size), :]
            copies.append(pltpu.make_async_copy(w.at[rows, :], dst, sem.at[len(copies)]))
            place += rows.size
    for copy in copies:
        copy.start()
    for copy in copies:
        copy.wait()


def held(plane, here):
    apart = plane ^ here
    mid = jnp.logical_or(here == 1, here == 2)
    return jnp.where(apart < 2, apart, jnp.where(mid, 5 - apart, 2 + apart))


def cache_kernel(req_dev, span, steps, meta, *refs):
    blocks, (mine, theirs, _, out, kept_sc, out_sc, sem, out_sem) = refs[:-8], refs[-8:]
    place, tp_place = lax.axis_index("req"), lax.axis_index("tp")
    side = place % 2
    kv_heads, segment = out.shape[1], out.shape[2]
    count = mine.shape[2]
    start = (side * lax.axis_size("tp") + tp_place) * segment
    skip = pl.multiple_of(start - jnp.minimum(start, span - segment), 16)
    first = (place // 2) * 2 * req_dev
    numbers = range(2 * req_dev)
    found = []
    for number in numbers:
        row = jnp.where(live(meta, first + number), meta[1, first + number], place)
        step = 0 if len(blocks[0].shape) == 5 else held(row // 2, place // 2)
        found.append((row // 2, (row % 2) ^ side, step))

    def here(number, action):
        wanted = functools.reduce(jnp.logical_or, [found[number][2] == step for step in steps])
        pl.when(wanted)(action)

    def fetch(number):
        plane, which, step = found[number]
        dst = kept_sc.at[number, :, pl.ds(0, segment), :]
        if len(blocks[0].shape) == 5:
            pltpu.make_async_copy(blocks[0].at[plane, which], dst, sem.at[number]).start()
            return
        for step_of, block in zip(steps, blocks):

            @pl.when(step == step_of)
            def _():
                pltpu.make_async_copy(block.at[which], dst, sem.at[number]).start()

    def write(number):
        return pltpu.make_async_copy(out_sc.at[number], out.at[number], out_sem.at[number])

    def fill(number):
        ahead = live_length(meta, first + number) - start
        rows = lax.broadcasted_iota(jnp.int32, (segment, count), 0)
        cols = lax.broadcasted_iota(jnp.int32, (segment, count), 1)
        shift = jnp.where(rows - cols == ahead, 1.0, 0.0).astype(BF16)
        local = number // req_dev == side
        place_of = number % req_dev
        new = jnp.concatenate(
            [jnp.where(local, mine[place_of, h], theirs[place_of, h]) for h in range(kv_heads)],
            axis=1,
        )
        moved = jnp.dot(shift, new, preferred_element_type=F32)
        old = lax.broadcasted_iota(jnp.int32, (segment, LANES), 0) < ahead
        dst = kept_sc.at[number, :, pl.ds(0, segment), :]
        pltpu.make_async_copy(dst, dst, sem.at[number]).wait()
        for head in range(kv_heads):
            kept = kept_sc[number, head, pl.ds(skip, segment), :].astype(F32)
            part = moved[:, head * LANES : head * LANES + LANES]
            out_sc[number, head] = jnp.where(old, kept, part).astype(BF16)
        write(number).start()

    for number in numbers:
        fetch(number)
    for number in numbers:
        here(number, functools.partial(fill, number))
    for number in numbers:
        here(number, lambda number=number: write(number).wait())


def permuted(value, axis, mask):
    pairs = [(source, source ^ mask) for source in range(lax.axis_size(axis))]
    return lax.ppermute(value, axis, pairs)


def exchanged(value):
    return lax.all_to_all(value, "req", split_axis=0, concat_axis=0, tiled=True)


def full(shape):
    return pl.BlockSpec(shape, lambda *_: (0,) * len(shape))


def on_device(
    tokens,
    attn_gain,
    w_query,
    key_value_weight,
    w_out,
    q_gain,
    k_gain,
    stored,
    continuing,
    cache_row,
    cache_len,
):
    n_req = lax.axis_size("req")
    tp_count = lax.axis_size("tp")
    req_dev, count, width = tokens.shape
    head_dim = q_gain.shape[0]
    kv_heads = key_value_weight.shape[1] // (2 * head_dim)
    heads = w_query.shape[1] // head_dim
    groups = heads * tp_count // kv_heads
    span = stored.shape[2]
    requests = continuing.shape[0]
    segments = 2 * tp_count
    segment = (span + count) // segments
    q_rows = heads * head_dim * count // LANES
    o_rows = -(-heads * head_dim // LANES) * count
    q_chunk = -(-q_rows // (16 * n_req)) * 16
    o_chunk = -(-o_rows // (16 * n_req)) * 16

    table = jnp.asarray(angle_tables(head_dim, count, span))
    table_spec = full(table.shape)
    meta = jnp.stack([continuing, cache_row, cache_len])
    gain_row = attn_gain.reshape(1, width)
    q_gain_row = q_gain.reshape(1, head_dim)
    k_gain_row = k_gain.reshape(1, head_dim)
    w_query_rows = w_query.T
    any_spec = pl.BlockSpec(memory_space=pl.ANY)
    hbm_spec = pl.BlockSpec(memory_space=pltpu.HBM)
    vmem_spec = pl.BlockSpec(memory_space=pltpu.VMEM)
    token_spec = pl.BlockSpec((1, count, width), lambda b: (b, 0, 0))

    side = lax.axis_index("req") % 2
    tp_place = lax.axis_index("tp")

    def part(source, which):
        start = (which * tp_count + tp_place) * segment
        return lax.dynamic_slice_in_dim(source[0], start, segment, 1)

    partner_part = permuted(part(stored, 1 - side), "req", 1)
    q = pl.pallas_call(
        functools.partial(query_kernel, req_dev, q_chunk),
        grid=(req_dev,),
        out_shape=jax.ShapeDtypeStruct((n_req, req_dev, q_chunk, LANES), BF16),
        in_specs=[
            SMEM,
            SMEM,
            token_spec,
            full((1, width)),
            full(w_query_rows.shape),
            full((1, head_dim)),
            table_spec,
        ],
        out_specs=pl.BlockSpec((n_req, 1, q_chunk, LANES), lambda b: (0, b, 0, 0)),
        compiler_params=params(60),
        cost_estimate=cost(2 * req_dev * count * width * 384, 6 << 20),
        name="query",
    )(continuing, cache_len, tokens, gain_row, w_query_rows, q_gain_row, table)
    q_mid = exchanged(q).reshape(requests, q_chunk, LANES)

    partner_part, later = lax.optimization_barrier((partner_part, stored, q))[:2]
    both = jnp.stack([part(later, side), partner_part])
    planes = n_req // 2
    hops = planes == 4

    def crossed(value, pairs):
        pairs = [(2 * a + parity, 2 * b + parity) for a, b in pairs for parity in range(2)]
        return lax.ppermute(value, "req", pairs)

    if hops:
        outer = [(z, z ^ 1) for z in range(planes)]
        beside = crossed(both, outer)
        middle = crossed(both, [(1, 2), (2, 1)])
    else:
        column = [list(range(parity, n_req, 2)) for parity in range(2)]
        blocks = [lax.all_gather(both, "req", axis_index_groups=column)]
        beside = middle = both

    w_x = permuted(w_out, "tp", tp_count // 2)
    w_c = permuted(w_out, "tp", 1)
    w_xc = permuted(w_x, "tp", 1)

    later = lax.optimization_barrier((stored, q_mid))[0]
    pair = lax.dynamic_slice_in_dim(later[0], tp_place * heads // groups, 2, 0)
    fresh = pl.pallas_call(
        functools.partial(fresh_kernel, req_dev),
        grid=(req_dev,),
        out_shape=jax.ShapeDtypeStruct((req_dev, kv_heads, count, LANES), BF16),
        in_specs=[
            SMEM,
            token_spec,
            full((1, width)),
            full(key_value_weight.shape),
            full((1, head_dim)),
            table_spec,
            any_spec,
        ],
        out_specs=pl.BlockSpec((1, kv_heads, count, LANES), lambda b: (b, 0, 0, 0)),
        compiler_params=params(),
        cost_estimate=HINT,
        name="fresh",
    )(meta, tokens, gain_row, key_value_weight, k_gain_row, table, pair)

    q_out = pl.pallas_call(
        functools.partial(route_query_kernel, requests),
        out_shape=jax.ShapeDtypeStruct((n_req, q_chunk, LANES), BF16),
        in_specs=[SMEM, vmem_spec],
        out_specs=vmem_spec,
        compiler_params=params(),
        cost_estimate=cost(0, 1 << 20),
        name="route_query",
    )(meta, q_mid)
    q_row, beside, middle, _ = lax.optimization_barrier((exchanged(q_out), beside, middle, fresh))
    if hops:
        far_middle = crossed(beside, [(1, 2), (2, 1)])
        outward = crossed(middle, outer)
    fresh_partner = permuted(fresh, "req", 1)

    near = pl.pallas_call(
        functools.partial(local_kernel, groups),
        grid=(req_dev,),
        out_shape=jax.ShapeDtypeStruct((req_dev, 3, count, LANES), F32),
        in_specs=[
            pl.BlockSpec((n_req, 1, q_chunk, LANES), lambda b: (0, b, 0, 0)),
            pl.BlockSpec((1, kv_heads, count, LANES), lambda b: (b, 0, 0, 0)),
        ],
        out_specs=pl.BlockSpec((1, 3, count, LANES), lambda b: (b, 0, 0, 0)),
        compiler_params=params(),
        cost_estimate=HINT,
        name="attend_new",
    )(q, fresh)

    far = pl.pallas_call(
        functools.partial(row_kernel, requests, count, heads, groups, o_chunk),
        out_shape=jax.ShapeDtypeStruct((n_req, o_chunk, LANES), BF16),
        in_specs=[SMEM, vmem_spec, vmem_spec],
        out_specs=vmem_spec,
        compiler_params=params(60),
        cost_estimate=cost(4 * heads * count * span * 256, 32 << 20),
        name="attend_row",
    )(meta, q_row, pair)

    far_mid = exchanged(far)
    if hops:
        far_mid = lax.optimization_barrier((far_mid, far_middle, outward, fresh_partner, near))[0]
        far_outward = crossed(far_middle, outer)
        blocks = [both, beside, middle, far_middle, outward, far_outward]
    def fill_cache(steps, blocks, after, aliases):
        return pl.pallas_call(
            functools.partial(cache_kernel, req_dev, span, steps),
            in_specs=[SMEM] + [any_spec] * len(blocks) + [vmem_spec, vmem_spec, any_spec],
            out_specs=any_spec,
            scratch_shapes=[
                pltpu.VMEM((2 * req_dev, kv_heads, 2 * segment, LANES), BF16),
                pltpu.VMEM((2 * req_dev, kv_heads, segment, LANES), BF16),
                pltpu.SemaphoreType.DMA((2 * req_dev,)),
                pltpu.SemaphoreType.DMA((2 * req_dev,)),
            ],
            out_shape=jax.ShapeDtypeStruct((2 * req_dev, kv_heads, segment, LANES), BF16),
            input_output_aliases=aliases,
            compiler_params=params(),
            cost_estimate=HINT,
            name="cache",
        )(meta, *blocks, fresh, fresh_partner, after)

    if hops:
        cache = fill_cache(tuple(range(5)), blocks[:5], far_mid, {})

    far_out = pl.pallas_call(
        functools.partial(route_result_kernel, requests),
        out_shape=jax.ShapeDtypeStruct((requests, o_chunk, LANES), BF16),
        in_specs=[SMEM, vmem_spec],
        out_specs=vmem_spec,
        compiler_params=params(),
        cost_estimate=cost(0, 1 << 20),
        name="route_result",
    )(meta, far_mid)
    far_home = exchanged(far_out.reshape(n_req, req_dev, o_chunk, LANES))
    if hops:
        far_home = lax.optimization_barrier((far_home, cache))[0]

    mixed = pl.pallas_call(
        functools.partial(merge_kernel, req_dev),
        grid=(req_dev,),
        out_shape=jax.ShapeDtypeStruct((req_dev, q_rows, LANES), BF16),
        in_specs=[
            SMEM,
            pl.BlockSpec((n_req, 1, o_chunk, LANES), lambda b: (0, b, 0, 0)),
            pl.BlockSpec((1, 3, count, LANES), lambda b: (b, 0, 0, 0)),
        ],
        out_specs=pl.BlockSpec((1, q_rows, LANES), lambda b: (b, 0, 0)),
        compiler_params=params(),
        cost_estimate=HINT,
        name="merge",
    )(meta, far_home, near)

    m_x = permuted(mixed, "tp", tp_count // 2)
    m_c = permuted(mixed, "tp", 1)

    def project(m_a, m_b, ws, base, dtype, name):
        m_spec = pl.BlockSpec((1, q_rows, LANES), lambda b: (b, 0, 0))
        return pl.pallas_call(
            functools.partial(project_kernel, 512),
            grid=(req_dev,),
            out_shape=jax.ShapeDtypeStruct(tokens.shape, dtype),
            in_specs=[m_spec] * 2 + [full(w.shape) for w in ws] + [token_spec],
            out_specs=token_spec,
            scratch_shapes=[pltpu.VMEM((count, 640), BF16)],
            compiler_params=params(),
            cost_estimate=HINT,
            name=name,
        )(m_a, m_b, *ws, base)

    partial = project(mixed, m_c, (w_out, w_c), tokens, F32, "project_chip")
    staged = pl.pallas_call(
        stage_kernel,
        out_shape=jax.ShapeDtypeStruct((2 * w_out.shape[0], width), BF16),
        in_specs=[any_spec] * 3,
        out_specs=vmem_spec,
        scratch_shapes=[pltpu.SemaphoreType.DMA((4,))],
        compiler_params=params(),
        cost_estimate=HINT,
        name="stage",
    )(w_x, w_xc, partial)
    if hops:
        last = lax.optimization_barrier((far_outward, staged))[0]
        cache = fill_cache((5,), [last], cache, {4: 0})
        m_x = lax.optimization_barrier((m_x, cache))[0]
    m_x = lax.optimization_barrier((m_x, partial, staged))[0]
    m_xc = permuted(m_x, "tp", 1)
    layer = project(m_x, m_xc, (staged,), partial, BF16, "project_rest")

    if not hops:
        cache = fill_cache((0,), blocks, layer, {})
    return (layer, cache)


def solution(mesh):
    return jax.shard_map(
        on_device,
        mesh=mesh,
        in_specs=(
            P("req", None, None),
            P(),
            P(None, "tp"),
            P(),
            P("tp", None),
            P(),
            P(),
            P("req", None, None, None),
            P(),
            P(),
            P(),
        ),
        out_specs=(P("req", None, None), P("req", None, "tp", None)),
        check_vma=False,
    )
```

```python
import functools
import math

import jax
import jax.numpy as jnp
import numpy as np
from jax import lax
from jax.experimental import pallas as pl
from jax.experimental.pallas import tpu as pltpu
from jax.sharding import PartitionSpec as P

BF16 = jnp.bfloat16
F32 = jnp.float32
LANES = 128
EPS = 1e-06
NEG = -1e30
SMEM = pl.BlockSpec(memory_space=pltpu.SMEM)


HINT = pl.CostEstimate(flops=0, bytes_accessed=1024, transcendentals=0)


def cost(flops, moved):
    return pl.CostEstimate(flops=int(flops), bytes_accessed=int(moved), transcendentals=0)


def params(mib=20):
    return pltpu.CompilerParams(vmem_limit_bytes=mib << 20)


def lane_iota(rows):
    return lax.broadcasted_iota(jnp.int32, (rows, LANES), 1)


def angle_tables(head_dim, new_count, cache_span):
    half = head_dim // 2
    freq = np.exp(-math.log(10000.0) * np.arange(half, dtype=np.float64) * 2.0 / head_dim)
    freq = np.tile(freq.astype(np.float32).astype(np.float64), LANES // half)

    def pair(positions):
        angle = positions[:, None].astype(np.float64) * freq[None, :]
        return np.cos(angle).astype(np.float32), np.sin(angle).astype(np.float32)

    fine = pair(np.arange(new_count))
    coarse = pair(np.arange(cache_span // 16 + 8) * 16)
    small = pair(np.arange(16))
    return np.stack([np.concatenate(part) for part in zip(fine, small, coarse)])


def rotation(length, count, table):
    high = length // 16
    low = length - high * 16
    row = lambda which, place: table[which, pl.ds(place, 1), :]
    ch, sh = row(0, count + 16 + high), row(1, count + 16 + high)
    cl, sl = row(0, count + low), row(1, count + low)
    cb, sb = ch * cl - sh * sl, sh * cl + ch * sl
    ci, si = table[0, :count], table[1, :count]
    cosine = ci * cb - si * sb
    sine = si * cb + ci * sb
    lanes = lane_iota(ci.shape[0])
    return cosine, jnp.where(lanes % 64 < 32, -sine, sine)


def norm_rope(tile, gain, cosine, sine, blocks):
    square = tile * tile
    high = square.astype(BF16)
    low = (square - high.astype(F32)).astype(BF16)
    mean = jnp.dot(high, blocks, preferred_element_type=F32) + jnp.dot(
        low, blocks, preferred_element_type=F32
    )
    unit = tile * lax.rsqrt(mean + EPS) * gain
    lanes = lane_iota(tile.shape[0])
    other = jnp.where(lanes % 64 < 32, pltpu.roll(unit, 96, 1), pltpu.roll(unit, 32, 1))
    return unit * cosine + other * sine


def half_blocks():
    rows = lax.broadcasted_iota(jnp.int32, (LANES, LANES), 0)
    cols = lax.broadcasted_iota(jnp.int32, (LANES, LANES), 1)
    return jnp.where(rows // 64 == cols // 64, 1.0 / 64.0, 0.0).astype(BF16)


def live(meta, request):
    return meta[0, request] == 1


def live_length(meta, request):
    return jnp.where(live(meta, request), meta[2, request], 0)


def to_chunks(ref, lead, value, chunk):
    rows = value.shape[0]
    for start in range(0, rows, chunk):
        size = min(chunk, rows - start)
        ref[(start // chunk,) + lead + (pl.ds(0, size),)] = value[start : start + size]


def normalized(tok, gain):
    x = tok[0].astype(F32)
    mean = jnp.mean(x * x, axis=-1, keepdims=True)
    return (x * lax.rsqrt(mean + EPS) * gain[...]).astype(BF16)


def query_kernel(req_dev, chunk, cont, clen, tok, gain, w, qg, table, q):
    b = pl.program_id(0)
    count = tok.shape[1]
    half = count // 2
    request = lax.axis_index("req") * req_dev + b
    length = jnp.where(cont[request] == 1, clen[request], 0)
    out = lax.dot_general(
        normalized(tok, gain), w[...], (((1,), (1,)), ((), ())), preferred_element_type=F32
    )
    cosine, sine = rotation(length, count, table)
    blocks = half_blocks()
    gains = jnp.concatenate([qg[...]] * 2, axis=1)
    pair01 = norm_rope(out[:, :128], gains, cosine, sine, blocks)
    pair23 = norm_rope(out[:, 128:256], gains, cosine, sine, blocks)
    last = out[:, 256:320]
    last = jnp.concatenate([last[:half], last[half:]], axis=1)
    lanes = lane_iota(half)
    pick = lambda v: jnp.where(lanes < 64, v[:half], v[half:])
    last = norm_rope(last, gains, pick(cosine), pick(sine), blocks)
    packed = (jnp.concatenate([pair01, pair23, last], axis=0) * 0.125).astype(BF16)
    to_chunks(q, (0,), packed, chunk)


def fresh_kernel(req_dev, meta, tok, gain, w, kg, table, after, fresh):
    del after
    b = pl.program_id(0)
    count = tok.shape[1]
    length = live_length(meta, lax.axis_index("req") * req_dev + b)
    out = jnp.dot(normalized(tok, gain), w[...], preferred_element_type=F32)
    cosine, sine = rotation(length, count, table)
    blocks = half_blocks()
    lanes = lane_iota(count)
    gains = jnp.concatenate([kg[...]] * 2, axis=1)
    for head in range(fresh.shape[1]):
        tile = out[:, head * 128 : head * 128 + 128]
        keys = norm_rope(tile, gains, cosine, sine, blocks)
        fresh[0, head] = jnp.where(lanes < 64, keys, tile).astype(BF16)


def split_heads(packed, count):
    half = count // 2
    wide = packed.astype(F32)
    lanes = lane_iota(count)
    tiles = [wide[:count], pltpu.roll(wide[:count], 64, 1)]
    tiles += [wide[count : 2 * count], pltpu.roll(wide[count : 2 * count], 64, 1)]
    last = wide[2 * count : 2 * count + half]
    tiles.append(jnp.concatenate([last, pltpu.roll(last, 64, 1)], axis=0))
    return [jnp.where(lanes < 64, tile, 0.0).astype(BF16) for tile in tiles]


def soft(scores, values):
    top = jnp.max(scores, axis=-1, keepdims=True)
    weights = jnp.exp(scores - top)
    total = jnp.sum(weights, axis=-1, keepdims=True)
    out = jnp.dot(weights.astype(BF16), values, preferred_element_type=F32)
    return out / total, top + jnp.log(total)


def local_kernel(groups, q, fresh, out):
    heads = 5
    count = fresh.shape[2]
    first = lax.axis_index("tp") * heads
    lanes = lane_iota(count)
    rows = lax.broadcasted_iota(jnp.int32, (count, count), 0)
    cols = lax.broadcasted_iota(jnp.int32, (count, count), 1)
    packed = q[...].reshape(-1, LANES)
    tiles = split_heads(packed, count)
    stats = jnp.zeros((count, LANES), F32)
    kept = []
    for head in range(heads):
        kv = fresh[0, (first + head) // groups]
        scores = lax.dot_general(
            tiles[head], kv, (((1,), (1,)), ((), ())), preferred_element_type=F32
        )
        scores = jnp.where(cols <= rows, scores, NEG)
        mixed, level = soft(scores, kv)
        stats = jnp.where(lanes == head, level, stats)
        kept.append(mixed)
    roll = lambda v: pltpu.roll(v, 64, 1)
    out[0, 0] = jnp.where(lanes < 64, roll(kept[0]), kept[1])
    out[0, 1] = jnp.where(lanes < 64, roll(kept[2]), kept[3])
    out[0, 2] = jnp.where(lanes < 64, roll(kept[4]), roll(stats))


def each(requests, step):
    if requests <= 32:
        for r in range(requests):
            step(r)
    else:
        pl.loop(0, requests)(step)


def route_query_kernel(requests, meta, src, dst):
    def step(r):
        @pl.when(live(meta, r))
        def _():
            dst[meta[1, r]] = src[r]

    each(requests, step)


def route_result_kernel(requests, meta, src, dst):
    def step(r):
        dst[r] = src[jnp.where(live(meta, r), meta[1, r], 0)]

    each(requests, step)


def row_kernel(requests, count, heads, groups, chunk, meta, q, pair, out):
    span = pair.shape[1]
    offset = lax.axis_index("tp") * heads
    first = offset // groups

    row = lax.axis_index("req")

    def find(r, length):
        mine = jnp.logical_and(live(meta, r), meta[1, r] == row)
        return jnp.where(mine, meta[2, r], length)

    length = lax.fori_loop(0, requests, find, 0)
    position = lax.broadcasted_iota(jnp.int32, (8, span), 1)
    bias = jnp.where(position < length, 0.0, NEG)[0:1]
    tiles = split_heads(q[...].reshape(-1, LANES), count)
    lanes = lane_iota(count)
    level = jnp.zeros((count, LANES), F32)
    kept = []
    for head in range(heads):
        kv = pair[(offset + head) // groups - first]
        scores = lax.dot_general(
            tiles[head], kv, (((1,), (1,)), ((), ())), preferred_element_type=F32
        )
        mixed, one = soft(scores + bias, kv)
        level = jnp.where(lanes == head, one, level)
        kept.append(mixed)
    roll = lambda v, n: pltpu.roll(v, n, 1)
    high = level.astype(BF16).astype(F32)
    mid = (level - high).astype(BF16).astype(F32)
    low = (level - high - mid).astype(BF16).astype(F32)
    stats = roll(high, 64) + roll(mid, 64 + heads) + roll(low, 64 + 2 * heads)
    tiles = [
        jnp.where(lanes < 64, roll(kept[0], 64), kept[1]),
        jnp.where(lanes < 64, roll(kept[2], 64), kept[3]),
        jnp.where(lanes < 64, roll(kept[4], 64), stats),
    ]
    to_chunks(out, (), jnp.concatenate(tiles, axis=0).astype(BF16), chunk)


def merge_kernel(req_dev, meta, far, near, mixed):
    heads = 5
    count = near.shape[2]
    b = pl.program_id(0)
    request = lax.axis_index("req") * req_dev + b
    lanes = lane_iota(count)
    roll = lambda v, n: pltpu.roll(v, n, 1)
    packed = far[...].reshape(-1, LANES)
    tiles = [packed[p * count : (p + 1) * count].astype(F32) for p in range(3)]
    stats = roll(tiles[2], 64) + roll(tiles[2], 64 - heads) + roll(tiles[2], 64 - 2 * heads)
    far_level = jnp.where(jnp.logical_and(live(meta, request), lanes < heads), stats, NEG)
    near_level = jnp.where(lanes < heads, roll(near[0, 2], 64), 0.0)
    top = jnp.maximum(far_level, near_level)
    far_part = jnp.exp(far_level - top)
    near_part = jnp.exp(near_level - top)
    share = far_part / (far_part + near_part)
    done = []
    for p in range(3):
        left = share[:, 2 * p : 2 * p + 1]
        right = share[:, 2 * p + 1 : 2 * p + 2] if 2 * p + 1 < heads else left
        weight = jnp.where(lanes < 64, left, right)
        done.append(weight * tiles[p] + (1.0 - weight) * near[0, p])
    half = count // 2
    last = jnp.where(lane_iota(half) < 64, done[2][:half], roll(done[2][half:], 64))
    mixed[0] = jnp.concatenate([done[0], done[1], last], axis=0).astype(BF16)


def project_kernel(block, m_a, m_b, *refs):
    ws, (base, out, lhs) = refs[:-3], refs[-3:]
    count, width = out.shape[1:]
    half = count // 2
    lanes = lane_iota(half)
    for number, m in enumerate((m_a, m_b)):
        for p in range(2):
            col = number * 256 + p * 128
            lhs[:, col : col + 128] = m[0, p * count : (p + 1) * count]
    left = m_a[0, 2 * count :].astype(F32)
    right = m_b[0, 2 * count :].astype(F32)
    lhs[:half, 512:] = jnp.where(lanes < 64, left, pltpu.roll(right, 64, 1)).astype(BF16)
    lhs[half:, 512:] = jnp.where(lanes < 64, pltpu.roll(left, 64, 1), right).astype(BF16)
    for start in range(0, width, block):
        part = pl.ds(start, block)
        if len(ws) == 1:
            weights = ws[0][:, part]
        else:
            weights = jnp.concatenate(
                [w[rows, part] for rows in (pl.ds(0, 256), pl.ds(256, 64)) for w in ws], axis=0
            )
        total = base[0, :, part].astype(F32)
        total += jnp.dot(lhs[...], weights, preferred_element_type=F32)
        out[0, :, part] = total.astype(out.dtype)


def stage_kernel(w_a, w_b, after, out, sem):
    del after
    copies, place = [], 0
    for rows in (pl.ds(0, 256), pl.ds(256, 64)):
        for w in (w_a, w_b):
            dst = out.at[pl.ds(place, rows.size), :]
            copies.append(pltpu.make_async_copy(w.at[rows, :], dst, sem.at[len(copies)]))
            place += rows.size
    for copy in copies:
        copy.start()
    for copy in copies:
        copy.wait()


def held(plane, here):
    apart = plane ^ here
    mid = jnp.logical_or(here == 1, here == 2)
    return jnp.where(apart < 2, apart, jnp.where(mid, 5 - apart, 2 + apart))


def cache_kernel(req_dev, span, steps, meta, *refs):
    blocks, (mine, theirs, _, out, kept_sc, out_sc, sem, out_sem) = refs[:-8], refs[-8:]
    place, tp_place = lax.axis_index("req"), lax.axis_index("tp")
    side = place % 2
    kv_heads, segment = out.shape[1], out.shape[2]
    count = mine.shape[2]
    start = (side * lax.axis_size("tp") + tp_place) * segment
    skip = pl.multiple_of(start - jnp.minimum(start, span - segment), 16)
    first = (place // 2) * 2 * req_dev
    numbers = range(2 * req_dev)
    found = []
    for number in numbers:
        row = jnp.where(live(meta, first + number), meta[1, first + number], place)
        step = 0 if len(blocks[0].shape) == 5 else held(row // 2, place // 2)
        found.append((row // 2, (row % 2) ^ side, step))

    def here(number, action):
        wanted = functools.reduce(jnp.logical_or, [found[number][2] == step for step in steps])
        pl.when(wanted)(action)

    def fetch(number):
        plane, which, step = found[number]
        dst = kept_sc.at[number, :, pl.ds(0, segment), :]
        if len(blocks[0].shape) == 5:
            pltpu.make_async_copy(blocks[0].at[plane, which], dst, sem.at[number]).start()
            return
        for step_of, block in zip(steps, blocks):

            @pl.when(step == step_of)
            def _():
                pltpu.make_async_copy(block.at[which], dst, sem.at[number]).start()

    def write(number):
        return pltpu.make_async_copy(out_sc.at[number], out.at[number], out_sem.at[number])

    def fill(number):
        ahead = live_length(meta, first + number) - start
        rows = lax.broadcasted_iota(jnp.int32, (segment, count), 0)
        cols = lax.broadcasted_iota(jnp.int32, (segment, count), 1)
        shift = jnp.where(rows - cols == ahead, 1.0, 0.0).astype(BF16)
        local = number // req_dev == side
        place_of = number % req_dev
        new = jnp.concatenate(
            [jnp.where(local, mine[place_of, h], theirs[place_of, h]) for h in range(kv_heads)],
            axis=1,
        )
        moved = jnp.dot(shift, new, preferred_element_type=F32)
        old = lax.broadcasted_iota(jnp.int32, (segment, LANES), 0) < ahead
        dst = kept_sc.at[number, :, pl.ds(0, segment), :]
        pltpu.make_async_copy(dst, dst, sem.at[number]).wait()
        for head in range(kv_heads):
            kept = kept_sc[number, head, pl.ds(skip, segment), :].astype(F32)
            part = moved[:, head * LANES : head * LANES + LANES]
            out_sc[number, head] = jnp.where(old, kept, part).astype(BF16)
        write(number).start()

    for number in numbers:
        fetch(number)
    for number in numbers:
        here(number, functools.partial(fill, number))
    for number in numbers:
        here(number, lambda number=number: write(number).wait())


def permuted(value, axis, mask):
    pairs = [(source, source ^ mask) for source in range(lax.axis_size(axis))]
    return lax.ppermute(value, axis, pairs)


def exchanged(value):
    return lax.all_to_all(value, "req", split_axis=0, concat_axis=0, tiled=True)


def full(shape):
    return pl.BlockSpec(shape, lambda *_: (0,) * len(shape))


def on_device(
    tokens,
    attn_gain,
    w_query,
    key_value_weight,
    w_out,
    q_gain,
    k_gain,
    stored,
    continuing,
    cache_row,
    cache_len,
):
    n_req = lax.axis_size("req")
    tp_count = lax.axis_size("tp")
    req_dev, count, width = tokens.shape
    head_dim = q_gain.shape[0]
    kv_heads = key_value_weight.shape[1] // (2 * head_dim)
    heads = w_query.shape[1] // head_dim
    groups = heads * tp_count // kv_heads
    span = stored.shape[2]
    requests = continuing.shape[0]
    segments = 2 * tp_count
    segment = (span + count) // segments
    q_rows = heads * head_dim * count // LANES
    o_rows = -(-heads * head_dim // LANES) * count
    q_chunk = -(-q_rows // (16 * n_req)) * 16
    o_chunk = -(-o_rows // (16 * n_req)) * 16

    table = jnp.asarray(angle_tables(head_dim, count, span))
    table_spec = full(table.shape)
    meta = jnp.stack([continuing, cache_row, cache_len])
    gain_row = attn_gain.reshape(1, width)
    q_gain_row = q_gain.reshape(1, head_dim)
    k_gain_row = k_gain.reshape(1, head_dim)
    w_query_rows = w_query.T
    any_spec = pl.BlockSpec(memory_space=pl.ANY)
    hbm_spec = pl.BlockSpec(memory_space=pltpu.HBM)
    vmem_spec = pl.BlockSpec(memory_space=pltpu.VMEM)
    token_spec = pl.BlockSpec((1, count, width), lambda b: (b, 0, 0))

    side = lax.axis_index("req") % 2
    tp_place = lax.axis_index("tp")

    def part(source, which):
        start = (which * tp_count + tp_place) * segment
        return lax.dynamic_slice_in_dim(source[0], start, segment, 1)

    partner_part = permuted(part(stored, 1 - side), "req", 1)
    q = pl.pallas_call(
        functools.partial(query_kernel, req_dev, q_chunk),
        grid=(req_dev,),
        out_shape=jax.ShapeDtypeStruct((n_req, req_dev, q_chunk, LANES), BF16),
        in_specs=[
            SMEM,
            SMEM,
            token_spec,
            full((1, width)),
            full(w_query_rows.shape),
            full((1, head_dim)),
            table_spec,
        ],
        out_specs=pl.BlockSpec((n_req, 1, q_chunk, LANES), lambda b: (0, b, 0, 0)),
        compiler_params=params(60),
        cost_estimate=cost(2 * req_dev * count * width * 384, 6 << 20),
        name="query",
    )(continuing, cache_len, tokens, gain_row, w_query_rows, q_gain_row, table)
    q_mid = exchanged(q).reshape(requests, q_chunk, LANES)

    partner_part, later = lax.optimization_barrier((partner_part, stored, q))[:2]
    both = jnp.stack([part(later, side), partner_part])
    planes = n_req // 2
    hops = planes == 4

    def crossed(value, pairs):
        pairs = [(2 * a + parity, 2 * b + parity) for a, b in pairs for parity in range(2)]
        return lax.ppermute(value, "req", pairs)

    if hops:
        outer = [(z, z ^ 1) for z in range(planes)]
        beside = crossed(both, outer)
        middle = crossed(both, [(1, 2), (2, 1)])
    else:
        column = [list(range(parity, n_req, 2)) for parity in range(2)]
        blocks = [lax.all_gather(both, "req", axis_index_groups=column)]
        beside = middle = both

    w_x = permuted(w_out, "tp", tp_count // 2)
    w_c = permuted(w_out, "tp", 1)
    w_xc = permuted(w_x, "tp", 1)

    later = lax.optimization_barrier((stored, q_mid))[0]
    pair = lax.dynamic_slice_in_dim(later[0], tp_place * heads // groups, 2, 0)
    fresh = pl.pallas_call(
        functools.partial(fresh_kernel, req_dev),
        grid=(req_dev,),
        out_shape=jax.ShapeDtypeStruct((req_dev, kv_heads, count, LANES), BF16),
        in_specs=[
            SMEM,
            token_spec,
            full((1, width)),
            full(key_value_weight.shape),
            full((1, head_dim)),
            table_spec,
            any_spec,
        ],
        out_specs=pl.BlockSpec((1, kv_heads, count, LANES), lambda b: (b, 0, 0, 0)),
        compiler_params=params(),
        cost_estimate=HINT,
        name="fresh",
    )(meta, tokens, gain_row, key_value_weight, k_gain_row, table, pair)

    q_out = pl.pallas_call(
        functools.partial(route_query_kernel, requests),
        out_shape=jax.ShapeDtypeStruct((n_req, q_chunk, LANES), BF16),
        in_specs=[SMEM, vmem_spec],
        out_specs=vmem_spec,
        compiler_params=params(),
        cost_estimate=cost(0, 1 << 20),
        name="route_query",
    )(meta, q_mid)
    q_row, beside, middle, _ = lax.optimization_barrier((exchanged(q_out), beside, middle, fresh))
    if hops:
        far_middle = crossed(beside, [(1, 2), (2, 1)])
        outward = crossed(middle, outer)
    fresh_partner = permuted(fresh, "req", 1)

    near = pl.pallas_call(
        functools.partial(local_kernel, groups),
        grid=(req_dev,),
        out_shape=jax.ShapeDtypeStruct((req_dev, 3, count, LANES), F32),
        in_specs=[
            pl.BlockSpec((n_req, 1, q_chunk, LANES), lambda b: (0, b, 0, 0)),
            pl.BlockSpec((1, kv_heads, count, LANES), lambda b: (b, 0, 0, 0)),
        ],
        out_specs=pl.BlockSpec((1, 3, count, LANES), lambda b: (b, 0, 0, 0)),
        compiler_params=params(60),
        cost_estimate=HINT,
        name="attend_new",
    )(q, fresh)

    far = pl.pallas_call(
        functools.partial(row_kernel, requests, count, heads, groups, o_chunk),
        out_shape=jax.ShapeDtypeStruct((n_req, o_chunk, LANES), BF16),
        in_specs=[SMEM, vmem_spec, vmem_spec],
        out_specs=vmem_spec,
        compiler_params=params(60),
        cost_estimate=cost(4 * heads * count * span * 256, 32 << 20),
        name="attend_row",
    )(meta, q_row, pair)

    far_mid = exchanged(far)
    if hops:
        far_mid = lax.optimization_barrier((far_mid, far_middle, outward, fresh_partner, near))[0]
        far_outward = crossed(far_middle, outer)
        blocks = [both, beside, middle, far_middle, outward, far_outward]
    def fill_cache(steps, blocks, after, aliases):
        return pl.pallas_call(
            functools.partial(cache_kernel, req_dev, span, steps),
            in_specs=[SMEM] + [any_spec] * len(blocks) + [vmem_spec, vmem_spec, any_spec],
            out_specs=any_spec,
            scratch_shapes=[
                pltpu.VMEM((2 * req_dev, kv_heads, 2 * segment, LANES), BF16),
                pltpu.VMEM((2 * req_dev, kv_heads, segment, LANES), BF16),
                pltpu.SemaphoreType.DMA((2 * req_dev,)),
                pltpu.SemaphoreType.DMA((2 * req_dev,)),
            ],
            out_shape=jax.ShapeDtypeStruct((2 * req_dev, kv_heads, segment, LANES), BF16),
            input_output_aliases=aliases,
            compiler_params=params(),
            cost_estimate=HINT,
            name="cache",
        )(meta, *blocks, fresh, fresh_partner, after)

    if hops:
        cache = fill_cache(tuple(range(5)), blocks[:5], far_mid, {})

    far_out = pl.pallas_call(
        functools.partial(route_result_kernel, requests),
        out_shape=jax.ShapeDtypeStruct((requests, o_chunk, LANES), BF16),
        in_specs=[SMEM, vmem_spec],
        out_specs=vmem_spec,
        compiler_params=params(),
        cost_estimate=cost(0, 1 << 20),
        name="route_result",
    )(meta, far_mid)
    far_home = exchanged(far_out.reshape(n_req, req_dev, o_chunk, LANES))
    if hops:
        far_home = lax.optimization_barrier((far_home, cache))[0]

    mixed = pl.pallas_call(
        functools.partial(merge_kernel, req_dev),
        grid=(req_dev,),
        out_shape=jax.ShapeDtypeStruct((req_dev, q_rows, LANES), BF16),
        in_specs=[
            SMEM,
            pl.BlockSpec((n_req, 1, o_chunk, LANES), lambda b: (0, b, 0, 0)),
            pl.BlockSpec((1, 3, count, LANES), lambda b: (b, 0, 0, 0)),
        ],
        out_specs=pl.BlockSpec((1, q_rows, LANES), lambda b: (b, 0, 0)),
        compiler_params=params(),
        cost_estimate=HINT,
        name="merge",
    )(meta, far_home, near)

    m_x = permuted(mixed, "tp", tp_count // 2)
    m_c = permuted(mixed, "tp", 1)

    def project(m_a, m_b, ws, base, dtype, name):
        m_spec = pl.BlockSpec((1, q_rows, LANES), lambda b: (b, 0, 0))
        return pl.pallas_call(
            functools.partial(project_kernel, 512),
            grid=(req_dev,),
            out_shape=jax.ShapeDtypeStruct(tokens.shape, dtype),
            in_specs=[m_spec] * 2 + [full(w.shape) for w in ws] + [token_spec],
            out_specs=token_spec,
            scratch_shapes=[pltpu.VMEM((count, 640), BF16)],
            compiler_params=params(),
            cost_estimate=HINT,
            name=name,
        )(m_a, m_b, *ws, base)

    partial = project(mixed, m_c, (w_out, w_c), tokens, F32, "project_chip")
    staged = pl.pallas_call(
        stage_kernel,
        out_shape=jax.ShapeDtypeStruct((2 * w_out.shape[0], width), BF16),
        in_specs=[any_spec] * 3,
        out_specs=vmem_spec,
        scratch_shapes=[pltpu.SemaphoreType.DMA((4,))],
        compiler_params=params(),
        cost_estimate=HINT,
        name="stage",
    )(w_x, w_xc, partial)
    if hops:
        last = lax.optimization_barrier((far_outward, staged))[0]
        cache = fill_cache((5,), [last], cache, {4: 0})
        m_x = lax.optimization_barrier((m_x, cache))[0]
    m_x = lax.optimization_barrier((m_x, partial, staged))[0]
    m_xc = permuted(m_x, "tp", 1)
    layer = project(m_x, m_xc, (staged,), partial, BF16, "project_rest")

    if not hops:
        cache = fill_cache((0,), blocks, layer, {})
    return (layer, cache)


def solution(mesh):
    return jax.shard_map(
        on_device,
        mesh=mesh,
        in_specs=(
            P("req", None, None),
            P(),
            P(None, "tp"),
            P(),
            P("tp", None),
            P(),
            P(),
            P("req", None, None, None),
            P(),
            P(),
            P(),
        ),
        out_specs=(P("req", None, None), P("req", None, "tp", None)),
        check_vma=False,
    )
```
